256 devices in a mesh: det: 64 (over z, y, core), tm: 4 (over x).
Axes of the slice: x: 4, y: 4, z: 8, core: 2. Of those that a mesh axis runs over, the one named last changes fastest.
Arguments:
- time_streams: float32 [64, 1, 4096], P('det', None, 'tm'), may hold values from -12 to 12
- pol_angle: float32 [64, 1, 4096], P('det', None, 'tm'), may hold values from -3.140625 to 3.140625
- offsets: int32 [64, 1, 4096], P('det', None, 'tm'), may hold values from 0 to 255
- block_slots: int32 [64, 1, 16], P('det', None, 'tm'), may hold values from 0 to 127
- hit_ids: int32 [64, 128], P('det'), may hold values from 0 to 1023, as said below
- valid_counts: int32 [64, 1], P('det'), may hold values from 1024 to 4096
- filter_taps: float32 [64, 1, 65], P('det'), may hold values from -0.75 to 0.75
- white_weight: float32 [64, 1], P('det'), may hold values from 0.5 to 2
Outputs:
- solution_map: float32 [1024, 3, 256], P('det')
- precond_residual: float32 [1024, 3, 256], P('det')
The draws below stay inside these ranges and needn't reach their ends.
Inputs may be any that keep to these rules, and one draw needn't show every extreme that they name: `hit_ids`: slot o * 2 + c of a section names a block of o * 16 .. (o + 1) * 16 - 1, and the 2 blocks of one o in one section differ.
All inputs are finite; a program needn't handle non-finite values.
Results may differ from the reference program's by a relative error of at most 0.0003.
Values sent between devices are 32-bit elements; how exact they have to be, the bound alone decides.
A program may use at most 128 MiB of HBM per device.

```python
import math
import jax
import jax.numpy as jnp
from jax import lax

BLK = 256
WIN = 256
BAND = 64
ITERS = 2
NDET = 1
BPD = 16
CAP = 2
SECTIONS = 64
TIME = 4096
NTB = 16
HIT = 128
NBLK = 1024


def draw_hit_ids(key, part):
    owner_count = HIT // CAP
    scores = jax.random.randint(key, (SECTIONS, owner_count, BPD), 0, 1 << 20)
    scores = scores * BPD + jnp.arange(BPD, dtype=jnp.int32)
    order = jnp.argsort(scores, axis=-1)[..., :CAP].astype(jnp.int32)
    base = jnp.arange(owner_count, dtype=jnp.int32)[None, :, None] * BPD
    return (order + base).reshape(SECTIONS, HIT).astype(jnp.int32)


def with_ends(drawn, rng, low, high):
    dims = drawn.shape
    spot = [jax.random.randint(jax.random.fold_in(rng, axis), (), 0, dims[axis]) for axis in range(len(dims))]
    drawn = drawn.at[tuple(spot)].set(low)
    longest = dims.index(max(dims))
    spot[longest] = (spot[longest] + 1) % dims[longest]
    return drawn.at[tuple(spot)].set(high)


def levels(rng, extent, split, smallest, high):
    level, own = 1.0, jax.random.fold_in(rng, 6)
    for dim, shards_of in split:
        draws = jnp.exp(jax.random.uniform(jax.random.fold_in(own, dim), (shards_of,), jnp.float32, smallest / len(split), high / len(split)))
        level = level * jnp.repeat(draws, extent[dim] // shards_of).reshape([-1 if axis == dim else 1 for axis in range(len(extent))])
    return level


def bell_draw(stream_key, extent, scale, reach, shards=(), kind=jnp.bfloat16):
    drawn = jax.random.normal(stream_key, extent, jnp.float32) * scale
    if len(shards) > 0:
        drawn = levels(stream_key, extent, shards, -0.22, 0.18) * drawn
    return jnp.clip(drawn, min=-reach, max=reach).astype(kind)


def setup_inputs(seed: int = 0) -> dict:
    seeds = jax.random.split(jax.random.key(seed), 9)
    time_streams = bell_draw(seeds[0], (SECTIONS, NDET, TIME), 2.0, 12.0, ((0, 64), (2, 4)), jnp.float32)
    pol_angle = jnp.clip(jax.random.uniform(seeds[1], (SECTIONS, NDET, TIME), jnp.float32, -3.140625, 3.140625), -3.140625, 3.140625)
    offsets = with_ends(jax.random.randint(seeds[2], (SECTIONS, NDET, TIME), 0, BLK), jax.random.fold_in(seeds[2], 1), 0, BLK - 1).astype(jnp.int32)
    block_slots = with_ends(jax.random.randint(seeds[3], (SECTIONS, NDET, NTB), 0, HIT), jax.random.fold_in(seeds[3], 1), 0, HIT - 1).astype(jnp.int32)
    hit_ids = draw_hit_ids(jax.random.fold_in(seeds[8], 71), 0)
    valid_counts = with_ends(jax.random.randint(seeds[5], (SECTIONS, NDET), TIME // 4, TIME + 1), jax.random.fold_in(seeds[5], 1), TIME // 4, TIME).astype(jnp.int32)
    filter_taps = bell_draw(seeds[6], (SECTIONS, NDET, BAND + 1), (BAND + 1) ** -0.5, 0.75, ((0, 64),), jnp.float32)
    white_weight = jnp.clip(jnp.exp(math.log(2.0) - 1.3862944 * jax.random.uniform(seeds[7], (SECTIONS, NDET), jnp.float32) ** levels(seeds[7], (SECTIONS, NDET), ((0, 64),), -0.2, 0.2)), 0.5, 2.0)
    return dict(time_streams=time_streams, pol_angle=pol_angle, offsets=offsets, block_slots=block_slots, hit_ids=hit_ids, valid_counts=valid_counts, filter_taps=filter_taps, white_weight=white_weight)


def lag_table(filter_taps, white_weight):
    columns = []
    for shift_lag in range(BAND + 1):
        columns.append(jnp.sum(filter_taps[..., :BAND + 1 - shift_lag] * filter_taps[..., shift_lag:], axis=-1))
    lags = jnp.stack(columns, axis=-1)
    return lags.at[..., 0].add(white_weight)


def noise_filter(signal, lags):
    padded = jnp.pad(signal, ((0, 0), (BAND, BAND)))
    result = lags[:, 0:1] * signal
    for shift_lag in range(1, BAND + 1):
        result = result + lags[:, shift_lag:shift_lag + 1] * (padded[:, BAND + shift_lag:BAND + shift_lag + TIME] + padded[:, BAND - shift_lag:BAND - shift_lag + TIME])
    return result


def precondition(weights, residual):
    entry_aa = 1.0 + weights[:, 0]
    entry_ab = weights[:, 1]
    entry_ac = weights[:, 2]
    entry_bb = 1.0 + weights[:, 3]
    entry_bc = weights[:, 4]
    entry_cc = 1.0 + weights[:, 5]
    minor_aa = entry_bb * entry_cc - entry_bc * entry_bc
    minor_ab = entry_ac * entry_bc - entry_ab * entry_cc
    minor_ac = entry_ab * entry_bc - entry_ac * entry_bb
    minor_bb = entry_aa * entry_cc - entry_ac * entry_ac
    minor_bc = entry_ab * entry_ac - entry_aa * entry_bc
    minor_cc = entry_aa * entry_bb - entry_ab * entry_ab
    determinant = entry_aa * minor_aa + entry_ab * minor_ab + entry_ac * minor_ac
    stokes_i = residual[:, 0]
    stokes_q = residual[:, 1]
    stokes_u = residual[:, 2]
    return jnp.stack([
        (minor_aa * stokes_i + minor_ab * stokes_q + minor_ac * stokes_u) / determinant,
        (minor_ab * stokes_i + minor_bb * stokes_q + minor_bc * stokes_u) / determinant,
        (minor_ac * stokes_i + minor_bc * stokes_q + minor_cc * stokes_u) / determinant], axis=1)


def reference(time_streams, pol_angle, offsets, block_slots, hit_ids, valid_counts, filter_taps, white_weight):
    lags = lag_table(filter_taps, white_weight)
    pixel_count = NBLK * BLK
    sample_time = jnp.arange(TIME, dtype=jnp.int32)

    def binned(components_of, count):
        def accumulate(accumulated, section):
            streams, angles, offset_row, slot_row, hit_row, counts, lag_row = section
            blocks = jnp.take(hit_row, slot_row, axis=0)
            pixels = (jnp.repeat(blocks, WIN, axis=1) * BLK + offset_row).astype(jnp.int32)
            live_mask = (sample_time[None, :] < counts[:, None]).astype(jnp.float32)
            cosine = jnp.cos(2.0 * angles)
            sine_term = jnp.sin(2.0 * angles)
            components = components_of(streams, lag_row, pixels, live_mask, cosine, sine_term)
            return accumulated.at[:, pixels].add(components), None

        empty_map = jnp.zeros((count, pixel_count), jnp.float32)
        accumulated, _ = lax.scan(accumulate, empty_map, (time_streams, pol_angle, offsets, block_slots, hit_ids, valid_counts, lags))
        return jnp.transpose(accumulated.reshape(count, NBLK, BLK), (1, 0, 2))

    def initial_parts(streams, lag_row, pixels, live_mask, cosine, sine_term):
        filtered = noise_filter(streams * live_mask, lag_row) * live_mask
        weight = lag_row[:, 0:1] * live_mask
        return jnp.stack([filtered, filtered * cosine, filtered * sine_term, weight, weight * cosine, weight * sine_term,
                          weight * cosine * cosine, weight * cosine * sine_term, weight * sine_term * sine_term])

    def apply_operator(direction):
        flat_map = jnp.transpose(direction, (1, 0, 2)).reshape(3, pixel_count)

        def operator_parts(streams, lag_row, pixels, live_mask, cosine, sine_term):
            values = flat_map[:, pixels]
            signal = (values[0] + values[1] * cosine + values[2] * sine_term) * live_mask
            filtered = noise_filter(signal, lag_row) * live_mask
            return jnp.stack([filtered, filtered * cosine, filtered * sine_term])

        return binned(operator_parts, 3)

    initial = binned(initial_parts, 9)
    right_side = initial[:, :3]
    weights = initial[:, 3:]
    solution = jnp.zeros_like(right_side)
    residual = right_side
    descent = precondition(weights, residual)
    direction = descent
    product_now = jnp.sum(residual * descent)
    for iteration in range(ITERS):
        image_map = apply_operator(direction)
        step_size = product_now / jnp.sum(direction * image_map)
        solution = solution + step_size * direction
        residual = residual - step_size * image_map
        descent = precondition(weights, residual)
        product_next = jnp.sum(residual * descent)
        direction = descent + (product_next / product_now) * direction
        product_now = product_next
    return solution, descent
```

```python
import functools

import jax
import jax.numpy as jnp
from jax import lax
from jax.experimental import pallas as pl
from jax.experimental.pallas import tpu as pltpu
from jax.sharding import PartitionSpec as P

WIN = 256
BAND = 64
BPD = 16
HALF = 128
SPAN = 1024
BLOCKS = 4
DEVICES = 256
LABELS = DEVICES * BLOCKS

HIGHEST = lax.Precision.HIGHEST
NT = (((1,), (1,)), ((), ()))
MESH = pl.DeviceIdType.MESH

vmem = pl.BlockSpec(memory_space=pltpu.VMEM)
smem = pl.BlockSpec(memory_space=pltpu.SMEM)


def lanes(shape):
    return lax.broadcasted_iota(jnp.int32, shape, len(shape) - 1)


def rows_of(shape):
    return lax.broadcasted_iota(jnp.int32, shape, 0)


def band_filter(extended, band):
    turned = pltpu.roll(extended, HALF // 2, 1)
    keep = lanes((8, HALF)) < HALF // 2
    first = jnp.where(keep, turned[0:8], turned[1:9])
    second = jnp.where(keep, turned[1:9], turned[2:10])
    window = jnp.concatenate([first, second], axis=1)
    return jnp.dot(window, band, precision=HIGHEST, preferred_element_type=jnp.float32)


def grid_place():
    det = lax.axis_index("det")
    x = lax.axis_index("tm")
    return lax.div(det, 8), lax.rem(lax.div(det, 2), 4), lax.rem(det, 2), x


def device_at(z, y, core, x):
    return {"det": (z * 4 + y) * 2 + core, "tm": x}


def slot_of(z, y, core, x):
    major = y + core * (x - y)
    minor = x + core * (y - x)
    return ((core * 8 + z) * 4 + major) * 4 + minor


def meet():
    z, y, core, x = grid_place()
    barrier = pltpu.get_barrier_semaphore()
    peers = (
        [device_at(lax.rem(z + d, 8), y, core, x) for d in range(1, 8)]
        + [device_at(z, lax.rem(y + d, 4), core, x) for d in range(1, 4)]
        + [device_at(z, y, core, lax.rem(x + d, 4)) for d in range(1, 4)]
        + [device_at(z, y, 1 - core, x)]
    )
    for peer in peers:
        pl.semaphore_signal(barrier, inc=1, device_id=peer, device_id_type=MESH)
    pl.semaphore_wait(barrier, len(peers))


def exchange(sources, buffers, send_sems, recv_sems, local_sems):
    z, y, core, x = grid_place()
    a = y + core * (x - y)
    b = x + core * (y - x)

    def major_peer(step):
        return device_at(
            z,
            y + (1 - core) * (lax.rem(y + step, 4) - y),
            core,
            x + core * (lax.rem(x + step, 4) - x),
        )

    def minor_peer(step):
        return device_at(
            z,
            y + core * (lax.rem(y + step, 4) - y),
            core,
            x + (1 - core) * (lax.rem(x + step, 4) - x),
        )

    arrays = range(len(sources))

    def send(number, source_of, target_of, peer):
        copies = []
        for i in arrays:
            copy = pltpu.make_async_remote_copy(
                src_ref=source_of(i),
                dst_ref=target_of(i),
                send_sem=send_sems.at[i, number],
                recv_sem=recv_sems.at[i, number],
                device_id=peer,
                device_id_type=MESH,
            )
            copy.start()
            copies.append(copy)
        return copies

    def landed(copies):
        for copy in copies:
            copy.wait_recv()

    started = []
    keep = [
        pltpu.make_async_copy(sources[i], buffers[i].at[core, z, a, b], local_sems.at[i])
        for i in arrays
    ]
    first = [
        send(
            d - 1,
            lambda i: sources[i],
            lambda i: buffers[i].at[core, z, a, b],
            device_at(lax.rem(z + d, 8), y, core, x),
        )
        for d in (4, 3, 5, 2, 6, 1, 7)
    ]
    for copy in keep:
        copy.start()
    for copy in keep:
        copy.wait()
    for copies in first:
        landed(copies)
    started += first

    def column(i):
        return buffers[i].at[core, :, a, b]

    second = [send(6 + d, column, column, major_peer(d)) for d in (2, 1, 3)]
    for copies in second:
        landed(copies)
    started += second

    def part(number, half):
        depth = pl.ds(4 * half, 4)
        return lambda i: buffers[i].at[core, depth, :, number]

    def whole(number):
        return lambda i: buffers[i].at[core, :, :, number]

    after = minor_peer(1)
    before = minor_peer(3)
    partner = device_at(z, y, 1 - core, x)
    left = lax.rem(b + 3, 4)
    right = lax.rem(b + 1, 4)
    far = lax.rem(b + 2, 4)
    up = [send(10, part(b, 0), part(b, 0), after)]
    down = [send(12, part(b, 1), part(b, 1), before)]
    up.append(send(11, part(b, 1), part(b, 1), after))
    down.append(send(13, part(b, 0), part(b, 0), before))
    swaps = [send(16, whole(b), whole(b), partner)]
    landed(up[0])
    up.append(send(14, part(left, 0), part(left, 0), after))
    landed(down[0])
    down.append(send(15, part(right, 1), part(right, 1), before))
    landed(up[1])
    swaps.append(send(17, whole(left), whole(left), partner))
    landed(down[1])
    swaps.append(send(18, whole(right), whole(right), partner))
    landed(up[2])
    landed(down[2])
    swaps.append(send(19, whole(far), whole(far), partner))
    for copies in swaps:
        landed(copies)
    started += up + down + swaps
    for copies in started:
        for copy in copies:
            copy.wait_send()


EXCHANGE_SCRATCH = [
    pltpu.SemaphoreType.DMA((2, 20)),
    pltpu.SemaphoreType.DMA((2, 20)),
    pltpu.SemaphoreType.DMA((2,)),
]


def gather_kernel(values, meta, values_out, meta_out, send_sems, recv_sems, local_sems):
    meet()
    exchange([values, meta], [values_out, meta_out], send_sems, recv_sems, local_sems)


def prepare_kernel(
    valid, slots, hits, white, taps, stream, angle, offset,
    message_out, meta_out, base_out, band,
    hold, taps_row, message, meta, send_sems, recv_sems, local_sems, halo_send, halo_recv,
):
    meet()
    z, y, core, x = grid_place()
    tm = x
    halos = [
        pltpu.make_async_remote_copy(
            src_ref=stream.at[pl.ds(7, 1)],
            dst_ref=hold.at[0],
            send_sem=halo_send.at[0],
            recv_sem=halo_recv.at[0],
            device_id=device_at(z, y, core, lax.rem(x + 1, 4)),
            device_id_type=MESH,
        ),
        pltpu.make_async_remote_copy(
            src_ref=stream.at[pl.ds(0, 1)],
            dst_ref=hold.at[1],
            send_sem=halo_send.at[1],
            recv_sem=halo_recv.at[1],
            device_id=device_at(z, y, core, lax.rem(x + 3, 4)),
            device_id_type=MESH,
        ),
    ]
    for copy in halos:
        copy.start()
    cosine = jnp.cos(2.0 * angle[...])
    sine = jnp.sin(2.0 * angle[...])
    place_of = offset[...].astype(jnp.float32)
    for block in range(BLOCKS):
        for half in range(2):
            row = 2 * block + half
            for part, values in enumerate((cosine, sine, place_of)):
                at = 8 * block + 4 * half + part + 1
                message[at : at + 1, :] = values[row : row + 1]
    taps_row[...] = jnp.zeros_like(taps_row)
    taps_row[:, : BAND + 1] = taps[...]
    spread = jnp.broadcast_to(taps_row[...], (WIN, WIN))
    shifted = pltpu.roll(spread, HALF, 1, stride=1, stride_axis=0)
    lag_row = lax.dot_general(
        spread[:8], shifted, NT, precision=HIGHEST, preferred_element_type=jnp.float32
    )
    lag_row = lag_row + jnp.where(lanes((8, WIN)) == HALF, white[0], 0.0)
    table = pltpu.roll(
        jnp.broadcast_to(lag_row[0:1], (WIN, WIN)), WIN - HALF - BAND, 1, stride=1, stride_axis=0
    )
    band[...] = table[:, :HALF]
    lag_zero = lag_row[0:1, HALF : HALF + 1]

    remaining = valid[0] - tm * SPAN
    lane = lanes((1, HALF))
    header = jnp.where(lane == 8, jnp.broadcast_to(lag_zero, (1, HALF)), 0.0)
    for block in range(BLOCKS):
        found = hits[slots[block]].astype(jnp.float32)
        count = jnp.clip(remaining - block * WIN, 0, WIN).astype(jnp.float32)
        header = jnp.where(lane == block, found, header)
        header = jnp.where(lane == 4 + block, count, header)
    meta[...] = header

    for copy in halos:
        copy.wait_recv()
    extended = jnp.concatenate(
        [hold[0], stream[...], hold[1], jnp.zeros((6, HALF), jnp.float32)], axis=0
    )
    place = (rows_of((16, HALF)) - 1) * HALF + lanes((16, HALF))
    extended = jnp.where((place < remaining) & (place + tm * SPAN >= 0), extended, 0.0)
    own_live = rows_of((8, HALF)) * HALF + lanes((8, HALF)) < remaining
    filtered = jnp.where(own_live, band_filter(extended, table[:, :HALF]), 0.0)
    for block in range(BLOCKS):
        for half in range(2):
            row = 2 * block + half
            at = 8 * block + 4 * half
            message[at : at + 1, :] = filtered[row : row + 1]
    base_out[...] = filtered
    exchange([message, meta], [message_out, meta_out], send_sems, recv_sems, local_sems)
    for copy in halos:
        copy.wait_send()


def split_rows(values):
    high = values.astype(jnp.bfloat16)
    rest = values - high.astype(jnp.float32)
    middle = rest.astype(jnp.bfloat16)
    low = (rest - middle.astype(jnp.float32)).astype(jnp.bfloat16)
    return jnp.concatenate([high, middle, low], axis=0)


def wide(tile, row):
    return jnp.concatenate([tile[row : row + 1], tile[row + 4 : row + 5]], axis=1)


def match_sum(column, places, values):
    count = values.shape[0]
    picked = jnp.where(column == places, 1.0, 0.0).astype(jnp.bfloat16)
    out = lax.dot_general(split_rows(values), picked, NT, preferred_element_type=jnp.float32)
    return out[:count] + out[count : 2 * count] + out[2 * count :]


def weight_rows(weight, cosine, sine):
    first = weight * cosine
    second = weight * sine
    return [weight, first, second, first * cosine, first * sine, second * sine]


def own_labels():
    z, y, core, x = grid_place()
    own = slot_of(z, y, core, x) * BLOCKS
    before = slot_of(z, y, core, jnp.maximum(x - 1, 0)) * BLOCKS + BLOCKS - 1
    after = slot_of(z, y, core, jnp.minimum(x + 1, 3)) * BLOCKS
    usable = [jnp.minimum(x, 1)] + [1] * BLOCKS + [jnp.minimum(3 - x, 1)]
    return [before] + [own + block for block in range(BLOCKS)] + [after], usable


def own_columns(labels, gathered):
    rows = []
    for seg in range(6):
        tile = gathered[labels[seg]]
        rows += [tile[3:4], tile[7:8]]
    rows.append(jnp.zeros((HALF - 12, HALF), jnp.float32))
    turned = jnp.concatenate(rows, axis=0).T
    return [
        jnp.concatenate([turned[:, 2 * s : 2 * s + 1], turned[:, 2 * s + 1 : 2 * s + 2]], axis=0)
        for s in range(6)
    ]


def adjugate(w1, w2, w3, w4, w5, w6):
    aa = 1.0 + w1
    bb = 1.0 + w4
    cc = 1.0 + w6
    m_aa = bb * cc - w5 * w5
    m_ab = w3 * w5 - w2 * cc
    m_ac = w2 * w5 - w3 * bb
    m_bb = aa * cc - w3 * w3
    m_bc = w2 * w3 - aa * w5
    m_cc = aa * bb - w2 * w2
    det = aa * m_aa + w2 * m_ab + w3 * m_ac
    return m_aa, m_ab, m_ac, m_bb, m_bc, m_cc, det


def rows_to_hold(signal, hold):
    hold[0:1] = signal[0:1, HALF:]
    for seg in range(1, 5):
        hold[2 * seg - 1 : 2 * seg] = signal[seg : seg + 1, :HALF]
        hold[2 * seg : 2 * seg + 1] = signal[seg : seg + 1, HALF:]
    hold[9:10] = signal[5:6, :HALF]


def total(values):
    return jnp.sum(jnp.sum(values, axis=1, keepdims=True), axis=0, keepdims=True)


def own_live_of(info):
    remaining = info[0] - lax.axis_index("tm") * SPAN
    return rows_of((8, HALF)) * HALF + lanes((8, HALF)) < remaining


def first_kernel(
    info, nexts, counts, lives, lag_zero, gathered, base, band,
    filtered_out, part_out, factors, signal_out, comps, hold,
):
    labels, flags = own_labels()
    columns = own_columns(labels, gathered)
    lane = lanes((1, WIN))
    comps[...] = jnp.zeros_like(comps)
    for seg in range(6):
        column = columns[seg]
        usable = flags[seg]

        def body(_, carry, column=column):
            label, acc = carry
            tile = gathered[label]
            f = wide(tile, 0)
            co = wide(tile, 1)
            si = wide(tile, 2)
            weight = jnp.where(lane < lives[label], lag_zero[label // BLOCKS], 0.0)
            values = jnp.concatenate(
                [f, f * co, f * si] + weight_rows(weight, co, si)
                + [jnp.zeros((7, WIN), jnp.float32)], axis=0,
            )
            return nexts[label], acc + match_sum(column, wide(tile, 3), values)

        start = labels[seg]
        _, acc = lax.fori_loop(
            0, counts[start] * usable, body, (start, jnp.zeros((16, WIN), jnp.float32))
        )
        for comp in range(9):
            comps[comp, seg : seg + 1, :] = acc[comp : comp + 1]
        tile = gathered[start]
        comps[9, seg : seg + 1, :] = wide(tile, 1)
        comps[10, seg : seg + 1, :] = wide(tile, 2)
        comps[11, seg : seg + 1, :] = jnp.where(lane < lives[start] * usable, 1.0, 0.0)
    m_aa, m_ab, m_ac, m_bb, m_bc, m_cc, det = adjugate(*(comps[c] for c in range(3, 9)))
    co, si, live = comps[9], comps[10], comps[11]
    scale = live / det
    q1 = (m_aa + m_ab * co + m_ac * si) * scale
    q2 = (m_ab + m_bb * co + m_bc * si) * scale
    q3 = (m_ac + m_bc * co + m_cc * si) * scale
    factors[0] = q1
    factors[1] = q2
    factors[2] = q3
    signal = q1 * comps[0] + q2 * comps[1] + q3 * comps[2]
    signal_out[...] = signal
    hold[...] = jnp.zeros_like(hold)
    rows_to_hold(signal, hold)
    filtered = jnp.where(own_live_of(info), band_filter(hold[...], band[...]), 0.0)
    filtered_out[...] = filtered
    own = hold[1:9]
    lane = lanes((1, HALF))
    part_out[...] = jnp.where(lane == 0, total(base[...] * own), 0.0) + jnp.where(
        lane == 1, total(filtered * own), 0.0
    )


def second_kernel(
    info, nexts, counts, gathered, second, parts, base, own_first, band, factors, signal_in,
    filtered_out, part_out, comps, hold,
):
    sums = jnp.sum(parts[...], axis=0, keepdims=True)
    alpha = sums[:, 0:1] / sums[:, 1:2]
    labels, flags = own_labels()
    columns = own_columns(labels, gathered)
    comps[...] = jnp.zeros_like(comps)
    for seg in range(6):
        column = columns[seg]

        def body(_, carry, column=column):
            label, acc = carry
            tile = gathered[label]
            pair = second[label]
            f = jnp.concatenate([pair[0:1], pair[1:2]], axis=1)
            values = jnp.concatenate(
                [f, f * wide(tile, 1), f * wide(tile, 2), jnp.zeros((13, WIN), jnp.float32)], axis=0
            )
            return nexts[label], acc + match_sum(column, wide(tile, 3), values)

        start = labels[seg]
        _, acc = lax.fori_loop(
            0, counts[start] * flags[seg], body, (start, jnp.zeros((16, WIN), jnp.float32))
        )
        for comp in range(3):
            comps[comp, seg : seg + 1, :] = acc[comp : comp + 1]
    change = factors[0] * comps[0] + factors[1] * comps[1] + factors[2] * comps[2]
    signal = signal_in[...] - alpha * change
    hold[...] = jnp.zeros_like(hold)
    rows_to_hold(signal, hold)
    filtered = jnp.where(own_live_of(info), band_filter(hold[...], band[...]), 0.0)
    filtered_out[...] = filtered
    own = hold[1:9]
    first = own_first[...]
    lane = lanes((1, HALF))
    part_out[...] = (
        jnp.where(lane == 0, total((base[...] - alpha * first) * own), 0.0)
        + jnp.where(lane == 1, total(filtered * own), 0.0)
        + jnp.where(lane == 2, total(first * own), 0.0)
    )


def last_kernel(
    heads, nexts, lives, lag_zero, gathered, second, third, parts_two, parts_three,
    solution_out, residual_out, comps,
):
    sums = jnp.sum(parts_two[...], axis=0, keepdims=True)
    product, curve = sums[:, 0:1], sums[:, 1:2]
    alpha = product / curve
    sums = jnp.sum(parts_three[...], axis=0, keepdims=True)
    product_next = sums[:, 0:1]
    beta = product_next / product
    curve_next = sums[:, 1:2] + 2.0 * beta * sums[:, 2:3] + beta * beta * curve
    alpha_next = product_next / curve_next
    column = rows_of((WIN, 1)).astype(jnp.float32)
    lane = lanes((1, WIN))
    for block in range(BPD):

        def body(_, carry):
            label, acc = carry
            tile = gathered[label]
            co = wide(tile, 1)
            si = wide(tile, 2)
            pair = second[label]
            trio = third[label]
            rows = []
            for f in (
                wide(tile, 0),
                jnp.concatenate([pair[0:1], pair[1:2]], axis=1),
                jnp.concatenate([trio[0:1], trio[1:2]], axis=1),
            ):
                rows += [f, f * co, f * si]
            weight = jnp.where(lane < lives[label], lag_zero[label // BLOCKS], 0.0)
            values = jnp.concatenate(
                rows + weight_rows(weight, co, si) + [jnp.zeros((1, WIN), jnp.float32)], axis=0
            )
            return nexts[label], acc + match_sum(column, wide(tile, 3), values)

        _, acc = lax.fori_loop(
            0, heads[BPD + block], body, (heads[block], jnp.zeros((16, WIN), jnp.float32))
        )
        for comp in range(15):
            comps[comp, block : block + 1, :] = acc[comp : comp + 1]
    m_aa, m_ab, m_ac, m_bb, m_bc, m_cc, det = adjugate(*(comps[c] for c in range(9, 15)))

    def solve(r1, r2, r3):
        return (
            (m_aa * r1 + m_ab * r2 + m_ac * r3) / det,
            (m_ab * r1 + m_bb * r2 + m_bc * r3) / det,
            (m_ac * r1 + m_bc * r2 + m_cc * r3) / det,
        )

    right = [comps[c] for c in range(3)]
    image = [comps[3 + c] for c in range(3)]
    other = [comps[6 + c] for c in range(3)]
    residual = [r - alpha * w for r, w in zip(right, image)]
    start = solve(*right)
    middle = solve(*residual)
    direction = [m + beta * s for m, s in zip(middle, start)]
    final = solve(
        *(r - alpha_next * (v + beta * w) for r, v, w in zip(residual, other, image))
    )
    for comp in range(3):
        answer = alpha * start[comp] + alpha_next * direction[comp]
        solution_out[comp] = answer
        residual_out[comp] = final[comp]


def f32(*shape):
    return jax.ShapeDtypeStruct(shape, jnp.float32)


def gathered_shape(rows):
    return f32(2, 8, 4, 4, rows, HALF)


def gather_rows(values, part, number):
    rows, parts = pl.pallas_call(
        gather_kernel,
        out_shape=(gathered_shape(8), gathered_shape(1)),
        in_specs=[vmem] * 2,
        out_specs=(vmem,) * 2,
        scratch_shapes=EXCHANGE_SCRATCH,
        compiler_params=pltpu.CompilerParams(collective_id=number, has_side_effects=True),
        name="gather",
    )(values, part)
    return rows.reshape(LABELS, 2, HALF), parts.reshape(DEVICES, HALF)


def per_device(
    time_streams, pol_angle, offsets, block_slots, hit_ids, valid_counts, filter_taps, white_weight
):
    valid = valid_counts.reshape(1)
    message, metas, base, band = pl.pallas_call(
        prepare_kernel,
        out_shape=(gathered_shape(32), gathered_shape(1), f32(8, HALF), f32(WIN, HALF)),
        in_specs=[smem] * 4 + [vmem] * 4,
        out_specs=(vmem,) * 4,
        scratch_shapes=[
            pltpu.VMEM((2, 1, HALF), jnp.float32),
            pltpu.VMEM((1, WIN), jnp.float32),
            pltpu.VMEM((32, HALF), jnp.float32),
            pltpu.VMEM((1, HALF), jnp.float32),
        ]
        + EXCHANGE_SCRATCH
        + [pltpu.SemaphoreType.DMA((2,)), pltpu.SemaphoreType.DMA((2,))],
        compiler_params=pltpu.CompilerParams(collective_id=0, has_side_effects=True),
        name="prepare",
    )(
        valid, block_slots.reshape(BLOCKS), hit_ids.reshape(-1), white_weight.reshape(1),
        filter_taps.reshape(1, BAND + 1), time_streams.reshape(8, HALF), pol_angle.reshape(8, HALF),
        offsets.reshape(8, HALF),
    )
    gathered = message.reshape(LABELS, 8, HALF)
    metas = metas.reshape(DEVICES, HALF)

    blocks = metas[:, 0:4].reshape(LABELS)
    lives = metas[:, 4:8].reshape(LABELS).astype(jnp.int32)
    lag_zero = metas[:, 8]
    order = jnp.arange(LABELS, dtype=jnp.int32)
    same = blocks[:, None] == blocks[None, :]
    ahead = (order[None, :] - order[:, None] - 1) % LABELS
    nexts = (order + 1 + jnp.min(jnp.where(same, ahead, LABELS), axis=1)) % LABELS
    counts = jnp.sum(same, axis=1, dtype=jnp.int32)
    owned = (lax.axis_index("det") * BPD + jnp.arange(BPD, dtype=jnp.int32)).astype(jnp.float32)
    mine = owned[:, None] == blocks[None, :]
    heads = jnp.concatenate(
        [
            jnp.min(jnp.where(mine, order[None, :], LABELS - 1), axis=1),
            jnp.sum(mine, axis=1, dtype=jnp.int32),
        ]
    )

    first, part_one, factors, signal = pl.pallas_call(
        first_kernel,
        out_shape=(f32(8, HALF), f32(1, HALF), f32(3, 8, WIN), f32(8, WIN)),
        in_specs=[smem] * 5 + [vmem] * 3,
        out_specs=(vmem,) * 4,
        scratch_shapes=[
            pltpu.VMEM((12, 8, WIN), jnp.float32),
            pltpu.VMEM((16, HALF), jnp.float32),
        ],
        name="first",
    )(valid, nexts, counts, lives, lag_zero, gathered, base, band)
    second, parts_two = gather_rows(first, part_one, 1)
    other, part_two = pl.pallas_call(
        second_kernel,
        out_shape=(f32(8, HALF), f32(1, HALF)),
        in_specs=[smem] * 3 + [vmem] * 8,
        out_specs=(vmem,) * 2,
        scratch_shapes=[
            pltpu.VMEM((3, 8, WIN), jnp.float32),
            pltpu.VMEM((16, HALF), jnp.float32),
        ],
        name="second",
    )(valid, nexts, counts, gathered, second, parts_two, base, first, band, factors, signal)
    third, parts_three = gather_rows(other, part_two, 2)
    answers = pl.pallas_call(
        last_kernel,
        out_shape=(f32(3, BPD, WIN), f32(3, BPD, WIN)),
        in_specs=[smem] * 4 + [vmem] * 5,
        out_specs=(vmem,) * 2,
        scratch_shapes=[pltpu.VMEM((15, BPD, WIN), jnp.float32)],
        name="last",
    )(heads, nexts, lives, lag_zero, gathered, second, third, parts_two, parts_three)
    return tuple(jnp.transpose(answer, (1, 0, 2)) for answer in answers)


def solution(mesh):
    in_specs = (
        P("det", None, "tm"),
        P("det", None, "tm"),
        P("det", None, "tm"),
        P("det", None, "tm"),
        P("det", None),
        P("det", None),
        P("det", None, None),
        P("det", None),
    )
    out_specs = (P("det", None, None), P("det", None, None))
    return jax.shard_map(
        per_device, mesh=mesh, in_specs=in_specs, out_specs=out_specs, check_vma=False
    )
```

```python
import functools

import jax
import jax.numpy as jnp
from jax import lax
from jax.experimental import pallas as pl
from jax.experimental.pallas import tpu as pltpu
from jax.sharding import PartitionSpec as P

WIN = 256
BAND = 64
BPD = 16
HALF = 128
SPAN = 1024
BLOCKS = 4
DEVICES = 256
PAIRS = 28
SLOTS = 40
LABELS = DEVICES * BLOCKS

HIGHEST = lax.Precision.HIGHEST
NT = (((1,), (1,)), ((), ()))
MESH = pl.DeviceIdType.MESH

vmem = pl.BlockSpec(memory_space=pltpu.VMEM)
smem = pl.BlockSpec(memory_space=pltpu.SMEM)


def lanes(shape):
    return lax.broadcasted_iota(jnp.int32, shape, len(shape) - 1)


def rows_of(shape):
    return lax.broadcasted_iota(jnp.int32, shape, 0)


def band_filter(extended, band):
    turned = pltpu.roll(extended, HALF // 2, 1)
    keep = lanes((8, HALF)) < HALF // 2
    first = jnp.where(keep, turned[0:8], turned[1:9])
    second = jnp.where(keep, turned[1:9], turned[2:10])
    window = jnp.concatenate([first, second], axis=1)
    return jnp.dot(window, band, precision=HIGHEST, preferred_element_type=jnp.float32)


def grid_place():
    det = lax.axis_index("det")
    x = lax.axis_index("tm")
    return lax.div(det, 8), lax.rem(lax.div(det, 2), 4), lax.rem(det, 2), x


def device_at(z, y, core, x):
    return {"det": (z * 4 + y) * 2 + core, "tm": x}


def slot_of(z, y, core, x):
    major = y + core * (x - y)
    minor = x + core * (y - x)
    return ((core * 8 + z) * 4 + major) * 4 + minor


def meet():
    z, y, core, x = grid_place()
    barrier = pltpu.get_barrier_semaphore()
    peers = (
        [device_at(lax.rem(z + d, 8), y, core, x) for d in range(1, 8)]
        + [device_at(z, lax.rem(y + d, 4), core, x) for d in range(1, 4)]
        + [device_at(z, y, core, lax.rem(x + d, 4)) for d in range(1, 4)]
        + [device_at(z, y, 1 - core, x)]
    )
    for peer in peers:
        pl.semaphore_signal(barrier, inc=1, device_id=peer, device_id_type=MESH)
    pl.semaphore_wait(barrier, len(peers))


def exchange(sources, buffers, send_sems, recv_sems, local_sems):
    z, y, core, x = grid_place()
    a = y + core * (x - y)
    b = x + core * (y - x)

    def major_peer(step):
        return device_at(
            z,
            y + (1 - core) * (lax.rem(y + step, 4) - y),
            core,
            x + core * (lax.rem(x + step, 4) - x),
        )

    def minor_peer(step):
        return device_at(
            z,
            y + core * (lax.rem(y + step, 4) - y),
            core,
            x + (1 - core) * (lax.rem(x + step, 4) - x),
        )

    arrays = range(len(sources))

    def send(number, source_of, target_of, peer):
        copies = []
        for i in arrays:
            copy = pltpu.make_async_remote_copy(
                src_ref=source_of(i),
                dst_ref=target_of(i),
                send_sem=send_sems.at[i, number],
                recv_sem=recv_sems.at[i, number],
                device_id=peer,
                device_id_type=MESH,
            )
            copy.start()
            copies.append(copy)
        return copies

    def landed(copies):
        for copy in copies:
            copy.wait_recv()

    started = []
    keep = [
        pltpu.make_async_copy(sources[i], buffers[i].at[core, z, a, b], local_sems.at[i])
        for i in arrays
    ]
    first = [
        send(
            d - 1,
            lambda i: sources[i],
            lambda i: buffers[i].at[core, z, a, b],
            device_at(lax.rem(z + d, 8), y, core, x),
        )
        for d in (4, 3, 5, 2, 6, 1, 7)
    ]
    for copy in keep:
        copy.start()
    for copy in keep:
        copy.wait()
    for copies in first:
        landed(copies)
    started += first

    def column(i):
        return buffers[i].at[core, :, a, b]

    second = [send(6 + d, column, column, major_peer(d)) for d in (2, 1, 3)]
    for copies in second:
        landed(copies)
    started += second

    def part(number, half):
        depth = pl.ds(4 * half, 4)
        return lambda i: buffers[i].at[core, depth, :, number]

    def whole(number):
        return lambda i: buffers[i].at[core, :, :, number]

    after = minor_peer(1)
    before = minor_peer(3)
    partner = device_at(z, y, 1 - core, x)
    left = lax.rem(b + 3, 4)
    right = lax.rem(b + 1, 4)
    far = lax.rem(b + 2, 4)
    up = [send(10, part(b, 0), part(b, 0), after)]
    down = [send(12, part(b, 1), part(b, 1), before)]
    up.append(send(11, part(b, 1), part(b, 1), after))
    down.append(send(13, part(b, 0), part(b, 0), before))
    swaps = [send(16, whole(b), whole(b), partner)]
    landed(up[0])
    up.append(send(14, part(left, 0), part(left, 0), after))
    landed(down[0])
    down.append(send(15, part(right, 1), part(right, 1), before))
    landed(up[1])
    swaps.append(send(17, whole(left), whole(left), partner))
    landed(down[1])
    swaps.append(send(18, whole(right), whole(right), partner))
    landed(up[2])
    landed(down[2])
    swaps.append(send(19, whole(far), whole(far), partner))
    for copies in swaps:
        landed(copies)
    started += up + down + swaps
    for copies in started:
        for copy in copies:
            copy.wait_send()


EXCHANGE_SCRATCH = [
    pltpu.SemaphoreType.DMA((2, 20)),
    pltpu.SemaphoreType.DMA((2, 20)),
    pltpu.SemaphoreType.DMA((2,)),
]


def gather_kernel(values, meta, values_out, meta_out, send_sems, recv_sems, local_sems):
    meet()
    exchange([values, meta], [values_out, meta_out], send_sems, recv_sems, local_sems)


def prepare_kernel(
    valid, slots, hits, white, taps, stream, angle, offset,
    message_out, meta_out, base_out, band,
    hold, taps_row, message, meta, send_sems, recv_sems, local_sems, halo_send, halo_recv,
):
    meet()
    z, y, core, x = grid_place()
    tm = x
    halos = [
        pltpu.make_async_remote_copy(
            src_ref=stream.at[pl.ds(7, 1)],
            dst_ref=hold.at[0],
            send_sem=halo_send.at[0],
            recv_sem=halo_recv.at[0],
            device_id=device_at(z, y, core, lax.rem(x + 1, 4)),
            device_id_type=MESH,
        ),
        pltpu.make_async_remote_copy(
            src_ref=stream.at[pl.ds(0, 1)],
            dst_ref=hold.at[1],
            send_sem=halo_send.at[1],
            recv_sem=halo_recv.at[1],
            device_id=device_at(z, y, core, lax.rem(x + 3, 4)),
            device_id_type=MESH,
        ),
    ]
    for copy in halos:
        copy.start()
    cosine = jnp.cos(2.0 * angle[...])
    sine = jnp.sin(2.0 * angle[...])
    place_of = offset[...].astype(jnp.float32)
    for block in range(BLOCKS):
        for half in range(2):
            row = 2 * block + half
            for part, values in enumerate((cosine, sine, place_of)):
                at = 8 * block + 4 * half + part + 1
                message[at : at + 1, :] = values[row : row + 1]
    taps_row[...] = jnp.zeros_like(taps_row)
    taps_row[:, : BAND + 1] = taps[...]
    spread = jnp.broadcast_to(taps_row[...], (WIN, WIN))
    shifted = pltpu.roll(spread, HALF, 1, stride=1, stride_axis=0)
    lag_row = lax.dot_general(
        spread[:8], shifted, NT, precision=HIGHEST, preferred_element_type=jnp.float32
    )
    lag_row = lag_row + jnp.where(lanes((8, WIN)) == HALF, white[0], 0.0)
    table = pltpu.roll(
        jnp.broadcast_to(lag_row[0:1], (WIN, WIN)), WIN - HALF - BAND, 1, stride=1, stride_axis=0
    )
    band[...] = table[:, :HALF]
    lag_zero = lag_row[0:1, HALF : HALF + 1]

    remaining = valid[0] - tm * SPAN
    lane = lanes((1, HALF))
    header = jnp.where(lane == 8, jnp.broadcast_to(lag_zero, (1, HALF)), 0.0)
    for block in range(BLOCKS):
        found = hits[slots[block]].astype(jnp.float32)
        count = jnp.clip(remaining - block * WIN, 0, WIN).astype(jnp.float32)
        header = jnp.where(lane == block, found, header)
        header = jnp.where(lane == 4 + block, count, header)
    meta[...] = header

    for copy in halos:
        copy.wait_recv()
    extended = jnp.concatenate(
        [hold[0], stream[...], hold[1], jnp.zeros((6, HALF), jnp.float32)], axis=0
    )
    place = (rows_of((16, HALF)) - 1) * HALF + lanes((16, HALF))
    extended = jnp.where((place < remaining) & (place + tm * SPAN >= 0), extended, 0.0)
    own_live = rows_of((8, HALF)) * HALF + lanes((8, HALF)) < remaining
    filtered = jnp.where(own_live, band_filter(extended, table[:, :HALF]), 0.0)
    for block in range(BLOCKS):
        for half in range(2):
            row = 2 * block + half
            at = 8 * block + 4 * half
            message[at : at + 1, :] = filtered[row : row + 1]
    base_out[...] = filtered
    exchange([message, meta], [message_out, meta_out], send_sems, recv_sems, local_sems)
    for copy in halos:
        copy.wait_send()


def split_rows(values):
    high = values.astype(jnp.bfloat16)
    rest = values - high.astype(jnp.float32)
    middle = rest.astype(jnp.bfloat16)
    low = (rest - middle.astype(jnp.float32)).astype(jnp.bfloat16)
    return jnp.concatenate([high, middle, low], axis=0)


def wide(tile, row):
    return jnp.concatenate([tile[row : row + 1], tile[row + 4 : row + 5]], axis=1)


def match_sum(column, places, values):
    count = values.shape[0]
    picked = jnp.where(column == places, 1.0, 0.0).astype(jnp.bfloat16)
    out = lax.dot_general(split_rows(values), picked, NT, preferred_element_type=jnp.float32)
    return out[:count] + out[count : 2 * count] + out[2 * count :]


def weight_rows(weight, cosine, sine):
    first = weight * cosine
    second = weight * sine
    return [weight, first, second, first * cosine, first * sine, second * sine]


def own_labels():
    z, y, core, x = grid_place()
    own = slot_of(z, y, core, x) * BLOCKS
    before = slot_of(z, y, core, jnp.maximum(x - 1, 0)) * BLOCKS + BLOCKS - 1
    after = slot_of(z, y, core, jnp.minimum(x + 1, 3)) * BLOCKS
    usable = [jnp.minimum(x, 1)] + [1] * BLOCKS + [jnp.minimum(3 - x, 1)]
    return [before] + [own + block for block in range(BLOCKS)] + [after], usable


def own_columns(labels, gathered):
    rows = []
    for seg in range(6):
        tile = gathered[labels[seg]]
        rows += [tile[3:4], tile[7:8]]
    rows.append(jnp.zeros((HALF - 12, HALF), jnp.float32))
    turned = jnp.concatenate(rows, axis=0).T
    return [
        jnp.concatenate([turned[:, 2 * s : 2 * s + 1], turned[:, 2 * s + 1 : 2 * s + 2]], axis=0)
        for s in range(6)
    ]


def adjugate(w1, w2, w3, w4, w5, w6):
    aa = 1.0 + w1
    bb = 1.0 + w4
    cc = 1.0 + w6
    m_aa = bb * cc - w5 * w5
    m_ab = w3 * w5 - w2 * cc
    m_ac = w2 * w5 - w3 * bb
    m_bb = aa * cc - w3 * w3
    m_bc = w2 * w3 - aa * w5
    m_cc = aa * bb - w2 * w2
    det = aa * m_aa + w2 * m_ab + w3 * m_ac
    return m_aa, m_ab, m_ac, m_bb, m_bc, m_cc, det


def rows_to_hold(signal, hold):
    hold[0:1] = signal[0:1, HALF:]
    for seg in range(1, 5):
        hold[2 * seg - 1 : 2 * seg] = signal[seg : seg + 1, :HALF]
        hold[2 * seg : 2 * seg + 1] = signal[seg : seg + 1, HALF:]
    hold[9:10] = signal[5:6, :HALF]


def total(values):
    return jnp.sum(jnp.sum(values, axis=1, keepdims=True), axis=0, keepdims=True)


def own_live_of(info):
    remaining = info[0] - lax.axis_index("tm") * SPAN
    return rows_of((8, HALF)) * HALF + lanes((8, HALF)) < remaining


def first_kernel(
    info, nexts, counts, lives, lag_zero, gathered, base, band,
    filtered_out, part_out, factors, signal_out, comps, hold,
):
    labels, flags = own_labels()
    columns = own_columns(labels, gathered)
    lane = lanes((1, WIN))
    comps[...] = jnp.zeros_like(comps)
    for seg in range(6):
        column = columns[seg]
        usable = flags[seg]

        def body(_, carry, column=column):
            label, acc = carry
            tile = gathered[label]
            f = wide(tile, 0)
            co = wide(tile, 1)
            si = wide(tile, 2)
            weight = jnp.where(lane < lives[label], lag_zero[label // BLOCKS], 0.0)
            values = jnp.concatenate(
                [f, f * co, f * si] + weight_rows(weight, co, si)
                + [jnp.zeros((7, WIN), jnp.float32)], axis=0,
            )
            return nexts[label], acc + match_sum(column, wide(tile, 3), values)

        start = labels[seg]
        _, acc = lax.fori_loop(
            0, counts[start] * usable, body, (start, jnp.zeros((16, WIN), jnp.float32))
        )
        for comp in range(9):
            comps[comp, seg : seg + 1, :] = acc[comp : comp + 1]
        tile = gathered[start]
        comps[9, seg : seg + 1, :] = wide(tile, 1)
        comps[10, seg : seg + 1, :] = wide(tile, 2)
        comps[11, seg : seg + 1, :] = jnp.where(lane < lives[start] * usable, 1.0, 0.0)
    m_aa, m_ab, m_ac, m_bb, m_bc, m_cc, det = adjugate(*(comps[c] for c in range(3, 9)))
    co, si, live = comps[9], comps[10], comps[11]
    scale = live / det
    q1 = (m_aa + m_ab * co + m_ac * si) * scale
    q2 = (m_ab + m_bb * co + m_bc * si) * scale
    q3 = (m_ac + m_bc * co + m_cc * si) * scale
    factors[0] = q1
    factors[1] = q2
    factors[2] = q3
    signal = q1 * comps[0] + q2 * comps[1] + q3 * comps[2]
    signal_out[...] = signal
    hold[...] = jnp.zeros_like(hold)
    rows_to_hold(signal, hold)
    filtered = jnp.where(own_live_of(info), band_filter(hold[...], band[...]), 0.0)
    filtered_out[...] = filtered
    own = hold[1:9]
    lane = lanes((1, HALF))
    part_out[...] = jnp.where(lane == 0, total(base[...] * own), 0.0) + jnp.where(
        lane == 1, total(filtered * own), 0.0
    )


def second_kernel(
    info, nexts, counts, gathered, second, parts, base, own_first, band, factors, signal_in,
    filtered_out, part_out, comps, hold,
):
    sums = jnp.sum(parts[...], axis=0, keepdims=True)
    alpha = sums[:, 0:1] / sums[:, 1:2]
    labels, flags = own_labels()
    columns = own_columns(labels, gathered)
    comps[...] = jnp.zeros_like(comps)
    for seg in range(6):
        column = columns[seg]

        def body(_, carry, column=column):
            label, acc = carry
            tile = gathered[label]
            pair = second[label]
            f = jnp.concatenate([pair[0:1], pair[1:2]], axis=1)
            values = jnp.concatenate(
                [f, f * wide(tile, 1), f * wide(tile, 2), jnp.zeros((13, WIN), jnp.float32)], axis=0
            )
            return nexts[label], acc + match_sum(column, wide(tile, 3), values)

        start = labels[seg]
        _, acc = lax.fori_loop(
            0, counts[start] * flags[seg], body, (start, jnp.zeros((16, WIN), jnp.float32))
        )
        for comp in range(3):
            comps[comp, seg : seg + 1, :] = acc[comp : comp + 1]
    change = factors[0] * comps[0] + factors[1] * comps[1] + factors[2] * comps[2]
    signal = signal_in[...] - alpha * change
    hold[...] = jnp.zeros_like(hold)
    rows_to_hold(signal, hold)
    filtered = jnp.where(own_live_of(info), band_filter(hold[...], band[...]), 0.0)
    filtered_out[...] = filtered
    own = hold[1:9]
    first = own_first[...]
    lane = lanes((1, HALF))
    part_out[...] = (
        jnp.where(lane == 0, total((base[...] - alpha * first) * own), 0.0)
        + jnp.where(lane == 1, total(filtered * own), 0.0)
        + jnp.where(lane == 2, total(first * own), 0.0)
    )


def last_kernel(
    heads, nexts, lives, lag_zero, gathered, second, third, parts_two, parts_three,
    solution_out, residual_out, comps,
):
    sums = jnp.sum(parts_two[...], axis=0, keepdims=True)
    product, curve = sums[:, 0:1], sums[:, 1:2]
    alpha = product / curve
    sums = jnp.sum(parts_three[...], axis=0, keepdims=True)
    product_next = sums[:, 0:1]
    beta = product_next / product
    curve_next = sums[:, 1:2] + 2.0 * beta * sums[:, 2:3] + beta * beta * curve
    alpha_next = product_next / curve_next
    column = rows_of((WIN, 1)).astype(jnp.float32)
    lane = lanes((1, WIN))
    for block in range(BPD):

        def body(_, carry):
            label, acc = carry
            tile = gathered[label]
            co = wide(tile, 1)
            si = wide(tile, 2)
            pair = second[label]
            trio = third[label]
            rows = []
            for f in (
                wide(tile, 0),
                jnp.concatenate([pair[0:1], pair[1:2]], axis=1),
                jnp.concatenate([trio[0:1], trio[1:2]], axis=1),
            ):
                rows += [f, f * co, f * si]
            weight = jnp.where(lane < lives[label], lag_zero[label // BLOCKS], 0.0)
            values = jnp.concatenate(
                rows + weight_rows(weight, co, si) + [jnp.zeros((1, WIN), jnp.float32)], axis=0
            )
            return nexts[label], acc + match_sum(column, wide(tile, 3), values)

        _, acc = lax.fori_loop(
            0, heads[BPD + block], body, (heads[block], jnp.zeros((16, WIN), jnp.float32))
        )
        for comp in range(15):
            comps[comp, block : block + 1, :] = acc[comp : comp + 1]
    m_aa, m_ab, m_ac, m_bb, m_bc, m_cc, det = adjugate(*(comps[c] for c in range(9, 15)))

    def solve(r1, r2, r3):
        return (
            (m_aa * r1 + m_ab * r2 + m_ac * r3) / det,
            (m_ab * r1 + m_bb * r2 + m_bc * r3) / det,
            (m_ac * r1 + m_bc * r2 + m_cc * r3) / det,
        )

    right = [comps[c] for c in range(3)]
    image = [comps[3 + c] for c in range(3)]
    other = [comps[6 + c] for c in range(3)]
    residual = [r - alpha * w for r, w in zip(right, image)]
    start = solve(*right)
    middle = solve(*residual)
    direction = [m + beta * s for m, s in zip(middle, start)]
    final = solve(
        *(r - alpha_next * (v + beta * w) for r, v, w in zip(residual, other, image))
    )
    for comp in range(3):
        answer = alpha * start[comp] + alpha_next * direction[comp]
        solution_out[comp] = answer
        residual_out[comp] = final[comp]


class Mover:
    def __init__(self, source, buffer, sems, number):
        self.source, self.buffer = source, buffer
        self.send_sems, self.recv_sems, self.local_sems = sems
        self.number = number
        self.z, self.y, self.core, self.x = grid_place()
        self.a = self.y + self.core * (self.x - self.y)
        self.b = self.x + self.core * (self.y - self.x)
        self.started = []

    def major_peer(self, step):
        z, y, core, x = self.z, self.y, self.core, self.x
        return device_at(
            z,
            y + (1 - core) * (lax.rem(y + step, 4) - y),
            core,
            x + core * (lax.rem(x + step, 4) - x),
        )

    def minor_peer(self, step):
        z, y, core, x = self.z, self.y, self.core, self.x
        return device_at(
            z,
            y + core * (lax.rem(y + step, 4) - y),
            core,
            x + (1 - core) * (lax.rem(x + step, 4) - x),
        )

    def send(self, number, source, target, peer):
        copy = pltpu.make_async_remote_copy(
            src_ref=source,
            dst_ref=target,
            send_sem=self.send_sems.at[self.number, number],
            recv_sem=self.recv_sems.at[self.number, number],
            device_id=peer,
            device_id_type=MESH,
        )
        copy.start()
        self.started.append(copy)
        return copy

    def start_first(self):
        z, y, core, x = self.z, self.y, self.core, self.x
        own = self.buffer.at[core, z, self.a, self.b]
        self.first = [
            self.send(d - 1, self.source, own, device_at(lax.rem(z + d, 8), y, core, x))
            for d in (4, 3, 5, 2, 6, 1, 7)
        ]
        self.keep = pltpu.make_async_copy(self.source, own, self.local_sems.at[self.number])
        self.keep.start()

    def start_second(self):
        self.keep.wait()
        for copy in self.first:
            copy.wait_recv()
        column = self.buffer.at[self.core, :, self.a, self.b]
        self.second = [self.send(6 + d, column, column, self.major_peer(d)) for d in (2, 1, 3)]

    def part(self, number, half):
        return self.buffer.at[self.core, pl.ds(4 * half, 4), :, number]

    def whole(self, number):
        return self.buffer.at[self.core, :, :, number]

    def pass_on(self, number, ref, peer):
        return self.send(number, ref, ref, peer)

    def start_small(self):
        for copy in self.second:
            copy.wait_recv()
        self.third = [
            self.pass_on(9 + d, self.whole(self.b), self.minor_peer(d)) for d in (2, 1, 3)
        ]

    def start_small_swap(self):
        for copy in self.third:
            copy.wait_recv()
        partner = device_at(self.z, self.y, 1 - self.core, self.x)
        self.swaps = [self.pass_on(16, self.buffer.at[self.core], partner)]

    def start_third(self):
        for copy in self.second:
            copy.wait_recv()
        self.after, self.before = self.minor_peer(1), self.minor_peer(3)
        self.partner = device_at(self.z, self.y, 1 - self.core, self.x)
        self.up = [self.pass_on(10, self.part(self.b, 0), self.after)]
        self.down = [self.pass_on(12, self.part(self.b, 1), self.before)]
        self.up.append(self.pass_on(11, self.part(self.b, 1), self.after))
        self.down.append(self.pass_on(13, self.part(self.b, 0), self.before))
        self.swaps = [self.pass_on(16, self.whole(self.b), self.partner)]

    def forward(self):
        left, right = lax.rem(self.b + 3, 4), lax.rem(self.b + 1, 4)
        self.up[0].wait_recv()
        self.up.append(self.pass_on(14, self.part(left, 0), self.after))
        self.down[0].wait_recv()
        self.down.append(self.pass_on(15, self.part(right, 1), self.before))

    def near(self):
        left, right = lax.rem(self.b + 3, 4), lax.rem(self.b + 1, 4)
        self.up[1].wait_recv()
        self.swaps.append(self.pass_on(17, self.whole(left), self.partner))
        self.down[1].wait_recv()
        self.swaps.append(self.pass_on(18, self.whole(right), self.partner))

    def far(self):
        far = lax.rem(self.b + 2, 4)
        self.up[2].wait_recv()
        self.down[2].wait_recv()
        self.swaps.append(self.pass_on(19, self.whole(far), self.partner))

    def arrive(self):
        for copy in self.swaps:
            copy.wait_recv()

    def finish(self):
        for copy in self.started:
            copy.wait_send()


def locate(label):
    return (
        lax.shift_right_logical(label, 9) & 1,
        lax.shift_right_logical(label, 6) & 7,
        lax.shift_right_logical(label, 4) & 3,
        lax.shift_right_logical(label, 2) & 3,
        label & 3,
    )


def joined(tile):
    return jnp.concatenate([tile[0:1], tile[1:2]], axis=1)


def split_product(rows, picked):
    count = len(rows)
    values = jnp.concatenate(rows, axis=0)
    high = values.astype(jnp.bfloat16).astype(jnp.float32)
    rest = values - high
    middle = rest.astype(jnp.bfloat16).astype(jnp.float32)
    low = rest - middle
    pad = -3 * count % 16
    stack = [high, middle, low]
    if pad:
        stack.append(jnp.zeros((pad, WIN), jnp.float32))
    left = jnp.concatenate(stack, axis=0).astype(jnp.bfloat16)
    out = lax.dot_general(left, picked, NT, preferred_element_type=jnp.float32)
    return [
        out[c : c + 1] + out[count + c : count + c + 1] + out[2 * count + c : 2 * count + c + 1]
        for c in range(count)
    ]


def matches(column, places):
    low = jnp.where(column == places[0:1], 1.0, 0.0)
    high = jnp.where(column == places[1:2], 1.0, 0.0)
    return jnp.concatenate([low, high], axis=1).astype(jnp.bfloat16)


def make_lists(metas, list_a, list_b, live_a, live_b, lag_a, lag_b):
    z, y, core, x = grid_place()
    labels, usable = own_labels()
    table = metas[...].reshape(DEVICES, HALF).T
    blocks = jnp.concatenate(
        [table[j : j + 1, HALF * h : HALF * h + HALF] for j in range(4) for h in range(2)], axis=0
    )
    lives = jnp.concatenate(
        [table[4 + j : 5 + j, HALF * h : HALF * h + HALF] for j in range(4) for h in range(2)], axis=0
    )
    lags = jnp.concatenate(
        [table[8:9, HALF * h : HALF * h + HALF] for _ in range(4) for h in range(2)], axis=0
    )
    row = rows_of((8, HALF))
    label = (((row & 1) * HALF + lanes((8, HALF))) * 4 + lax.shift_right_logical(row, 1)).astype(
        jnp.float32
    )
    masks = []
    for seg in range(6):
        c, zz, a, b, _ = locate(labels[seg])
        number = (3, 0, 1, 2, 3, 0)[seg]
        own = metas[c, zz, a, b][:, number : number + 1]
        flag = usable[seg] if isinstance(usable[seg], int) else usable[seg].astype(jnp.float32)
        masks.append(jnp.where(blocks == own, 1.0, 0.0) * flag)
    det = lax.axis_index("det")
    base = (det * BPD).astype(jnp.float32)
    masks.append(jnp.where((blocks >= base) & (blocks < base + BPD), 1.0, 0.0))
    masks.append(jnp.zeros((8, HALF), jnp.float32))
    mask = jnp.concatenate(masks, axis=0)
    ahead = jnp.where(rows_of((HALF, HALF)) < lanes((HALF, HALF)), 1.0, 0.0)
    within = jnp.dot(mask, ahead, precision=HIGHEST, preferred_element_type=jnp.float32)
    totals = jnp.broadcast_to(jnp.sum(mask, axis=1, keepdims=True), (64, HALF))
    above = jnp.where(
        (rows_of((64, 64)) > lanes((64, 64))) & ((rows_of((64, 64)) >= 48) == (lanes((64, 64)) >= 48)),
        1.0, 0.0,
    )
    rank = within + jnp.dot(above, totals, precision=HIGHEST, preferred_element_type=jnp.float32)
    rank = jnp.where(mask > 0.0, rank, -1.0)
    count_a = jnp.sum(totals[0:48, 0:1], axis=0, keepdims=True)
    count_b = jnp.sum(totals[48:56, 0:1], axis=0, keepdims=True)
    over = jnp.where((count_a > PAIRS) | (count_b > SLOTS), 1.0, 0.0)

    def fill(rows, first, size, code_of, list_ref, live_ref, lag_ref):
        wanted = rows_of((size, HALF)).astype(jnp.float32)
        code = jnp.zeros((size, HALF), jnp.float32)
        live = jnp.zeros((size, HALF), jnp.float32)
        lag = jnp.zeros((size, HALF), jnp.float32)
        for r in range(rows):
            k = r % 8
            hit = wanted == rank[first + r : first + r + 1]
            code += jnp.where(hit, code_of(r), 0.0)
            live += jnp.where(hit, lives[k : k + 1], 0.0)
            lag += jnp.where(hit, lags[k : k + 1], 0.0)

        def spread(values):
            return jnp.broadcast_to(jnp.sum(values, axis=1, keepdims=True), (size, HALF))

        list_ref[...] = spread(code).astype(jnp.int32)
        live_ref[...] = spread(live)
        lag_ref[...] = spread(lag)

    fill(
        48, 0, 32, lambda r: label[r % 8 : r % 8 + 1] * 8.0 + (r // 8 + 1.0), list_a, live_a, lag_a
    )
    fill(
        8, 48, SLOTS, lambda r: label[r : r + 1] * 32.0 + (blocks[r : r + 1] - base + 1.0),
        list_b, live_b, lag_b,
    )
    return over


def whole_kernel(
    valid, slots, hits, white, taps, stream, angle, offset,
    solution_out, residual_out, over_out,
    hold, taps_row, fixed, meta, base, message, row_two, message_two,
    all_fixed, all_meta, all_base, all_first, meta_two, all_second, meta_three,
    columns, picked_a, picked_b, trig_a, trig_b, list_a, list_b, live_a, live_b, lag_a, lag_b,
    near_a, near_b, comps, owned, factors, halo_rows,
    send_sems, recv_sems, local_sems, halo_send, halo_recv, list_sems,
):
    z, y, core, x = grid_place()
    tm = x
    barrier = pltpu.get_barrier_semaphore()
    peers = (
        [device_at(lax.rem(z + d, 8), y, core, x) for d in range(1, 8)]
        + [device_at(z, lax.rem(y + d, 4), core, x) for d in range(1, 4)]
        + [device_at(z, y, core, lax.rem(x + d, 4)) for d in range(1, 4)]
        + [device_at(z, y, 1 - core, x)]
    )
    for peer in peers:
        pl.semaphore_signal(barrier, inc=1, device_id=peer, device_id_type=MESH)

    place_of = offset[...].astype(jnp.float32)
    for block in range(BLOCKS):
        fixed[block, 0:2, :] = angle[2 * block : 2 * block + 2]
        fixed[block, 2:4, :] = place_of[2 * block : 2 * block + 2]
    taps_row[...] = jnp.zeros_like(taps_row)
    taps_row[:, : BAND + 1] = taps[...]
    spread = jnp.broadcast_to(taps_row[...], (WIN, WIN))
    shifted = pltpu.roll(spread, HALF, 1, stride=1, stride_axis=0)
    lag_row = lax.dot_general(
        spread[:8], shifted, NT, precision=HIGHEST, preferred_element_type=jnp.float32
    )
    lag_row = lag_row + jnp.where(lanes((8, WIN)) == HALF, white[0], 0.0)
    band = pltpu.roll(
        jnp.broadcast_to(lag_row[0:1], (WIN, WIN)), WIN - HALF - BAND, 1, stride=1, stride_axis=0
    )[:, :HALF]
    lag_zero = lag_row[0:1, HALF : HALF + 1]
    remaining = valid[0] - tm * SPAN
    lane = lanes((1, HALF))
    header = jnp.where(lane == 8, jnp.broadcast_to(lag_zero, (1, HALF)), 0.0)
    for block in range(BLOCKS):
        found = hits[slots[block]].astype(jnp.float32)
        count = jnp.clip(remaining - block * WIN, 0, WIN).astype(jnp.float32)
        header = jnp.where(lane == block, found, header)
        header = jnp.where(lane == 4 + block, count, header)
    meta[...] = header
    own_live = rows_of((8, HALF)) * HALF + lanes((8, HALF)) < remaining

    pl.semaphore_wait(barrier, len(peers))
    halos = [
        pltpu.make_async_remote_copy(
            src_ref=stream.at[pl.ds(at, 1)],
            dst_ref=hold.at[i],
            send_sem=halo_send.at[i],
            recv_sem=halo_recv.at[i],
            device_id=device_at(z, y, core, lax.rem(x + step, 4)),
            device_id_type=MESH,
        )
        for i, (at, step) in enumerate(((7, 1), (0, 3)))
    ]
    for copy in halos:
        copy.start()
    sems = (send_sems, recv_sems, local_sems)
    movers = [
        Mover(fixed, all_fixed, sems, 0),
        Mover(meta, all_meta, sems, 1),
        Mover(base, all_base, sems, 2),
        Mover(message, all_first, sems, 3),
        Mover(row_two.at[0], meta_two, sems, 4),
        Mover(message_two, all_second, sems, 5),
        Mover(row_two.at[1], meta_three, sems, 6),
    ]
    big, small, mid = movers[:3]
    small.start_first()
    big.start_first()

    for copy in halos:
        copy.wait_recv()
    extended = jnp.concatenate(
        [hold[0], stream[...], hold[1], jnp.zeros((6, HALF), jnp.float32)], axis=0
    )
    place = (rows_of((16, HALF)) - 1) * HALF + lanes((16, HALF))
    extended = jnp.where((place < remaining) & (place + tm * SPAN >= 0), extended, 0.0)
    filtered = jnp.where(own_live, band_filter(extended, band), 0.0)
    base_own = filtered
    for block in range(BLOCKS):
        base[block] = filtered[2 * block : 2 * block + 2]
    mid.start_first()

    small.start_second()
    big.start_second()
    mid.start_second()
    small.start_small()
    big.start_third()
    mid.start_third()
    small.start_small_swap()
    small.arrive()
    over = make_lists(all_meta, near_a, near_b, live_a, live_b, lag_a, lag_b)
    copies = [
        pltpu.make_async_copy(near_a, list_a, list_sems.at[0]),
        pltpu.make_async_copy(near_b, list_b, list_sems.at[1]),
    ]
    for copy in copies:
        copy.start()
    big.forward()
    mid.forward()
    big.near()
    mid.near()
    big.far()
    mid.far()
    for copy in copies:
        copy.wait()
    comps[...] = jnp.zeros_like(comps)
    owned[...] = jnp.zeros_like(owned)
    big.arrive()
    mid.arrive()

    labels, usable = own_labels()
    rows = []
    for seg in range(6):
        tile = all_fixed[locate(labels[seg])]
        rows.append(tile[2:4])
        turn = 2.0 * tile[0:2]
        comps[9, seg : seg + 1, :] = joined(jnp.cos(turn))
        comps[10, seg : seg + 1, :] = joined(jnp.sin(turn))
    rows.append(jnp.zeros((HALF - 12, HALF), jnp.float32))
    turned = jnp.concatenate(rows, axis=0).T
    for seg in range(6):
        for half in range(2):
            at = 2 * seg + half
            columns[seg, HALF * half : HALF * half + HALF, :] = jnp.broadcast_to(
                turned[:, at : at + 1], (HALF, HALF)
            )
    wide_lane = lanes((1, WIN)).astype(jnp.float32)

    def doubled(row):
        return jnp.concatenate([row, row], axis=1)

    def nine(p, where_at, trig, live, lag):
        tile = all_fixed[where_at]
        turn = 2.0 * tile[0:2]
        co2, si2 = jnp.cos(turn), jnp.sin(turn)
        trig[p, 0:2, :] = co2
        trig[p, 2:4, :] = si2
        co, si = joined(co2), joined(si2)
        f = joined(all_base[where_at])
        weight = jnp.where(
            wide_lane < doubled(live[pl.ds(p, 1), :]), doubled(lag[pl.ds(p, 1), :]), 0.0
        )
        return tile[2:4], [f, f * co, f * si] + weight_rows(weight, co, si)

    def pair_first(p, carry):
        code = list_a[p, 0]
        seg = (code & 7) - 1
        places, values = nine(
            p, locate(lax.shift_right_logical(code, 3)), trig_a, live_a, lag_a
        )
        picked = matches(columns[jnp.clip(seg, 0, 5)], places)
        picked_a[p] = picked
        here = rows_of((8, WIN)) == seg
        for c, value in enumerate(split_product(values, picked)):
            comps[c] += jnp.where(here, value, 0.0)
        return carry

    lax.fori_loop(0, PAIRS, pair_first, 0, unroll=2)
    m_aa, m_ab, m_ac, m_bb, m_bc, m_cc, det = adjugate(*(comps[c] for c in range(3, 9)))
    co, si = comps[9], comps[10]
    seg_row = rows_of((8, WIN))
    time = tm * SPAN + (seg_row - 1) * WIN + lanes((8, WIN))
    live = (time >= 0) & (time < valid[0]) & (seg_row < 6)
    scale = jnp.where(live, 1.0, 0.0) / det
    factors[0] = (m_aa + m_ab * co + m_ac * si) * scale
    factors[1] = (m_ab + m_bb * co + m_bc * si) * scale
    factors[2] = (m_ac + m_bc * co + m_cc * si) * scale

    def change():
        return factors[0] * comps[0] + factors[1] * comps[1] + factors[2] * comps[2]

    def filter_signal(signal, out):
        rows_to_hold(signal, halo_rows)
        result = jnp.where(own_live, band_filter(halo_rows[...], band), 0.0)
        for block in range(BLOCKS):
            out[block] = result[2 * block : 2 * block + 2]
        return result

    halo_rows[...] = jnp.zeros_like(halo_rows)
    signal_first = change()
    filtered_first = filter_signal(signal_first, message)
    own = halo_rows[1:9]
    row_two[0] = (
        jnp.where(lane == 0, total(base_own * own), 0.0)
        + jnp.where(lane == 1, total(filtered_first * own), 0.0)
        + jnp.where(lane == 2, over, 0.0)
    )

    pixel = rows_of((WIN, HALF)).astype(jnp.float32)

    def owned_first(p, carry):
        code = list_b[p, 0]
        block = (code & 31) - 1
        places, values = nine(
            p, locate(lax.shift_right_logical(code, 5)), trig_b, live_b, lag_b
        )
        picked = matches(pixel, places)
        picked_b[p] = picked
        here = rows_of((BPD, WIN)) == block
        for c, value in enumerate(split_product(values, picked)):
            owned[c] += jnp.where(here, value, 0.0)
        return carry

    def three(p, where_at, trig, source):
        f = joined(source[where_at])
        return [f, f * joined(trig[p, 0:2, :]), f * joined(trig[p, 2:4, :])]

    def owned_next(source, at):
        def body(p, carry):
            code = list_b[p, 0]
            block = (code & 31) - 1
            values = three(p, locate(lax.shift_right_logical(code, 5)), trig_b, source)
            here = rows_of((BPD, WIN)) == block
            for c, value in enumerate(split_product(values, picked_b[p])):
                owned[at + c] += jnp.where(here, value, 0.0)
            return carry

        return body

    def send_round(big, small, work):
        small.start_first()
        big.start_first()
        work(0)
        small.start_second()
        big.start_second()
        work(1)
        small.start_small()
        big.start_third()
        work(2)
        small.start_small_swap()
        big.forward()
        big.near()
        big.far()
        small.arrive()
        big.arrive()

    def sums_of(metas):
        return jnp.sum(metas[...].reshape(DEVICES, 1, HALF), axis=0)

    steps = (0, 16, 28, SLOTS)
    send_round(
        movers[3], movers[4],
        lambda i: lax.fori_loop(steps[i], steps[i + 1], owned_first, 0, unroll=2),
    )
    sums = sums_of(meta_two)
    product, curve = sums[:, 0:1], sums[:, 1:2]
    over_out[...] = jnp.broadcast_to(sums[:, 2:3], (1, HALF))
    alpha = product / curve
    comps[0:3] = jnp.zeros((3, 8, WIN), jnp.float32)

    def pair_second(p, carry):
        code = list_a[p, 0]
        seg = (code & 7) - 1
        values = three(p, locate(lax.shift_right_logical(code, 3)), trig_a, all_first)
        here = rows_of((8, WIN)) == seg
        for c, value in enumerate(split_product(values, picked_a[p])):
            comps[c] += jnp.where(here, value, 0.0)
        return carry

    lax.fori_loop(0, PAIRS, pair_second, 0, unroll=4)
    filtered_second = filter_signal(signal_first - alpha * change(), message_two)
    own = halo_rows[1:9]
    row_two[1] = (
        jnp.where(lane == 0, total((base_own - alpha * filtered_first) * own), 0.0)
        + jnp.where(lane == 1, total(filtered_second * own), 0.0)
        + jnp.where(lane == 2, total(filtered_first * own), 0.0)
    )
    send_round(
        movers[5], movers[6],
        lambda i: lax.fori_loop(steps[i], steps[i + 1], owned_next(all_first, 9), 0, unroll=4),
    )
    lax.fori_loop(0, SLOTS, owned_next(all_second, 12), 0, unroll=4)

    sums = sums_of(meta_three)
    product_next = sums[:, 0:1]
    beta = product_next / product
    curve_next = sums[:, 1:2] + 2.0 * beta * sums[:, 2:3] + beta * beta * curve
    alpha_next = product_next / curve_next
    m_aa, m_ab, m_ac, m_bb, m_bc, m_cc, det = adjugate(*(owned[c] for c in range(3, 9)))

    def solve(r1, r2, r3):
        return (
            (m_aa * r1 + m_ab * r2 + m_ac * r3) / det,
            (m_ab * r1 + m_bb * r2 + m_bc * r3) / det,
            (m_ac * r1 + m_bc * r2 + m_cc * r3) / det,
        )

    right = [owned[c] for c in range(3)]
    image = [owned[9 + c] for c in range(3)]
    other = [owned[12 + c] for c in range(3)]
    residual = [r - alpha * w for r, w in zip(right, image)]
    start = solve(*right)
    middle = solve(*residual)
    final = solve(
        *(r - alpha_next * (v + beta * w) for r, v, w in zip(residual, other, image))
    )
    for comp in range(3):
        solution_out[comp] = alpha * start[comp] + alpha_next * (middle[comp] + beta * start[comp])
        residual_out[comp] = final[comp]
    for mover in movers:
        mover.finish()
    for copy in halos:
        copy.wait_send()


def f32(*shape):
    return jax.ShapeDtypeStruct(shape, jnp.float32)


def gathered_shape(rows):
    return f32(2, 8, 4, 4, rows, HALF)


def gather_rows(values, part, number):
    rows, parts = pl.pallas_call(
        gather_kernel,
        out_shape=(gathered_shape(8), gathered_shape(1)),
        in_specs=[vmem] * 2,
        out_specs=(vmem,) * 2,
        scratch_shapes=EXCHANGE_SCRATCH,
        compiler_params=pltpu.CompilerParams(collective_id=number, has_side_effects=True),
        name="gather",
    )(values, part)
    return rows.reshape(LABELS, 2, HALF), parts.reshape(DEVICES, HALF)


def any_lengths(
    time_streams, pol_angle, offsets, block_slots, hit_ids, valid_counts, filter_taps, white_weight
):
    valid = valid_counts.reshape(1)
    message, metas, base, band = pl.pallas_call(
        prepare_kernel,
        out_shape=(gathered_shape(32), gathered_shape(1), f32(8, HALF), f32(WIN, HALF)),
        in_specs=[smem] * 4 + [vmem] * 4,
        out_specs=(vmem,) * 4,
        scratch_shapes=[
            pltpu.VMEM((2, 1, HALF), jnp.float32),
            pltpu.VMEM((1, WIN), jnp.float32),
            pltpu.VMEM((32, HALF), jnp.float32),
            pltpu.VMEM((1, HALF), jnp.float32),
        ]
        + EXCHANGE_SCRATCH
        + [pltpu.SemaphoreType.DMA((2,)), pltpu.SemaphoreType.DMA((2,))],
        compiler_params=pltpu.CompilerParams(collective_id=0, has_side_effects=True),
        name="prepare",
    )(
        valid, block_slots.reshape(BLOCKS), hit_ids.reshape(-1), white_weight.reshape(1),
        filter_taps.reshape(1, BAND + 1), time_streams.reshape(8, HALF), pol_angle.reshape(8, HALF),
        offsets.reshape(8, HALF),
    )
    gathered = message.reshape(LABELS, 8, HALF)
    metas = metas.reshape(DEVICES, HALF)

    blocks = metas[:, 0:4].reshape(LABELS)
    lives = metas[:, 4:8].reshape(LABELS).astype(jnp.int32)
    lag_zero = metas[:, 8]
    order = jnp.arange(LABELS, dtype=jnp.int32)
    same = blocks[:, None] == blocks[None, :]
    ahead = (order[None, :] - order[:, None] - 1) % LABELS
    nexts = (order + 1 + jnp.min(jnp.where(same, ahead, LABELS), axis=1)) % LABELS
    counts = jnp.sum(same, axis=1, dtype=jnp.int32)
    owned = (lax.axis_index("det") * BPD + jnp.arange(BPD, dtype=jnp.int32)).astype(jnp.float32)
    mine = owned[:, None] == blocks[None, :]
    heads = jnp.concatenate(
        [
            jnp.min(jnp.where(mine, order[None, :], LABELS - 1), axis=1),
            jnp.sum(mine, axis=1, dtype=jnp.int32),
        ]
    )

    first, part_one, factors, signal = pl.pallas_call(
        first_kernel,
        out_shape=(f32(8, HALF), f32(1, HALF), f32(3, 8, WIN), f32(8, WIN)),
        in_specs=[smem] * 5 + [vmem] * 3,
        out_specs=(vmem,) * 4,
        scratch_shapes=[
            pltpu.VMEM((12, 8, WIN), jnp.float32),
            pltpu.VMEM((16, HALF), jnp.float32),
        ],
        name="first",
    )(valid, nexts, counts, lives, lag_zero, gathered, base, band)
    second, parts_two = gather_rows(first, part_one, 1)
    other, part_two = pl.pallas_call(
        second_kernel,
        out_shape=(f32(8, HALF), f32(1, HALF)),
        in_specs=[smem] * 3 + [vmem] * 8,
        out_specs=(vmem,) * 2,
        scratch_shapes=[
            pltpu.VMEM((3, 8, WIN), jnp.float32),
            pltpu.VMEM((16, HALF), jnp.float32),
        ],
        name="second",
    )(valid, nexts, counts, gathered, second, parts_two, base, first, band, factors, signal)
    third, parts_three = gather_rows(other, part_two, 2)
    answers = pl.pallas_call(
        last_kernel,
        out_shape=(f32(3, BPD, WIN), f32(3, BPD, WIN)),
        in_specs=[smem] * 4 + [vmem] * 5,
        out_specs=(vmem,) * 2,
        scratch_shapes=[pltpu.VMEM((15, BPD, WIN), jnp.float32)],
        name="last",
    )(heads, nexts, lives, lag_zero, gathered, second, third, parts_two, parts_three)
    return tuple(answers)


def wide_buffer(*shape):
    return pltpu.VMEM((2, 8, 4, 4) + shape, jnp.float32)


def room(*shape):
    return pltpu.VMEM(shape, jnp.float32)


def per_device(*args):
    (
        time_streams, pol_angle, offsets, block_slots, hit_ids, valid_counts, filter_taps,
        white_weight,
    ) = args
    fast = pl.pallas_call(
        whole_kernel,
        out_shape=(f32(3, BPD, WIN), f32(3, BPD, WIN), f32(1, HALF)),
        in_specs=[smem] * 4 + [vmem] * 4,
        out_specs=(vmem,) * 3,
        scratch_shapes=[
            room(2, 1, HALF), room(1, WIN), room(BLOCKS, 4, HALF), room(1, HALF),
            room(BLOCKS, 2, HALF), room(BLOCKS, 2, HALF), room(2, 1, HALF), room(BLOCKS, 2, HALF),
            wide_buffer(BLOCKS, 4, HALF), wide_buffer(1, HALF), wide_buffer(BLOCKS, 2, HALF),
            wide_buffer(BLOCKS, 2, HALF), wide_buffer(1, HALF), wide_buffer(BLOCKS, 2, HALF),
            wide_buffer(1, HALF),
            room(6, WIN, HALF),
            pltpu.VMEM((PAIRS, WIN, WIN), jnp.bfloat16),
            pltpu.VMEM((SLOTS, WIN, WIN), jnp.bfloat16),
            room(PAIRS, 4, HALF), room(SLOTS, 4, HALF),
            pltpu.SMEM((32, HALF), jnp.int32), pltpu.SMEM((SLOTS, HALF), jnp.int32),
            room(32, HALF), room(SLOTS, HALF), room(32, HALF), room(SLOTS, HALF),
            pltpu.VMEM((32, HALF), jnp.int32), pltpu.VMEM((SLOTS, HALF), jnp.int32),
            room(11, 8, WIN), room(15, BPD, WIN), room(3, 8, WIN), room(16, HALF),
            pltpu.SemaphoreType.DMA((7, 20)), pltpu.SemaphoreType.DMA((7, 20)),
            pltpu.SemaphoreType.DMA((7,)), pltpu.SemaphoreType.DMA((2,)),
            pltpu.SemaphoreType.DMA((2,)), pltpu.SemaphoreType.DMA((2,)),
        ],
        compiler_params=pltpu.CompilerParams(collective_id=3, has_side_effects=True),
        name="whole",
    )(
        valid_counts.reshape(1), block_slots.reshape(BLOCKS), hit_ids.reshape(-1),
        white_weight.reshape(1), filter_taps.reshape(1, BAND + 1), time_streams.reshape(8, HALF),
        pol_angle.reshape(8, HALF), offsets.reshape(8, HALF),
    )
    answers = lax.cond(
        fast[2][0, 0] > 0.0, lambda f, *a: any_lengths(*a), lambda f, *a: f, fast[:2], *args
    )
    return tuple(jnp.transpose(answer, (1, 0, 2)) for answer in answers)


def solution(mesh):
    in_specs = (
        P("det", None, "tm"),
        P("det", None, "tm"),
        P("det", None, "tm"),
        P("det", None, "tm"),
        P("det", None),
        P("det", None),
        P("det", None, None),
        P("det", None),
    )
    out_specs = (P("det", None, None), P("det", None, None))
    return jax.shard_map(
        per_device, mesh=mesh, in_specs=in_specs, out_specs=out_specs, check_vma=False
    )
```

```python
import functools

import jax
import jax.numpy as jnp
from jax import lax
from jax.experimental import pallas as pl
from jax.experimental.pallas import tpu as pltpu
from jax.sharding import PartitionSpec as P

WIN = 256
BAND = 64
BPD = 16
HALF = 128
SPAN = 1024
BLOCKS = 4
DEVICES = 256
PAIRS = 28
SLOTS = 40
LABELS = DEVICES * BLOCKS

HIGHEST = lax.Precision.HIGHEST
NT = (((1,), (1,)), ((), ()))
MESH = pl.DeviceIdType.MESH

vmem = pl.BlockSpec(memory_space=pltpu.VMEM)
smem = pl.BlockSpec(memory_space=pltpu.SMEM)


def lanes(shape):
    return lax.broadcasted_iota(jnp.int32, shape, len(shape) - 1)


def rows_of(shape):
    return lax.broadcasted_iota(jnp.int32, shape, 0)


def band_filter(extended, band):
    turned = pltpu.roll(extended, HALF // 2, 1)
    keep = lanes((8, HALF)) < HALF // 2
    first = jnp.where(keep, turned[0:8], turned[1:9])
    second = jnp.where(keep, turned[1:9], turned[2:10])
    window = jnp.concatenate([first, second], axis=1)
    return jnp.dot(window, band, precision=HIGHEST, preferred_element_type=jnp.float32)


def grid_place():
    det = lax.axis_index("det")
    x = lax.axis_index("tm")
    return lax.div(det, 8), lax.rem(lax.div(det, 2), 4), lax.rem(det, 2), x


def device_at(z, y, core, x):
    return {"det": (z * 4 + y) * 2 + core, "tm": x}


def slot_of(z, y, core, x):
    major = y + core * (x - y)
    minor = x + core * (y - x)
    return ((core * 8 + z) * 4 + major) * 4 + minor


def meet():
    z, y, core, x = grid_place()
    barrier = pltpu.get_barrier_semaphore()
    peers = (
        [device_at(lax.rem(z + d, 8), y, core, x) for d in range(1, 8)]
        + [device_at(z, lax.rem(y + d, 4), core, x) for d in range(1, 4)]
        + [device_at(z, y, core, lax.rem(x + d, 4)) for d in range(1, 4)]
        + [device_at(z, y, 1 - core, x)]
    )
    for peer in peers:
        pl.semaphore_signal(barrier, inc=1, device_id=peer, device_id_type=MESH)
    pl.semaphore_wait(barrier, len(peers))


def exchange(sources, buffers, send_sems, recv_sems, local_sems):
    z, y, core, x = grid_place()
    a = y + core * (x - y)
    b = x + core * (y - x)

    def major_peer(step):
        return device_at(
            z,
            y + (1 - core) * (lax.rem(y + step, 4) - y),
            core,
            x + core * (lax.rem(x + step, 4) - x),
        )

    def minor_peer(step):
        return device_at(
            z,
            y + core * (lax.rem(y + step, 4) - y),
            core,
            x + (1 - core) * (lax.rem(x + step, 4) - x),
        )

    arrays = range(len(sources))

    def send(number, source_of, target_of, peer):
        copies = []
        for i in arrays:
            copy = pltpu.make_async_remote_copy(
                src_ref=source_of(i),
                dst_ref=target_of(i),
                send_sem=send_sems.at[i, number],
                recv_sem=recv_sems.at[i, number],
                device_id=peer,
                device_id_type=MESH,
            )
            copy.start()
            copies.append(copy)
        return copies

    def landed(copies):
        for copy in copies:
            copy.wait_recv()

    started = []
    keep = [
        pltpu.make_async_copy(sources[i], buffers[i].at[core, z, a, b], local_sems.at[i])
        for i in arrays
    ]
    first = [
        send(
            d - 1,
            lambda i: sources[i],
            lambda i: buffers[i].at[core, z, a, b],
            device_at(lax.rem(z + d, 8), y, core, x),
        )
        for d in (4, 3, 5, 2, 6, 1, 7)
    ]
    for copy in keep:
        copy.start()
    for copy in keep:
        copy.wait()
    for copies in first:
        landed(copies)
    started += first

    def column(i):
        return buffers[i].at[core, :, a, b]

    second = [send(6 + d, column, column, major_peer(d)) for d in (2, 1, 3)]
    for copies in second:
        landed(copies)
    started += second

    def part(number, half):
        depth = pl.ds(4 * half, 4)
        return lambda i: buffers[i].at[core, depth, :, number]

    def whole(number):
        return lambda i: buffers[i].at[core, :, :, number]

    after = minor_peer(1)
    before = minor_peer(3)
    partner = device_at(z, y, 1 - core, x)
    left = lax.rem(b + 3, 4)
    right = lax.rem(b + 1, 4)
    far = lax.rem(b + 2, 4)
    up = [send(10, part(b, 0), part(b, 0), after)]
    down = [send(12, part(b, 1), part(b, 1), before)]
    up.append(send(11, part(b, 1), part(b, 1), after))
    down.append(send(13, part(b, 0), part(b, 0), before))
    swaps = [send(16, whole(b), whole(b), partner)]
    landed(up[0])
    up.append(send(14, part(left, 0), part(left, 0), after))
    landed(down[0])
    down.append(send(15, part(right, 1), part(right, 1), before))
    landed(up[1])
    swaps.append(send(17, whole(left), whole(left), partner))
    landed(down[1])
    swaps.append(send(18, whole(right), whole(right), partner))
    landed(up[2])
    landed(down[2])
    swaps.append(send(19, whole(far), whole(far), partner))
    for copies in swaps:
        landed(copies)
    started += up + down + swaps
    for copies in started:
        for copy in copies:
            copy.wait_send()


EXCHANGE_SCRATCH = [
    pltpu.SemaphoreType.DMA((2, 20)),
    pltpu.SemaphoreType.DMA((2, 20)),
    pltpu.SemaphoreType.DMA((2,)),
]


def gather_kernel(values, meta, values_out, meta_out, send_sems, recv_sems, local_sems):
    meet()
    exchange([values, meta], [values_out, meta_out], send_sems, recv_sems, local_sems)


def prepare_kernel(
    valid, slots, hits, white, taps, stream, angle, offset,
    message_out, meta_out, base_out, band,
    hold, taps_row, message, meta, send_sems, recv_sems, local_sems, halo_send, halo_recv,
):
    meet()
    z, y, core, x = grid_place()
    tm = x
    halos = [
        pltpu.make_async_remote_copy(
            src_ref=stream.at[pl.ds(7, 1)],
            dst_ref=hold.at[0],
            send_sem=halo_send.at[0],
            recv_sem=halo_recv.at[0],
            device_id=device_at(z, y, core, lax.rem(x + 1, 4)),
            device_id_type=MESH,
        ),
        pltpu.make_async_remote_copy(
            src_ref=stream.at[pl.ds(0, 1)],
            dst_ref=hold.at[1],
            send_sem=halo_send.at[1],
            recv_sem=halo_recv.at[1],
            device_id=device_at(z, y, core, lax.rem(x + 3, 4)),
            device_id_type=MESH,
        ),
    ]
    for copy in halos:
        copy.start()
    cosine = jnp.cos(2.0 * angle[...])
    sine = jnp.sin(2.0 * angle[...])
    place_of = offset[...].astype(jnp.float32)
    for block in range(BLOCKS):
        for half in range(2):
            row = 2 * block + half
            for part, values in enumerate((cosine, sine, place_of)):
                at = 8 * block + 4 * half + part + 1
                message[at : at + 1, :] = values[row : row + 1]
    taps_row[...] = jnp.zeros_like(taps_row)
    taps_row[:, : BAND + 1] = taps[...]
    spread = jnp.broadcast_to(taps_row[...], (WIN, WIN))
    shifted = pltpu.roll(spread, HALF, 1, stride=1, stride_axis=0)
    lag_row = lax.dot_general(
        spread[:8], shifted, NT, precision=HIGHEST, preferred_element_type=jnp.float32
    )
    lag_row = lag_row + jnp.where(lanes((8, WIN)) == HALF, white[0], 0.0)
    table = pltpu.roll(
        jnp.broadcast_to(lag_row[0:1], (WIN, WIN)), WIN - HALF - BAND, 1, stride=1, stride_axis=0
    )
    band[...] = table[:, :HALF]
    lag_zero = lag_row[0:1, HALF : HALF + 1]

    remaining = valid[0] - tm * SPAN
    lane = lanes((1, HALF))
    header = jnp.where(lane == 8, jnp.broadcast_to(lag_zero, (1, HALF)), 0.0)
    for block in range(BLOCKS):
        found = hits[slots[block]].astype(jnp.float32)
        count = jnp.clip(remaining - block * WIN, 0, WIN).astype(jnp.float32)
        header = jnp.where(lane == block, found, header)
        header = jnp.where(lane == 4 + block, count, header)
    meta[...] = header

    for copy in halos:
        copy.wait_recv()
    extended = jnp.concatenate(
        [hold[0], stream[...], hold[1], jnp.zeros((6, HALF), jnp.float32)], axis=0
    )
    place = (rows_of((16, HALF)) - 1) * HALF + lanes((16, HALF))
    extended = jnp.where((place < remaining) & (place + tm * SPAN >= 0), extended, 0.0)
    own_live = rows_of((8, HALF)) * HALF + lanes((8, HALF)) < remaining
    filtered = jnp.where(own_live, band_filter(extended, table[:, :HALF]), 0.0)
    for block in range(BLOCKS):
        for half in range(2):
            row = 2 * block + half
            at = 8 * block + 4 * half
            message[at : at + 1, :] = filtered[row : row + 1]
    base_out[...] = filtered
    exchange([message, meta], [message_out, meta_out], send_sems, recv_sems, local_sems)
    for copy in halos:
        copy.wait_send()


def split_rows(values):
    high = values.astype(jnp.bfloat16)
    rest = values - high.astype(jnp.float32)
    middle = rest.astype(jnp.bfloat16)
    low = (rest - middle.astype(jnp.float32)).astype(jnp.bfloat16)
    return jnp.concatenate([high, middle, low], axis=0)


def wide(tile, row):
    return jnp.concatenate([tile[row : row + 1], tile[row + 4 : row + 5]], axis=1)


def match_sum(column, places, values):
    count = values.shape[0]
    picked = jnp.where(column == places, 1.0, 0.0).astype(jnp.bfloat16)
    out = lax.dot_general(split_rows(values), picked, NT, preferred_element_type=jnp.float32)
    return out[:count] + out[count : 2 * count] + out[2 * count :]


def weight_rows(weight, cosine, sine):
    first = weight * cosine
    second = weight * sine
    return [weight, first, second, first * cosine, first * sine, second * sine]


def own_labels():
    z, y, core, x = grid_place()
    own = slot_of(z, y, core, x) * BLOCKS
    before = slot_of(z, y, core, jnp.maximum(x - 1, 0)) * BLOCKS + BLOCKS - 1
    after = slot_of(z, y, core, jnp.minimum(x + 1, 3)) * BLOCKS
    usable = [jnp.minimum(x, 1)] + [1] * BLOCKS + [jnp.minimum(3 - x, 1)]
    return [before] + [own + block for block in range(BLOCKS)] + [after], usable


def own_columns(labels, gathered):
    rows = []
    for seg in range(6):
        tile = gathered[labels[seg]]
        rows += [tile[3:4], tile[7:8]]
    rows.append(jnp.zeros((HALF - 12, HALF), jnp.float32))
    turned = jnp.concatenate(rows, axis=0).T
    return [
        jnp.concatenate([turned[:, 2 * s : 2 * s + 1], turned[:, 2 * s + 1 : 2 * s + 2]], axis=0)
        for s in range(6)
    ]


def adjugate(w1, w2, w3, w4, w5, w6):
    aa = 1.0 + w1
    bb = 1.0 + w4
    cc = 1.0 + w6
    m_aa = bb * cc - w5 * w5
    m_ab = w3 * w5 - w2 * cc
    m_ac = w2 * w5 - w3 * bb
    m_bb = aa * cc - w3 * w3
    m_bc = w2 * w3 - aa * w5
    m_cc = aa * bb - w2 * w2
    det = aa * m_aa + w2 * m_ab + w3 * m_ac
    return m_aa, m_ab, m_ac, m_bb, m_bc, m_cc, det


def rows_to_hold(signal, hold):
    hold[0:1] = signal[0:1, HALF:]
    for seg in range(1, 5):
        hold[2 * seg - 1 : 2 * seg] = signal[seg : seg + 1, :HALF]
        hold[2 * seg : 2 * seg + 1] = signal[seg : seg + 1, HALF:]
    hold[9:10] = signal[5:6, :HALF]


def total(values):
    return jnp.sum(jnp.sum(values, axis=1, keepdims=True), axis=0, keepdims=True)


def own_live_of(info):
    remaining = info[0] - lax.axis_index("tm") * SPAN
    return rows_of((8, HALF)) * HALF + lanes((8, HALF)) < remaining


def first_kernel(
    info, nexts, counts, lives, lag_zero, gathered, base, band,
    filtered_out, part_out, factors, signal_out, comps, hold,
):
    labels, flags = own_labels()
    columns = own_columns(labels, gathered)
    lane = lanes((1, WIN))
    comps[...] = jnp.zeros_like(comps)
    for seg in range(6):
        column = columns[seg]
        usable = flags[seg]

        def body(_, carry, column=column):
            label, acc = carry
            tile = gathered[label]
            f = wide(tile, 0)
            co = wide(tile, 1)
            si = wide(tile, 2)
            weight = jnp.where(lane < lives[label], lag_zero[label // BLOCKS], 0.0)
            values = jnp.concatenate(
                [f, f * co, f * si] + weight_rows(weight, co, si)
                + [jnp.zeros((7, WIN), jnp.float32)], axis=0,
            )
            return nexts[label], acc + match_sum(column, wide(tile, 3), values)

        start = labels[seg]
        _, acc = lax.fori_loop(
            0, counts[start] * usable, body, (start, jnp.zeros((16, WIN), jnp.float32))
        )
        for comp in range(9):
            comps[comp, seg : seg + 1, :] = acc[comp : comp + 1]
        tile = gathered[start]
        comps[9, seg : seg + 1, :] = wide(tile, 1)
        comps[10, seg : seg + 1, :] = wide(tile, 2)
        comps[11, seg : seg + 1, :] = jnp.where(lane < lives[start] * usable, 1.0, 0.0)
    m_aa, m_ab, m_ac, m_bb, m_bc, m_cc, det = adjugate(*(comps[c] for c in range(3, 9)))
    co, si, live = comps[9], comps[10], comps[11]
    scale = live / det
    q1 = (m_aa + m_ab * co + m_ac * si) * scale
    q2 = (m_ab + m_bb * co + m_bc * si) * scale
    q3 = (m_ac + m_bc * co + m_cc * si) * scale
    factors[0] = q1
    factors[1] = q2
    factors[2] = q3
    signal = q1 * comps[0] + q2 * comps[1] + q3 * comps[2]
    signal_out[...] = signal
    hold[...] = jnp.zeros_like(hold)
    rows_to_hold(signal, hold)
    filtered = jnp.where(own_live_of(info), band_filter(hold[...], band[...]), 0.0)
    filtered_out[...] = filtered
    own = hold[1:9]
    lane = lanes((1, HALF))
    part_out[...] = jnp.where(lane == 0, total(base[...] * own), 0.0) + jnp.where(
        lane == 1, total(filtered * own), 0.0
    )


def second_kernel(
    info, nexts, counts, gathered, second, parts, base, own_first, band, factors, signal_in,
    filtered_out, part_out, comps, hold,
):
    sums = jnp.sum(parts[...], axis=0, keepdims=True)
    alpha = sums[:, 0:1] / sums[:, 1:2]
    labels, flags = own_labels()
    columns = own_columns(labels, gathered)
    comps[...] = jnp.zeros_like(comps)
    for seg in range(6):
        column = columns[seg]

        def body(_, carry, column=column):
            label, acc = carry
            tile = gathered[label]
            pair = second[label]
            f = jnp.concatenate([pair[0:1], pair[1:2]], axis=1)
            values = jnp.concatenate(
                [f, f * wide(tile, 1), f * wide(tile, 2), jnp.zeros((13, WIN), jnp.float32)], axis=0
            )
            return nexts[label], acc + match_sum(column, wide(tile, 3), values)

        start = labels[seg]
        _, acc = lax.fori_loop(
            0, counts[start] * flags[seg], body, (start, jnp.zeros((16, WIN), jnp.float32))
        )
        for comp in range(3):
            comps[comp, seg : seg + 1, :] = acc[comp : comp + 1]
    change = factors[0] * comps[0] + factors[1] * comps[1] + factors[2] * comps[2]
    signal = signal_in[...] - alpha * change
    hold[...] = jnp.zeros_like(hold)
    rows_to_hold(signal, hold)
    filtered = jnp.where(own_live_of(info), band_filter(hold[...], band[...]), 0.0)
    filtered_out[...] = filtered
    own = hold[1:9]
    first = own_first[...]
    lane = lanes((1, HALF))
    part_out[...] = (
        jnp.where(lane == 0, total((base[...] - alpha * first) * own), 0.0)
        + jnp.where(lane == 1, total(filtered * own), 0.0)
        + jnp.where(lane == 2, total(first * own), 0.0)
    )


def last_kernel(
    heads, nexts, lives, lag_zero, gathered, second, third, parts_two, parts_three,
    solution_out, residual_out, comps,
):
    sums = jnp.sum(parts_two[...], axis=0, keepdims=True)
    product, curve = sums[:, 0:1], sums[:, 1:2]
    alpha = product / curve
    sums = jnp.sum(parts_three[...], axis=0, keepdims=True)
    product_next = sums[:, 0:1]
    beta = product_next / product
    curve_next = sums[:, 1:2] + 2.0 * beta * sums[:, 2:3] + beta * beta * curve
    alpha_next = product_next / curve_next
    column = rows_of((WIN, 1)).astype(jnp.float32)
    lane = lanes((1, WIN))
    for block in range(BPD):

        def body(_, carry):
            label, acc = carry
            tile = gathered[label]
            co = wide(tile, 1)
            si = wide(tile, 2)
            pair = second[label]
            trio = third[label]
            rows = []
            for f in (
                wide(tile, 0),
                jnp.concatenate([pair[0:1], pair[1:2]], axis=1),
                jnp.concatenate([trio[0:1], trio[1:2]], axis=1),
            ):
                rows += [f, f * co, f * si]
            weight = jnp.where(lane < lives[label], lag_zero[label // BLOCKS], 0.0)
            values = jnp.concatenate(
                rows + weight_rows(weight, co, si) + [jnp.zeros((1, WIN), jnp.float32)], axis=0
            )
            return nexts[label], acc + match_sum(column, wide(tile, 3), values)

        _, acc = lax.fori_loop(
            0, heads[BPD + block], body, (heads[block], jnp.zeros((16, WIN), jnp.float32))
        )
        for comp in range(15):
            comps[comp, block : block + 1, :] = acc[comp : comp + 1]
    m_aa, m_ab, m_ac, m_bb, m_bc, m_cc, det = adjugate(*(comps[c] for c in range(9, 15)))

    def solve(r1, r2, r3):
        return (
            (m_aa * r1 + m_ab * r2 + m_ac * r3) / det,
            (m_ab * r1 + m_bb * r2 + m_bc * r3) / det,
            (m_ac * r1 + m_bc * r2 + m_cc * r3) / det,
        )

    right = [comps[c] for c in range(3)]
    image = [comps[3 + c] for c in range(3)]
    other = [comps[6 + c] for c in range(3)]
    residual = [r - alpha * w for r, w in zip(right, image)]
    start = solve(*right)
    middle = solve(*residual)
    direction = [m + beta * s for m, s in zip(middle, start)]
    final = solve(
        *(r - alpha_next * (v + beta * w) for r, v, w in zip(residual, other, image))
    )
    for comp in range(3):
        answer = alpha * start[comp] + alpha_next * direction[comp]
        solution_out[comp] = answer
        residual_out[comp] = final[comp]


class Mover:
    def __init__(self, source, buffer, sems, number):
        self.source, self.buffer = source, buffer
        self.send_sems, self.recv_sems, self.local_sems = sems
        self.number = number
        self.z, self.y, self.core, self.x = grid_place()
        self.a = self.y + self.core * (self.x - self.y)
        self.b = self.x + self.core * (self.y - self.x)
        self.started = []

    def major_peer(self, step):
        z, y, core, x = self.z, self.y, self.core, self.x
        return device_at(
            z,
            y + (1 - core) * (lax.rem(y + step, 4) - y),
            core,
            x + core * (lax.rem(x + step, 4) - x),
        )

    def minor_peer(self, step):
        z, y, core, x = self.z, self.y, self.core, self.x
        return device_at(
            z,
            y + core * (lax.rem(y + step, 4) - y),
            core,
            x + (1 - core) * (lax.rem(x + step, 4) - x),
        )

    def send(self, number, source, target, peer):
        copy = pltpu.make_async_remote_copy(
            src_ref=source,
            dst_ref=target,
            send_sem=self.send_sems.at[self.number, number],
            recv_sem=self.recv_sems.at[self.number, number],
            device_id=peer,
            device_id_type=MESH,
        )
        copy.start()
        self.started.append(copy)
        return copy

    def start_first(self):
        z, y, core, x = self.z, self.y, self.core, self.x
        own = self.buffer.at[core, z, self.a, self.b]
        self.first = [
            self.send(d - 1, self.source, own, device_at(lax.rem(z + d, 8), y, core, x))
            for d in (4, 3, 5, 2, 6, 1, 7)
        ]
        self.keep = pltpu.make_async_copy(self.source, own, self.local_sems.at[self.number, 0])
        self.keep.start()

    def start_second(self):
        self.keep.wait()
        for copy in self.first:
            copy.wait_recv()
        column = self.buffer.at[self.core, :, self.a, self.b]
        self.second = [self.send(6 + d, column, column, self.major_peer(d)) for d in (2, 1, 3)]

    def whole(self, number):
        return self.buffer.at[self.core, :, :, number]

    def pass_on(self, number, ref, peer):
        return self.send(number, ref, ref, peer)

    def start_small(self):
        for copy in self.second:
            copy.wait_recv()
        self.third = [
            self.pass_on(9 + d, self.whole(self.b), self.minor_peer(d)) for d in (2, 1, 3)
        ]

    def start_small_swap(self):
        for copy in self.third:
            copy.wait_recv()
        partner = device_at(self.z, self.y, 1 - self.core, self.x)
        self.swaps = [self.pass_on(16, self.buffer.at[self.core], partner)]

    def arrive(self):
        for copy in self.swaps:
            copy.wait_recv()

    def finish(self):
        for copy in self.started:
            copy.wait_send()


class Relay(Mover):
    ORDER = (0, 3, 1, 2)

    def __init__(self, buffer, sems, number):
        super().__init__(None, buffer, sems, number)
        self.first, self.keep, self.sent = [], [], {}

    def start_part(self, source, target, number):
        z, y, core, x = self.z, self.y, self.core, self.x
        self.first += [
            self.send(number + d - 1, source, target, device_at(lax.rem(z + d, 8), y, core, x))
            for d in (4, 3, 5, 2, 6, 1, 7)
        ]
        copy = pltpu.make_async_copy(source, target, self.local_sems.at[self.number, number // 7])
        copy.start()
        self.keep.append(copy)

    def own(self):
        return self.buffer.at[self.core, self.z, self.a, self.b]

    def piece(self, k, m):
        return self.buffer.at[
            self.core, :, lax.rem(self.a + self.ORDER[k], 4), lax.rem(self.b + self.ORDER[m], 4)
        ]

    def pass_piece(self, number, k, m, peer):
        self.sent[number] = self.pass_on(number, self.piece(k, m), peer)

    def begin(self):
        for copy in self.keep:
            copy.wait()
        for copy in self.first:
            copy.wait_recv()
        self.after, self.before = self.minor_peer(1), self.minor_peer(3)
        self.partner = device_at(self.z, self.y, 1 - self.core, self.x)
        for d in (2, 1, 3):
            self.sent[13 + d] = self.pass_on(13 + d, self.piece(0, 0), self.major_peer(d))
        self.spread(0)

    def spread(self, k):
        if k:
            self.sent[(None, 14, 16, 15)[k]].wait_recv()
        self.pass_piece(17 + k, k, 0, self.after)
        self.pass_piece(21 + k, k, 0, self.before)
        self.pass_piece(29 + 4 * k, k, 0, self.partner)

    def hop(self, k):
        self.sent[17 + k].wait_recv()
        if k in (0, 2):
            self.pass_piece(25 + k, k, 1, self.after)
        self.pass_piece(30 + 4 * k, k, 1, self.partner)
        self.sent[21 + k].wait_recv()
        if k in (1, 3):
            self.pass_piece(25 + k, k, 2, self.before)
        self.pass_piece(31 + 4 * k, k, 2, self.partner)

    def last(self, k):
        self.sent[25 + k].wait_recv()
        self.pass_piece(32 + 4 * k, k, 3, self.partner)

    def arrive(self):
        for k in range(4):
            for m in range(4):
                self.sent[29 + 4 * k + m].wait_recv()


def locate(label):
    return (
        lax.shift_right_logical(label, 9) & 1,
        lax.shift_right_logical(label, 6) & 7,
        lax.shift_right_logical(label, 4) & 3,
        lax.shift_right_logical(label, 2) & 3,
        label & 3,
    )


def joined(tile):
    return jnp.concatenate([tile[0:1], tile[1:2]], axis=1)


def split_product(rows, picked):
    count = len(rows)
    values = jnp.concatenate(rows, axis=0)
    high = values.astype(jnp.bfloat16).astype(jnp.float32)
    rest = values - high
    middle = rest.astype(jnp.bfloat16).astype(jnp.float32)
    low = rest - middle
    pad = -3 * count % 16
    stack = [high, middle, low]
    if pad:
        stack.append(jnp.zeros((pad, WIN), jnp.float32))
    left = jnp.concatenate(stack, axis=0).astype(jnp.bfloat16)
    out = lax.dot_general(left, picked, NT, preferred_element_type=jnp.float32)
    return [
        out[c : c + 1] + out[count + c : count + c + 1] + out[2 * count + c : 2 * count + c + 1]
        for c in range(count)
    ]


def matches(column, places):
    low = jnp.where(column == places[0:1], 1.0, 0.0)
    high = jnp.where(column == places[1:2], 1.0, 0.0)
    return jnp.concatenate([low, high], axis=1).astype(jnp.bfloat16)


def make_lists(metas, list_a, list_b, live_a, live_b, lag_a, lag_b):
    z, y, core, x = grid_place()
    labels, usable = own_labels()
    table = metas[...].reshape(DEVICES, HALF).T
    blocks = jnp.concatenate(
        [table[j : j + 1, HALF * h : HALF * h + HALF] for j in range(4) for h in range(2)], axis=0
    )
    lives = jnp.concatenate(
        [table[4 + j : 5 + j, HALF * h : HALF * h + HALF] for j in range(4) for h in range(2)], axis=0
    )
    lags = jnp.concatenate(
        [table[8:9, HALF * h : HALF * h + HALF] for _ in range(4) for h in range(2)], axis=0
    )
    row = rows_of((8, HALF))
    label = (((row & 1) * HALF + lanes((8, HALF))) * 4 + lax.shift_right_logical(row, 1)).astype(
        jnp.float32
    )
    masks = []
    for seg in range(6):
        c, zz, a, b, _ = locate(labels[seg])
        number = (3, 0, 1, 2, 3, 0)[seg]
        own = metas[c, zz, a, b][:, number : number + 1]
        flag = usable[seg] if isinstance(usable[seg], int) else usable[seg].astype(jnp.float32)
        masks.append(jnp.where(blocks == own, 1.0, 0.0) * flag)
    det = lax.axis_index("det")
    base = (det * BPD).astype(jnp.float32)
    masks.append(jnp.where((blocks >= base) & (blocks < base + BPD), 1.0, 0.0))
    masks.append(jnp.zeros((8, HALF), jnp.float32))
    mask = jnp.concatenate(masks, axis=0)
    ahead = jnp.where(rows_of((HALF, HALF)) < lanes((HALF, HALF)), 1.0, 0.0)
    within = jnp.dot(mask, ahead, precision=HIGHEST, preferred_element_type=jnp.float32)
    totals = jnp.broadcast_to(jnp.sum(mask, axis=1, keepdims=True), (64, HALF))
    above = jnp.where(
        (rows_of((64, 64)) > lanes((64, 64))) & ((rows_of((64, 64)) >= 48) == (lanes((64, 64)) >= 48)),
        1.0, 0.0,
    )
    rank = within + jnp.dot(above, totals, precision=HIGHEST, preferred_element_type=jnp.float32)
    rank = jnp.where(mask > 0.0, rank, -1.0)
    count_a = jnp.sum(totals[0:48, 0:1], axis=0, keepdims=True)
    count_b = jnp.sum(totals[48:56, 0:1], axis=0, keepdims=True)
    over = jnp.where((count_a > PAIRS) | (count_b > SLOTS), 1.0, 0.0)

    def fill(rows, first, size, code_of, list_ref, live_ref, lag_ref):
        wanted = rows_of((size, HALF)).astype(jnp.float32)
        code = jnp.zeros((size, HALF), jnp.float32)
        live = jnp.zeros((size, HALF), jnp.float32)
        lag = jnp.zeros((size, HALF), jnp.float32)
        for r in range(rows):
            k = r % 8
            hit = wanted == rank[first + r : first + r + 1]
            code += jnp.where(hit, code_of(r), 0.0)
            live += jnp.where(hit, lives[k : k + 1], 0.0)
            lag += jnp.where(hit, lags[k : k + 1], 0.0)

        def spread(values):
            return jnp.broadcast_to(jnp.sum(values, axis=1, keepdims=True), (size, HALF))

        list_ref[...] = spread(code).astype(jnp.int32)
        live_ref[...] = spread(live)
        lag_ref[...] = spread(lag)

    fill(
        48, 0, 32, lambda r: label[r % 8 : r % 8 + 1] * 8.0 + (r // 8 + 1.0), list_a, live_a, lag_a
    )
    fill(
        8, 48, SLOTS, lambda r: label[r : r + 1] * 32.0 + (blocks[r : r + 1] - base + 1.0),
        list_b, live_b, lag_b,
    )
    return over


def whole_kernel(
    valid, slots, hits, white, taps, stream, angle, offset,
    solution_out, residual_out, over_out,
    hold, hold_fixed, taps_row, fixed, meta, base, message, row_two, message_two,
    all_fixed, all_meta, all_first, meta_two, all_second, meta_three,
    columns, picked_a, picked_b, trig_a, trig_b, list_a, list_b, live_a, live_b, lag_a, lag_b,
    near_a, near_b, comps, owned, factors, halo_rows, inverse,
    send_sems, recv_sems, local_sems, halo_send, halo_recv, list_sems,
):
    z, y, core, x = grid_place()
    tm = x
    barrier = pltpu.get_barrier_semaphore()
    peers = (
        [device_at(lax.rem(z + d, 8), y, core, x) for d in range(1, 8)]
        + [device_at(z, lax.rem(y + d, 4), core, x) for d in range(1, 4)]
        + [device_at(z, y, core, lax.rem(x + d, 4)) for d in range(1, 4)]
        + [device_at(z, y, 1 - core, x)]
    )
    for peer in peers:
        pl.semaphore_signal(barrier, inc=1, device_id=peer, device_id_type=MESH)

    place_of = offset[...].astype(jnp.float32)
    for block in range(BLOCKS):
        fixed[block, 0] = angle[2 * block : 2 * block + 2]
        fixed[block, 1] = place_of[2 * block : 2 * block + 2]
    taps_row[...] = jnp.zeros_like(taps_row)
    taps_row[:, : BAND + 1] = taps[...]
    lag_zero = jnp.sum(taps_row[...] * taps_row[...], axis=1, keepdims=True) + white[0, 0]
    remaining = valid[0, 0] - tm * SPAN
    lane = lanes((1, HALF))
    header = jnp.where(lane == 8, jnp.broadcast_to(lag_zero, (1, HALF)), 0.0)
    for block in range(BLOCKS):
        found = hits[0, slots[0, block]].astype(jnp.float32)
        count = jnp.clip(remaining - block * WIN, 0, WIN).astype(jnp.float32)
        header = jnp.where(lane == block, found, header)
        header = jnp.where(lane == 4 + block, count, header)
    meta[...] = header
    own_live = rows_of((8, HALF)) * HALF + lanes((8, HALF)) < remaining

    pl.semaphore_wait(barrier, len(peers))
    halos = [
        pltpu.make_async_remote_copy(
            src_ref=source,
            dst_ref=target,
            send_sem=halo_send.at[i],
            recv_sem=halo_recv.at[i],
            device_id=device_at(z, y, core, lax.rem(x + step, 4)),
            device_id_type=MESH,
        )
        for i, (source, target, step) in enumerate(
            (
                (stream.at[pl.ds(7, 1)], hold.at[0], 1),
                (stream.at[pl.ds(0, 1)], hold.at[1], 3),
                (fixed.at[BLOCKS - 1], hold_fixed.at[0], 1),
                (fixed.at[0], hold_fixed.at[1], 3),
            )
        )
    ]
    for copy in halos:
        copy.start()
    sems = (send_sems, recv_sems, local_sems)
    smalls = [
        Mover(meta, all_meta, sems, 0),
        Mover(row_two.at[0], meta_two, sems, 1),
        Mover(row_two.at[1], meta_three, sems, 2),
    ]
    relays = [
        Relay(all_fixed, sems, 3),
        Relay(all_first, sems, 4),
        Relay(all_second, sems, 5),
    ]
    big, small = relays[0], smalls[0]
    small.start_first()
    big.start_part(fixed, big.own().at[:, pl.ds(0, 2)], 0)

    spread = jnp.broadcast_to(taps_row[...], (WIN, WIN))
    shifted = pltpu.roll(spread, HALF, 1, stride=1, stride_axis=0)
    lag_row = lax.dot_general(
        spread[:8], shifted, NT, precision=HIGHEST, preferred_element_type=jnp.float32
    )
    lag_row = lag_row + jnp.where(lanes((8, WIN)) == HALF, white[0, 0], 0.0)
    band = pltpu.roll(
        jnp.broadcast_to(lag_row[0:1], (WIN, WIN)), WIN - HALF - BAND, 1, stride=1, stride_axis=0
    )[:, :HALF]
    for copy in halos[:2]:
        copy.wait_recv()
    extended = jnp.concatenate(
        [hold[0], stream[...], hold[1], jnp.zeros((6, HALF), jnp.float32)], axis=0
    )
    place = (rows_of((16, HALF)) - 1) * HALF + lanes((16, HALF))
    extended = jnp.where((place < remaining) & (place + tm * SPAN >= 0), extended, 0.0)
    base_own = jnp.where(own_live, band_filter(extended, band), 0.0)
    for block in range(BLOCKS):
        base[block, 0] = base_own[2 * block : 2 * block + 2]
    big.start_part(base, big.own().at[:, pl.ds(2, 1)], 7)

    comps[...] = jnp.zeros_like(comps)
    owned[...] = jnp.zeros_like(owned)
    halo_rows[...] = jnp.zeros_like(halo_rows)
    for copy in halos[2:]:
        copy.wait_recv()
    segments = (
        [(hold_fixed[0, 0], hold_fixed[0, 1])]
        + [(fixed[block, 0], fixed[block, 1]) for block in range(BLOCKS)]
        + [(hold_fixed[1, 0], hold_fixed[1, 1])]
    )
    for seg, (turn, _) in enumerate(segments):
        comps[9, seg : seg + 1, :] = joined(turn)
    rows = [places for _, places in segments]
    turned = jnp.concatenate(
        rows + [jnp.zeros((HALF - 12, HALF), jnp.float32)], axis=0
    ).T
    for seg in range(6):
        for half in range(2):
            at = 2 * seg + half
            columns[seg, HALF * half : HALF * half + HALF, :] = jnp.broadcast_to(
                turned[:, at : at + 1], (HALF, HALF)
            )
    turn = 2.0 * comps[9]
    comps[9] = jnp.cos(turn)
    comps[10] = jnp.sin(turn)

    small.start_second()
    big.begin()
    small.start_small()
    big.spread(1)
    big.spread(2)
    small.start_small_swap()
    big.hop(0)
    small.arrive()
    over = make_lists(all_meta, near_a, near_b, live_a, live_b, lag_a, lag_b)
    copies = [
        pltpu.make_async_copy(near_a, list_a, list_sems.at[0]),
        pltpu.make_async_copy(near_b, list_b, list_sems.at[1]),
    ]
    for copy in copies:
        copy.start()

    def wind_up(big):
        big.spread(3)
        big.hop(1)
        big.hop(2)
        big.last(0)
        big.last(1)
        big.last(2)
        big.hop(3)
        big.last(3)

    wind_up(big)
    for copy in copies:
        copy.wait()
    big.arrive()

    wide_lane = lanes((1, WIN)).astype(jnp.float32)

    def doubled(row):
        return jnp.concatenate([row, row], axis=1)

    def nine(p, where_at, trig, live, lag):
        turn = 2.0 * all_fixed[where_at + (0,)]
        co2, si2 = jnp.cos(turn), jnp.sin(turn)
        trig[p, 0:2, :] = co2
        trig[p, 2:4, :] = si2
        co, si = joined(co2), joined(si2)
        f = joined(all_fixed[where_at + (2,)])
        weight = jnp.where(
            wide_lane < doubled(live[pl.ds(p, 1), :]), doubled(lag[pl.ds(p, 1), :]), 0.0
        )
        return all_fixed[where_at + (1,)], [f, f * co, f * si] + weight_rows(weight, co, si)

    def pair_first(p, carry):
        code = list_a[p, 0]
        seg = (code & 7) - 1
        places, values = nine(
            p, locate(lax.shift_right_logical(code, 3)), trig_a, live_a, lag_a
        )
        picked = matches(columns[jnp.clip(seg, 0, 5)], places)
        picked_a[p] = picked
        here = rows_of((8, WIN)) == seg
        for c, value in enumerate(split_product(values, picked)):
            comps[c] += jnp.where(here, value, 0.0)
        return carry

    lax.fori_loop(0, PAIRS, pair_first, 0, unroll=2)
    m_aa, m_ab, m_ac, m_bb, m_bc, m_cc, det = adjugate(*(comps[c] for c in range(3, 9)))
    co, si = comps[9], comps[10]
    seg_row = rows_of((8, WIN))
    time = tm * SPAN + (seg_row - 1) * WIN + lanes((8, WIN))
    live = (time >= 0) & (time < valid[0, 0]) & (seg_row < 6)
    scale = jnp.where(live, 1.0, 0.0) / det
    factors[0] = (m_aa + m_ab * co + m_ac * si) * scale
    factors[1] = (m_ab + m_bb * co + m_bc * si) * scale
    factors[2] = (m_ac + m_bc * co + m_cc * si) * scale

    def change():
        return factors[0] * comps[0] + factors[1] * comps[1] + factors[2] * comps[2]

    def filter_signal(signal, out):
        rows_to_hold(signal, halo_rows)
        result = jnp.where(own_live, band_filter(halo_rows[...], band), 0.0)
        for block in range(BLOCKS):
            out[block] = result[2 * block : 2 * block + 2]
        return result

    signal_first = change()
    filtered_first = filter_signal(signal_first, message)
    own = halo_rows[1:9]
    row_two[0] = (
        jnp.where(lane == 0, total(base_own * own), 0.0)
        + jnp.where(lane == 1, total(filtered_first * own), 0.0)
        + jnp.where(lane == 2, over, 0.0)
    )

    pixel = rows_of((WIN, HALF)).astype(jnp.float32)

    def owned_first(p, carry):
        code = list_b[p, 0]
        block = (code & 31) - 1
        places, values = nine(
            p, locate(lax.shift_right_logical(code, 5)), trig_b, live_b, lag_b
        )
        picked = matches(pixel, places)
        picked_b[p] = picked
        here = rows_of((BPD, WIN)) == block
        for c, value in enumerate(split_product(values, picked)):
            owned[c] += jnp.where(here, value, 0.0)
        return carry

    def three(p, where_at, trig, source):
        f = joined(source[where_at])
        return [f, f * joined(trig[p, 0:2, :]), f * joined(trig[p, 2:4, :])]

    def owned_next(source, at):
        def body(p, carry):
            code = list_b[p, 0]
            block = (code & 31) - 1
            values = three(p, locate(lax.shift_right_logical(code, 5)), trig_b, source)
            here = rows_of((BPD, WIN)) == block
            for c, value in enumerate(split_product(values, picked_b[p])):
                owned[at + c] += jnp.where(here, value, 0.0)
            return carry

        return body

    def sums_of(metas):
        return jnp.sum(metas[...].reshape(DEVICES, 1, HALF), axis=0)

    def send_round(big, source, small, metas, work):
        big.start_part(source, big.own(), 0)
        small.start_first()
        work()
        big.begin()
        small.start_second()
        big.spread(1)
        big.spread(2)
        small.start_small()
        big.hop(0)
        small.start_small_swap()
        wind_up(big)
        small.arrive()
        sums = sums_of(metas)
        big.arrive()
        return sums

    def owned_weights():
        lax.fori_loop(0, SLOTS, owned_first, 0, unroll=2)

    sums = send_round(relays[1], message, smalls[1], meta_two, owned_weights)
    product, curve = sums[:, 0:1], sums[:, 1:2]
    over_out[...] = jnp.broadcast_to(sums[:, 2:3], (1, HALF))
    alpha = product / curve
    comps[0:3] = jnp.zeros((3, 8, WIN), jnp.float32)

    def pair_second(p, carry):
        code = list_a[p, 0]
        seg = (code & 7) - 1
        values = three(p, locate(lax.shift_right_logical(code, 3)), trig_a, all_first)
        here = rows_of((8, WIN)) == seg
        for c, value in enumerate(split_product(values, picked_a[p])):
            comps[c] += jnp.where(here, value, 0.0)
        return carry

    lax.fori_loop(0, PAIRS, pair_second, 0, unroll=4)
    filtered_second = filter_signal(signal_first - alpha * change(), message_two)
    own = halo_rows[1:9]
    row_two[1] = (
        jnp.where(lane == 0, total((base_own - alpha * filtered_first) * own), 0.0)
        + jnp.where(lane == 1, total(filtered_second * own), 0.0)
        + jnp.where(lane == 2, total(filtered_first * own), 0.0)
    )

    def solve(r1, r2, r3):
        i_aa, i_ab, i_ac, i_bb, i_bc, i_cc = (inverse[c] for c in range(6))
        return (
            i_aa * r1 + i_ab * r2 + i_ac * r3,
            i_ab * r1 + i_bb * r2 + i_bc * r3,
            i_ac * r1 + i_bc * r2 + i_cc * r3,
        )

    def owned_images():
        lax.fori_loop(0, SLOTS, owned_next(all_first, 9), 0, unroll=4)
        *minors, det = adjugate(*(owned[c] for c in range(3, 9)))
        scale = 1.0 / det
        for c, minor in enumerate(minors):
            inverse[c] = minor * scale
        start = solve(*(owned[c] for c in range(3)))
        for c in range(3):
            owned[c] = owned[c] - alpha * owned[9 + c]
        middle = solve(*(owned[c] for c in range(3)))
        for c in range(3):
            owned[3 + c] = start[c]
            owned[6 + c] = middle[c]

    sums = send_round(relays[2], message_two, smalls[2], meta_three, owned_images)
    product_next = sums[:, 0:1]
    beta = product_next / product
    curve_next = sums[:, 1:2] + 2.0 * beta * sums[:, 2:3] + beta * beta * curve
    alpha_next = product_next / curve_next
    for c in range(3):
        start = owned[3 + c]
        solution_out[c] = alpha * start + alpha_next * (owned[6 + c] + beta * start)
        owned[c] = owned[c] - alpha_next * beta * owned[9 + c]
    lax.fori_loop(0, SLOTS, owned_next(all_second, 12), 0, unroll=4)
    final = solve(*(owned[c] - alpha_next * owned[12 + c] for c in range(3)))
    for c in range(3):
        residual_out[c] = final[c]
    for mover in smalls + relays:
        mover.finish()
    for copy in halos:
        copy.wait_send()


def f32(*shape):
    return jax.ShapeDtypeStruct(shape, jnp.float32)


def gathered_shape(rows):
    return f32(2, 8, 4, 4, rows, HALF)


def gather_rows(values, part, number):
    rows, parts = pl.pallas_call(
        gather_kernel,
        out_shape=(gathered_shape(8), gathered_shape(1)),
        in_specs=[vmem] * 2,
        out_specs=(vmem,) * 2,
        scratch_shapes=EXCHANGE_SCRATCH,
        compiler_params=pltpu.CompilerParams(collective_id=number, has_side_effects=True),
        name="gather",
    )(values, part)
    return rows.reshape(LABELS, 2, HALF), parts.reshape(DEVICES, HALF)


def any_lengths(
    time_streams, pol_angle, offsets, block_slots, hit_ids, valid_counts, filter_taps, white_weight
):
    valid = valid_counts.reshape(1)
    message, metas, base, band = pl.pallas_call(
        prepare_kernel,
        out_shape=(gathered_shape(32), gathered_shape(1), f32(8, HALF), f32(WIN, HALF)),
        in_specs=[smem] * 4 + [vmem] * 4,
        out_specs=(vmem,) * 4,
        scratch_shapes=[
            pltpu.VMEM((2, 1, HALF), jnp.float32),
            pltpu.VMEM((1, WIN), jnp.float32),
            pltpu.VMEM((32, HALF), jnp.float32),
            pltpu.VMEM((1, HALF), jnp.float32),
        ]
        + EXCHANGE_SCRATCH
        + [pltpu.SemaphoreType.DMA((2,)), pltpu.SemaphoreType.DMA((2,))],
        compiler_params=pltpu.CompilerParams(collective_id=0, has_side_effects=True),
        name="prepare",
    )(
        valid, block_slots.reshape(BLOCKS), hit_ids.reshape(-1), white_weight.reshape(1),
        filter_taps.reshape(1, BAND + 1), time_streams.reshape(8, HALF), pol_angle.reshape(8, HALF),
        offsets.reshape(8, HALF),
    )
    gathered = message.reshape(LABELS, 8, HALF)
    metas = metas.reshape(DEVICES, HALF)

    blocks = metas[:, 0:4].reshape(LABELS)
    lives = metas[:, 4:8].reshape(LABELS).astype(jnp.int32)
    lag_zero = metas[:, 8]
    order = jnp.arange(LABELS, dtype=jnp.int32)
    same = blocks[:, None] == blocks[None, :]
    ahead = (order[None, :] - order[:, None] - 1) % LABELS
    nexts = (order + 1 + jnp.min(jnp.where(same, ahead, LABELS), axis=1)) % LABELS
    counts = jnp.sum(same, axis=1, dtype=jnp.int32)
    owned = (lax.axis_index("det") * BPD + jnp.arange(BPD, dtype=jnp.int32)).astype(jnp.float32)
    mine = owned[:, None] == blocks[None, :]
    heads = jnp.concatenate(
        [
            jnp.min(jnp.where(mine, order[None, :], LABELS - 1), axis=1),
            jnp.sum(mine, axis=1, dtype=jnp.int32),
        ]
    )

    first, part_one, factors, signal = pl.pallas_call(
        first_kernel,
        out_shape=(f32(8, HALF), f32(1, HALF), f32(3, 8, WIN), f32(8, WIN)),
        in_specs=[smem] * 5 + [vmem] * 3,
        out_specs=(vmem,) * 4,
        scratch_shapes=[
            pltpu.VMEM((12, 8, WIN), jnp.float32),
            pltpu.VMEM((16, HALF), jnp.float32),
        ],
        name="first",
    )(valid, nexts, counts, lives, lag_zero, gathered, base, band)
    second, parts_two = gather_rows(first, part_one, 1)
    other, part_two = pl.pallas_call(
        second_kernel,
        out_shape=(f32(8, HALF), f32(1, HALF)),
        in_specs=[smem] * 3 + [vmem] * 8,
        out_specs=(vmem,) * 2,
        scratch_shapes=[
            pltpu.VMEM((3, 8, WIN), jnp.float32),
            pltpu.VMEM((16, HALF), jnp.float32),
        ],
        name="second",
    )(valid, nexts, counts, gathered, second, parts_two, base, first, band, factors, signal)
    third, parts_three = gather_rows(other, part_two, 2)
    answers = pl.pallas_call(
        last_kernel,
        out_shape=(f32(3, BPD, WIN), f32(3, BPD, WIN)),
        in_specs=[smem] * 4 + [vmem] * 5,
        out_specs=(vmem,) * 2,
        scratch_shapes=[pltpu.VMEM((15, BPD, WIN), jnp.float32)],
        name="last",
    )(heads, nexts, lives, lag_zero, gathered, second, third, parts_two, parts_three)
    return tuple(answers)


def wide_buffer(*shape):
    return pltpu.VMEM((2, 8, 4, 4) + shape, jnp.float32)


def room(*shape):
    return pltpu.VMEM(shape, jnp.float32)


def per_device(*args):
    (
        time_streams, pol_angle, offsets, block_slots, hit_ids, valid_counts, filter_taps,
        white_weight,
    ) = args
    fast = pl.pallas_call(
        whole_kernel,
        out_shape=(f32(3, BPD, WIN), f32(3, BPD, WIN), f32(1, HALF)),
        in_specs=[smem] * 4 + [vmem] * 4,
        out_specs=(vmem,) * 3,
        scratch_shapes=[
            room(2, 1, HALF), room(2, 2, 2, HALF), room(1, WIN), room(BLOCKS, 2, 2, HALF),
            room(1, HALF), room(BLOCKS, 1, 2, HALF), room(BLOCKS, 2, HALF), room(2, 1, HALF),
            room(BLOCKS, 2, HALF),
            wide_buffer(BLOCKS, 3, 2, HALF), wide_buffer(1, HALF), wide_buffer(BLOCKS, 2, HALF),
            wide_buffer(1, HALF), wide_buffer(BLOCKS, 2, HALF), wide_buffer(1, HALF),
            room(6, WIN, HALF),
            pltpu.VMEM((PAIRS, WIN, WIN), jnp.bfloat16),
            pltpu.VMEM((SLOTS, WIN, WIN), jnp.bfloat16),
            room(PAIRS, 4, HALF), room(SLOTS, 4, HALF),
            pltpu.SMEM((32, HALF), jnp.int32), pltpu.SMEM((SLOTS, HALF), jnp.int32),
            room(32, HALF), room(SLOTS, HALF), room(32, HALF), room(SLOTS, HALF),
            pltpu.VMEM((32, HALF), jnp.int32), pltpu.VMEM((SLOTS, HALF), jnp.int32),
            room(11, 8, WIN), room(15, BPD, WIN), room(3, 8, WIN), room(16, HALF),
            room(6, BPD, WIN),
            pltpu.SemaphoreType.DMA((6, 45)), pltpu.SemaphoreType.DMA((6, 45)),
            pltpu.SemaphoreType.DMA((6, 2)), pltpu.SemaphoreType.DMA((4,)),
            pltpu.SemaphoreType.DMA((4,)), pltpu.SemaphoreType.DMA((2,)),
        ],
        compiler_params=pltpu.CompilerParams(collective_id=3, has_side_effects=True),
        name="whole",
    )(
        valid_counts, block_slots.reshape(1, BLOCKS), hit_ids, white_weight,
        filter_taps.reshape(1, BAND + 1), time_streams.reshape(8, HALF),
        pol_angle.reshape(8, HALF), offsets.reshape(8, HALF),
    )
    answers = lax.cond(
        fast[2][0, 0] > 0.0, lambda f, *a: any_lengths(*a), lambda f, *a: f, fast[:2], *args
    )
    return tuple(jnp.transpose(answer, (1, 0, 2)) for answer in answers)


def solution(mesh):
    in_specs = (
        P("det", None, "tm"),
        P("det", None, "tm"),
        P("det", None, "tm"),
        P("det", None, "tm"),
        P("det", None),
        P("det", None),
        P("det", None, None),
        P("det", None),
    )
    out_specs = (P("det", None, None), P("det", None, None))
    return jax.shard_map(
        per_device, mesh=mesh, in_specs=in_specs, out_specs=out_specs, check_vma=False
    )
```

```python
import functools

import jax
import jax.numpy as jnp
from jax import lax
from jax.experimental import pallas as pl
from jax.experimental.pallas import tpu as pltpu
from jax.sharding import PartitionSpec as P

WIN = 256
BAND = 64
BPD = 16
HALF = 128
SPAN = 1024
BLOCKS = 4
DEVICES = 256
PAIRS = 28
SLOTS = 20
LABELS = DEVICES * BLOCKS

HIGHEST = lax.Precision.HIGHEST
NT = (((1,), (1,)), ((), ()))
MESH = pl.DeviceIdType.MESH

vmem = pl.BlockSpec(memory_space=pltpu.VMEM)
smem = pl.BlockSpec(memory_space=pltpu.SMEM)


def lanes(shape):
    return lax.broadcasted_iota(jnp.int32, shape, len(shape) - 1)


def rows_of(shape):
    return lax.broadcasted_iota(jnp.int32, shape, 0)


def band_filter(extended, band):
    turned = pltpu.roll(extended, HALF // 2, 1)
    keep = lanes((8, HALF)) < HALF // 2
    first = jnp.where(keep, turned[0:8], turned[1:9])
    second = jnp.where(keep, turned[1:9], turned[2:10])
    window = jnp.concatenate([first, second], axis=1)
    return jnp.dot(window, band, precision=HIGHEST, preferred_element_type=jnp.float32)


def grid_place():
    det = lax.axis_index("det")
    x = lax.axis_index("tm")
    return lax.div(det, 8), lax.rem(lax.div(det, 2), 4), lax.rem(det, 2), x


def device_at(z, y, core, x):
    return {"det": (z * 4 + y) * 2 + core, "tm": x}


def slot_of(z, y, core, x):
    major = y + core * (x - y)
    minor = x + core * (y - x)
    return ((core * 8 + z) * 4 + major) * 4 + minor


def meet():
    z, y, core, x = grid_place()
    barrier = pltpu.get_barrier_semaphore()
    peers = (
        [device_at(lax.rem(z + d, 8), y, core, x) for d in range(1, 8)]
        + [device_at(z, lax.rem(y + d, 4), core, x) for d in range(1, 4)]
        + [device_at(z, y, core, lax.rem(x + d, 4)) for d in range(1, 4)]
        + [device_at(z, y, 1 - core, x)]
    )
    for peer in peers:
        pl.semaphore_signal(barrier, inc=1, device_id=peer, device_id_type=MESH)
    pl.semaphore_wait(barrier, len(peers))


def exchange(sources, buffers, send_sems, recv_sems, local_sems):
    z, y, core, x = grid_place()
    a = y + core * (x - y)
    b = x + core * (y - x)

    def major_peer(step):
        return device_at(
            z,
            y + (1 - core) * (lax.rem(y + step, 4) - y),
            core,
            x + core * (lax.rem(x + step, 4) - x),
        )

    def minor_peer(step):
        return device_at(
            z,
            y + core * (lax.rem(y + step, 4) - y),
            core,
            x + (1 - core) * (lax.rem(x + step, 4) - x),
        )

    arrays = range(len(sources))

    def send(number, source_of, target_of, peer):
        copies = []
        for i in arrays:
            copy = pltpu.make_async_remote_copy(
                src_ref=source_of(i),
                dst_ref=target_of(i),
                send_sem=send_sems.at[i, number],
                recv_sem=recv_sems.at[i, number],
                device_id=peer,
                device_id_type=MESH,
            )
            copy.start()
            copies.append(copy)
        return copies

    def landed(copies):
        for copy in copies:
            copy.wait_recv()

    started = []
    keep = [
        pltpu.make_async_copy(sources[i], buffers[i].at[core, z, a, b], local_sems.at[i])
        for i in arrays
    ]
    first = [
        send(
            d - 1,
            lambda i: sources[i],
            lambda i: buffers[i].at[core, z, a, b],
            device_at(lax.rem(z + d, 8), y, core, x),
        )
        for d in (4, 3, 5, 2, 6, 1, 7)
    ]
    for copy in keep:
        copy.start()
    for copy in keep:
        copy.wait()
    for copies in first:
        landed(copies)
    started += first

    def column(i):
        return buffers[i].at[core, :, a, b]

    second = [send(6 + d, column, column, major_peer(d)) for d in (2, 1, 3)]
    for copies in second:
        landed(copies)
    started += second

    def part(number, half):
        depth = pl.ds(4 * half, 4)
        return lambda i: buffers[i].at[core, depth, :, number]

    def whole(number):
        return lambda i: buffers[i].at[core, :, :, number]

    after = minor_peer(1)
    before = minor_peer(3)
    partner = device_at(z, y, 1 - core, x)
    left = lax.rem(b + 3, 4)
    right = lax.rem(b + 1, 4)
    far = lax.rem(b + 2, 4)
    up = [send(10, part(b, 0), part(b, 0), after)]
    down = [send(12, part(b, 1), part(b, 1), before)]
    up.append(send(11, part(b, 1), part(b, 1), after))
    down.append(send(13, part(b, 0), part(b, 0), before))
    swaps = [send(16, whole(b), whole(b), partner)]
    landed(up[0])
    up.append(send(14, part(left, 0), part(left, 0), after))
    landed(down[0])
    down.append(send(15, part(right, 1), part(right, 1), before))
    landed(up[1])
    swaps.append(send(17, whole(left), whole(left), partner))
    landed(down[1])
    swaps.append(send(18, whole(right), whole(right), partner))
    landed(up[2])
    landed(down[2])
    swaps.append(send(19, whole(far), whole(far), partner))
    for copies in swaps:
        landed(copies)
    started += up + down + swaps
    for copies in started:
        for copy in copies:
            copy.wait_send()


EXCHANGE_SCRATCH = [
    pltpu.SemaphoreType.DMA((2, 20)),
    pltpu.SemaphoreType.DMA((2, 20)),
    pltpu.SemaphoreType.DMA((2,)),
]


def gather_kernel(values, meta, values_out, meta_out, send_sems, recv_sems, local_sems):
    meet()
    exchange([values, meta], [values_out, meta_out], send_sems, recv_sems, local_sems)


def prepare_kernel(
    valid, slots, hits, white, taps, stream, angle, offset,
    message_out, meta_out, base_out, band,
    hold, taps_row, message, meta, send_sems, recv_sems, local_sems, halo_send, halo_recv,
):
    meet()
    z, y, core, x = grid_place()
    tm = x
    halos = [
        pltpu.make_async_remote_copy(
            src_ref=stream.at[pl.ds(7, 1)],
            dst_ref=hold.at[0],
            send_sem=halo_send.at[0],
            recv_sem=halo_recv.at[0],
            device_id=device_at(z, y, core, lax.rem(x + 1, 4)),
            device_id_type=MESH,
        ),
        pltpu.make_async_remote_copy(
            src_ref=stream.at[pl.ds(0, 1)],
            dst_ref=hold.at[1],
            send_sem=halo_send.at[1],
            recv_sem=halo_recv.at[1],
            device_id=device_at(z, y, core, lax.rem(x + 3, 4)),
            device_id_type=MESH,
        ),
    ]
    for copy in halos:
        copy.start()
    cosine = jnp.cos(2.0 * angle[...])
    sine = jnp.sin(2.0 * angle[...])
    place_of = offset[...].astype(jnp.float32)
    for block in range(BLOCKS):
        for half in range(2):
            row = 2 * block + half
            for part, values in enumerate((cosine, sine, place_of)):
                at = 8 * block + 4 * half + part + 1
                message[at : at + 1, :] = values[row : row + 1]
    taps_row[...] = jnp.zeros_like(taps_row)
    taps_row[:, : BAND + 1] = taps[...]
    spread = jnp.broadcast_to(taps_row[...], (WIN, WIN))
    shifted = pltpu.roll(spread, HALF, 1, stride=1, stride_axis=0)
    lag_row = lax.dot_general(
        spread[:8], shifted, NT, precision=HIGHEST, preferred_element_type=jnp.float32
    )
    lag_row = lag_row + jnp.where(lanes((8, WIN)) == HALF, white[0], 0.0)
    table = pltpu.roll(
        jnp.broadcast_to(lag_row[0:1], (WIN, WIN)), WIN - HALF - BAND, 1, stride=1, stride_axis=0
    )
    band[...] = table[:, :HALF]
    lag_zero = lag_row[0:1, HALF : HALF + 1]

    remaining = valid[0] - tm * SPAN
    lane = lanes((1, HALF))
    header = jnp.where(lane == 8, jnp.broadcast_to(lag_zero, (1, HALF)), 0.0)
    for block in range(BLOCKS):
        found = hits[slots[block]].astype(jnp.float32)
        count = jnp.clip(remaining - block * WIN, 0, WIN).astype(jnp.float32)
        header = jnp.where(lane == block, found, header)
        header = jnp.where(lane == 4 + block, count, header)
    meta[...] = header

    for copy in halos:
        copy.wait_recv()
    extended = jnp.concatenate(
        [hold[0], stream[...], hold[1], jnp.zeros((6, HALF), jnp.float32)], axis=0
    )
    place = (rows_of((16, HALF)) - 1) * HALF + lanes((16, HALF))
    extended = jnp.where((place < remaining) & (place + tm * SPAN >= 0), extended, 0.0)
    own_live = rows_of((8, HALF)) * HALF + lanes((8, HALF)) < remaining
    filtered = jnp.where(own_live, band_filter(extended, table[:, :HALF]), 0.0)
    for block in range(BLOCKS):
        for half in range(2):
            row = 2 * block + half
            at = 8 * block + 4 * half
            message[at : at + 1, :] = filtered[row : row + 1]
    base_out[...] = filtered
    exchange([message, meta], [message_out, meta_out], send_sems, recv_sems, local_sems)
    for copy in halos:
        copy.wait_send()


def split_rows(values):
    high = values.astype(jnp.bfloat16)
    rest = values - high.astype(jnp.float32)
    middle = rest.astype(jnp.bfloat16)
    low = (rest - middle.astype(jnp.float32)).astype(jnp.bfloat16)
    return jnp.concatenate([high, middle, low], axis=0)


def wide(tile, row):
    return jnp.concatenate([tile[row : row + 1], tile[row + 4 : row + 5]], axis=1)


def match_sum(column, places, values):
    count = values.shape[0]
    picked = jnp.where(column == places, 1.0, 0.0).astype(jnp.bfloat16)
    out = lax.dot_general(split_rows(values), picked, NT, preferred_element_type=jnp.float32)
    return out[:count] + out[count : 2 * count] + out[2 * count :]


def weight_rows(weight, cosine, sine):
    first = weight * cosine
    second = weight * sine
    return [weight, first, second, first * cosine, first * sine, second * sine]


def own_labels():
    z, y, core, x = grid_place()
    own = slot_of(z, y, core, x) * BLOCKS
    before = slot_of(z, y, core, jnp.maximum(x - 1, 0)) * BLOCKS + BLOCKS - 1
    after = slot_of(z, y, core, jnp.minimum(x + 1, 3)) * BLOCKS
    usable = [jnp.minimum(x, 1)] + [1] * BLOCKS + [jnp.minimum(3 - x, 1)]
    return [before] + [own + block for block in range(BLOCKS)] + [after], usable


def own_columns(labels, gathered):
    rows = []
    for seg in range(6):
        tile = gathered[labels[seg]]
        rows += [tile[3:4], tile[7:8]]
    rows.append(jnp.zeros((HALF - 12, HALF), jnp.float32))
    turned = jnp.concatenate(rows, axis=0).T
    return [
        jnp.concatenate([turned[:, 2 * s : 2 * s + 1], turned[:, 2 * s + 1 : 2 * s + 2]], axis=0)
        for s in range(6)
    ]


def adjugate(w1, w2, w3, w4, w5, w6):
    aa = 1.0 + w1
    bb = 1.0 + w4
    cc = 1.0 + w6
    m_aa = bb * cc - w5 * w5
    m_ab = w3 * w5 - w2 * cc
    m_ac = w2 * w5 - w3 * bb
    m_bb = aa * cc - w3 * w3
    m_bc = w2 * w3 - aa * w5
    m_cc = aa * bb - w2 * w2
    det = aa * m_aa + w2 * m_ab + w3 * m_ac
    return m_aa, m_ab, m_ac, m_bb, m_bc, m_cc, det


def rows_to_hold(signal, hold):
    hold[0:1] = signal[0:1, HALF:]
    for seg in range(1, 5):
        hold[2 * seg - 1 : 2 * seg] = signal[seg : seg + 1, :HALF]
        hold[2 * seg : 2 * seg + 1] = signal[seg : seg + 1, HALF:]
    hold[9:10] = signal[5:6, :HALF]


def total(values):
    return jnp.sum(jnp.sum(values, axis=1, keepdims=True), axis=0, keepdims=True)


def own_live_of(info):
    remaining = info[0] - lax.axis_index("tm") * SPAN
    return rows_of((8, HALF)) * HALF + lanes((8, HALF)) < remaining


def first_kernel(
    info, nexts, counts, lives, lag_zero, gathered, base, band,
    filtered_out, part_out, factors, signal_out, comps, hold,
):
    labels, flags = own_labels()
    columns = own_columns(labels, gathered)
    lane = lanes((1, WIN))
    comps[...] = jnp.zeros_like(comps)
    for seg in range(6):
        column = columns[seg]
        usable = flags[seg]

        def body(_, carry, column=column):
            label, acc = carry
            tile = gathered[label]
            f = wide(tile, 0)
            co = wide(tile, 1)
            si = wide(tile, 2)
            weight = jnp.where(lane < lives[label], lag_zero[label // BLOCKS], 0.0)
            values = jnp.concatenate(
                [f, f * co, f * si] + weight_rows(weight, co, si)
                + [jnp.zeros((7, WIN), jnp.float32)], axis=0,
            )
            return nexts[label], acc + match_sum(column, wide(tile, 3), values)

        start = labels[seg]
        _, acc = lax.fori_loop(
            0, counts[start] * usable, body, (start, jnp.zeros((16, WIN), jnp.float32))
        )
        for comp in range(9):
            comps[comp, seg : seg + 1, :] = acc[comp : comp + 1]
        tile = gathered[start]
        comps[9, seg : seg + 1, :] = wide(tile, 1)
        comps[10, seg : seg + 1, :] = wide(tile, 2)
        comps[11, seg : seg + 1, :] = jnp.where(lane < lives[start] * usable, 1.0, 0.0)
    m_aa, m_ab, m_ac, m_bb, m_bc, m_cc, det = adjugate(*(comps[c] for c in range(3, 9)))
    co, si, live = comps[9], comps[10], comps[11]
    scale = live / det
    q1 = (m_aa + m_ab * co + m_ac * si) * scale
    q2 = (m_ab + m_bb * co + m_bc * si) * scale
    q3 = (m_ac + m_bc * co + m_cc * si) * scale
    factors[0] = q1
    factors[1] = q2
    factors[2] = q3
    signal = q1 * comps[0] + q2 * comps[1] + q3 * comps[2]
    signal_out[...] = signal
    hold[...] = jnp.zeros_like(hold)
    rows_to_hold(signal, hold)
    filtered = jnp.where(own_live_of(info), band_filter(hold[...], band[...]), 0.0)
    filtered_out[...] = filtered
    own = hold[1:9]
    lane = lanes((1, HALF))
    part_out[...] = jnp.where(lane == 0, total(base[...] * own), 0.0) + jnp.where(
        lane == 1, total(filtered * own), 0.0
    )


def second_kernel(
    info, nexts, counts, gathered, second, parts, base, own_first, band, factors, signal_in,
    filtered_out, part_out, comps, hold,
):
    sums = jnp.sum(parts[...], axis=0, keepdims=True)
    alpha = sums[:, 0:1] / sums[:, 1:2]
    labels, flags = own_labels()
    columns = own_columns(labels, gathered)
    comps[...] = jnp.zeros_like(comps)
    for seg in range(6):
        column = columns[seg]

        def body(_, carry, column=column):
            label, acc = carry
            tile = gathered[label]
            pair = second[label]
            f = jnp.concatenate([pair[0:1], pair[1:2]], axis=1)
            values = jnp.concatenate(
                [f, f * wide(tile, 1), f * wide(tile, 2), jnp.zeros((13, WIN), jnp.float32)], axis=0
            )
            return nexts[label], acc + match_sum(column, wide(tile, 3), values)

        start = labels[seg]
        _, acc = lax.fori_loop(
            0, counts[start] * flags[seg], body, (start, jnp.zeros((16, WIN), jnp.float32))
        )
        for comp in range(3):
            comps[comp, seg : seg + 1, :] = acc[comp : comp + 1]
    change = factors[0] * comps[0] + factors[1] * comps[1] + factors[2] * comps[2]
    signal = signal_in[...] - alpha * change
    hold[...] = jnp.zeros_like(hold)
    rows_to_hold(signal, hold)
    filtered = jnp.where(own_live_of(info), band_filter(hold[...], band[...]), 0.0)
    filtered_out[...] = filtered
    own = hold[1:9]
    first = own_first[...]
    lane = lanes((1, HALF))
    part_out[...] = (
        jnp.where(lane == 0, total((base[...] - alpha * first) * own), 0.0)
        + jnp.where(lane == 1, total(filtered * own), 0.0)
        + jnp.where(lane == 2, total(first * own), 0.0)
    )


def last_kernel(
    heads, nexts, lives, lag_zero, gathered, second, third, parts_two, parts_three,
    solution_out, residual_out, comps,
):
    sums = jnp.sum(parts_two[...], axis=0, keepdims=True)
    product, curve = sums[:, 0:1], sums[:, 1:2]
    alpha = product / curve
    sums = jnp.sum(parts_three[...], axis=0, keepdims=True)
    product_next = sums[:, 0:1]
    beta = product_next / product
    curve_next = sums[:, 1:2] + 2.0 * beta * sums[:, 2:3] + beta * beta * curve
    alpha_next = product_next / curve_next
    column = rows_of((WIN, 1)).astype(jnp.float32)
    lane = lanes((1, WIN))
    for block in range(BPD):

        def body(_, carry):
            label, acc = carry
            tile = gathered[label]
            co = wide(tile, 1)
            si = wide(tile, 2)
            pair = second[label]
            trio = third[label]
            rows = []
            for f in (
                wide(tile, 0),
                jnp.concatenate([pair[0:1], pair[1:2]], axis=1),
                jnp.concatenate([trio[0:1], trio[1:2]], axis=1),
            ):
                rows += [f, f * co, f * si]
            weight = jnp.where(lane < lives[label], lag_zero[label // BLOCKS], 0.0)
            values = jnp.concatenate(
                rows + weight_rows(weight, co, si) + [jnp.zeros((1, WIN), jnp.float32)], axis=0
            )
            return nexts[label], acc + match_sum(column, wide(tile, 3), values)

        _, acc = lax.fori_loop(
            0, heads[BPD + block], body, (heads[block], jnp.zeros((16, WIN), jnp.float32))
        )
        for comp in range(15):
            comps[comp, block : block + 1, :] = acc[comp : comp + 1]
    m_aa, m_ab, m_ac, m_bb, m_bc, m_cc, det = adjugate(*(comps[c] for c in range(9, 15)))

    def solve(r1, r2, r3):
        return (
            (m_aa * r1 + m_ab * r2 + m_ac * r3) / det,
            (m_ab * r1 + m_bb * r2 + m_bc * r3) / det,
            (m_ac * r1 + m_bc * r2 + m_cc * r3) / det,
        )

    right = [comps[c] for c in range(3)]
    image = [comps[3 + c] for c in range(3)]
    other = [comps[6 + c] for c in range(3)]
    residual = [r - alpha * w for r, w in zip(right, image)]
    start = solve(*right)
    middle = solve(*residual)
    direction = [m + beta * s for m, s in zip(middle, start)]
    final = solve(
        *(r - alpha_next * (v + beta * w) for r, v, w in zip(residual, other, image))
    )
    for comp in range(3):
        answer = alpha * start[comp] + alpha_next * direction[comp]
        solution_out[comp] = answer
        residual_out[comp] = final[comp]


class Mover:
    def __init__(self, source, buffer, sems, number):
        self.source, self.buffer = source, buffer
        self.send_sems, self.recv_sems, self.local_sems = sems
        self.number = number
        self.z, self.y, self.core, self.x = grid_place()
        self.started = []

    def send(self, number, source, target, peer):
        copy = pltpu.make_async_remote_copy(
            src_ref=source,
            dst_ref=target,
            send_sem=self.send_sems.at[self.number, number],
            recv_sem=self.recv_sems.at[self.number, number],
            device_id=peer,
            device_id_type=MESH,
        )
        copy.start()
        self.started.append(copy)
        return copy

    def start_first(self):
        z, y, core, x = self.z, self.y, self.core, self.x
        own = self.buffer.at[z, y]
        self.first = [
            self.send(d - 1, self.source, own, device_at(lax.rem(z + d, 8), y, core, x))
            for d in (4, 3, 5, 2, 6, 1, 7)
        ]
        self.keep = pltpu.make_async_copy(self.source, own, self.local_sems.at[self.number])
        self.keep.start()

    def start_second(self):
        self.keep.wait()
        for copy in self.first:
            copy.wait_recv()
        column = self.buffer.at[:, self.y]
        self.second = [
            self.send(
                6 + d, column, column,
                device_at(self.z, lax.rem(self.y + d, 4), self.core, self.x),
            )
            for d in (2, 1, 3)
        ]

    def arrive(self):
        for copy in self.second:
            copy.wait_recv()

    def finish(self):
        for copy in self.started:
            copy.wait_send()


class Group:
    def __init__(self, send_sems, recv_sems):
        self.send_sems, self.recv_sems = send_sems, recv_sems
        self.z, self.y, self.core, self.x = grid_place()
        self.me = self.x * 2 + self.core
        self.started = []

    def send(self, number, k, source, target, peer):
        copy = pltpu.make_async_remote_copy(
            src_ref=source,
            dst_ref=target,
            send_sem=self.send_sems.at[number, k],
            recv_sem=self.recv_sems.at[number, k],
            device_id=peer,
            device_id_type=MESH,
        )
        copy.start()
        self.started.append(copy)
        return copy

    def to_all(self, number, source_of, target):
        copies = []
        for k in (4, 5, 2, 3, 6, 7, 1):
            x = lax.rem(self.x + k // 2, 4)
            core = lax.rem(self.core + k % 2, 2)
            copies.append(
                self.send(
                    number, k, source_of(x * 2 + core), target, device_at(self.z, self.y, core, x)
                )
            )
        return copies

    def to_partner(self, number, source, target):
        return [
            self.send(number, 0, source, target, device_at(self.z, self.y, 1 - self.core, self.x))
        ]

    def along(self, number, ref):
        return [
            self.send(
                number, d, ref, ref, device_at(self.z, self.y, self.core, lax.rem(self.x + d, 4))
            )
            for d in (2, 1, 3)
        ]

    def finish(self):
        for copy in self.started:
            copy.wait_send()


def landed(copies):
    for copy in copies:
        copy.wait_recv()


def locate(label):
    return (
        lax.shift_right_logical(label, 2) & 7,
        label & 3,
        lax.shift_right_logical(label, 5) & 3,
    )


def joined(tile):
    return jnp.concatenate([tile[0:1], tile[1:2]], axis=1)


def split_product(rows, picked):
    count = len(rows)
    values = jnp.concatenate(rows, axis=0)
    high = values.astype(jnp.bfloat16).astype(jnp.float32)
    rest = values - high
    middle = rest.astype(jnp.bfloat16).astype(jnp.float32)
    low = rest - middle
    pad = -3 * count % 16
    stack = [high, middle, low]
    if pad:
        stack.append(jnp.zeros((pad, WIN), jnp.float32))
    left = jnp.concatenate(stack, axis=0).astype(jnp.bfloat16)
    out = lax.dot_general(left, picked, NT, preferred_element_type=jnp.float32)
    return [
        out[c : c + 1] + out[count + c : count + c + 1] + out[2 * count + c : 2 * count + c + 1]
        for c in range(count)
    ]


def matches(column, places):
    low = jnp.where(column == places[0:1], 1.0, 0.0)
    high = jnp.where(column == places[1:2], 1.0, 0.0)
    return jnp.concatenate([low, high], axis=1).astype(jnp.bfloat16)


def make_lists(metas, group_meta, list_a, list_b, live_a, live_b, lag_a, lag_b):
    z, y, core, x = grid_place()
    table = jnp.concatenate(
        [metas[...].reshape(32, HALF), jnp.zeros((HALF - 32, HALF), jnp.float32)], axis=0
    ).T

    def lane_row(rows):
        out = rows[0]
        for j in range(1, 4):
            out = out + pltpu.roll(rows[j], 32 * j, 1)
        return out

    blocks = lane_row([table[j : j + 1] for j in range(4)])
    lives = lane_row([table[4 + j : 5 + j] for j in range(4)])
    lags = lane_row([table[8:9]] * 4)
    label = lanes((1, HALF)).astype(jnp.float32)
    none = jnp.full((1, 1), -5.0, jnp.float32)
    wanted = []
    for t in range(8):
        wanted.append(group_meta[t - 2][:, 3:4] if t >= 2 else none)
        wanted += [group_meta[t][:, j : j + 1] for j in range(BLOCKS)]
        wanted.append(group_meta[t + 2][:, 0:1] if t < 6 else none)
    wanted = jnp.concatenate(wanted, axis=0)
    base = ((z * 4 + y) * 2 * BPD).astype(jnp.float32)
    mask = jnp.concatenate(
        [
            jnp.where(wanted == blocks, 1.0, 0.0),
            jnp.where((blocks >= base) & (blocks < base + 2 * BPD), 1.0, 0.0),
            jnp.zeros((15, HALF), jnp.float32),
        ],
        axis=0,
    )
    ahead = jnp.where(rows_of((HALF, HALF)) < lanes((HALF, HALF)), 1.0, 0.0)
    within = jnp.dot(mask, ahead, precision=HIGHEST, preferred_element_type=jnp.float32)
    totals = jnp.broadcast_to(jnp.sum(mask, axis=1, keepdims=True), (64, HALF))
    above = jnp.where(
        (rows_of((64, 64)) > lanes((64, 64))) & ((rows_of((64, 64)) >= 48) == (lanes((64, 64)) >= 48)),
        1.0, 0.0,
    )
    rank = within + jnp.dot(above, totals, precision=HIGHEST, preferred_element_type=jnp.float32)
    rank = jnp.where(mask > 0.0, rank, -1.0)
    count_a = jnp.sum(totals[0:48, 0:1], axis=0, keepdims=True)
    count_b = totals[48:49, 0:1]
    over = jnp.where((count_a > PAIRS) | (count_b > SLOTS), 1.0, 0.0)

    def spread(values):
        return jnp.broadcast_to(jnp.sum(values, axis=1, keepdims=True), values.shape)

    def store(code, list_ref, live_ref, lag_ref):
        list_ref[...] = spread(code).astype(jnp.int32)
        live_ref[...] = spread(jnp.where(code > 0.0, lives, 0.0))
        lag_ref[...] = spread(jnp.where(code > 0.0, lags, 0.0))

    slot = rows_of((32, HALF)).astype(jnp.float32)
    code = jnp.zeros((32, HALF), jnp.float32)
    for r in range(48):
        row = 5 * (r // 6) + (4, 0, 1, 2, 3, 4)[r % 6]
        code += jnp.where(slot == rank[r : r + 1], label * 4096.0 + ((row + 1) * 64.0 + r + 1.0), 0.0)
    store(code, list_a, live_a, lag_a)
    slot = rows_of((24, HALF)).astype(jnp.float32)
    code = jnp.where(slot == rank[48:49], label * 64.0 + (blocks - base + 1.0), 0.0)
    store(code, list_b, live_b, lag_b)
    return over


def placing(codes, shift, count):
    row = (lax.shift_right_logical(codes, shift) & 63) - 1
    here = jnp.where(row == lanes(codes.shape), 1.0, 0.0)
    size = codes.shape[0]
    square = jnp.concatenate([here, jnp.zeros((HALF - size, HALF), jnp.float32)], axis=0).T
    return square[0:count, 0:size]


def whole_kernel(
    valid, slots, hits, white, taps, stream, angle, offset,
    solution_out, residual_out, over_out,
    hold, taps_row, fixed, meta, base, message, row_two, message_two,
    all_fixed, all_base, all_meta, all_first, meta_two, all_second, meta_three,
    group_fixed, group_meta, sums_out, sums_in, next_out, next_in, last_row, group_row,
    columns, picked_a, picked_b, trig_a, trig_b, list_a, list_b, live_a, live_b, lag_a, lag_b,
    near_a, near_b, result_a, result_b, comps, factors, halo_rows,
    own_part, partner_part, x_part, owned, inverse,
    send_sems, recv_sems, local_sems, group_send, group_recv, halo_send, halo_recv, list_sems,
):
    z, y, core, x = grid_place()
    tm = x
    barrier = pltpu.get_barrier_semaphore()
    peers = [device_at(lax.rem(z + d, 8), y, core, x) for d in range(1, 8)] + [
        device_at(z, lax.rem(y + d, 4), core, x) for d in range(1, 4)
    ]
    for k in range(1, 8):
        peers.append(device_at(z, y, lax.rem(core + k % 2, 2), lax.rem(x + k // 2, 4)))
    for peer in peers:
        pl.semaphore_signal(barrier, inc=1, device_id=peer, device_id_type=MESH)

    place_of = offset[...].astype(jnp.float32)
    for block in range(BLOCKS):
        fixed[block, 0] = angle[2 * block : 2 * block + 2]
        fixed[block, 1] = place_of[2 * block : 2 * block + 2]
    taps_row[...] = jnp.zeros_like(taps_row)
    taps_row[:, : BAND + 1] = taps[...]
    lag_zero = jnp.sum(taps_row[...] * taps_row[...], axis=1, keepdims=True) + white[0, 0]
    remaining = valid[0, 0] - tm * SPAN
    lane = lanes((1, HALF))
    header = jnp.where(lane == 8, jnp.broadcast_to(lag_zero, (1, HALF)), 0.0)
    for block in range(BLOCKS):
        found = hits[0, slots[0, block]].astype(jnp.float32)
        count = jnp.clip(remaining - block * WIN, 0, WIN).astype(jnp.float32)
        header = jnp.where(lane == block, found, header)
        header = jnp.where(lane == 4 + block, count, header)
    meta[...] = header
    own_live = rows_of((8, HALF)) * HALF + lanes((8, HALF)) < remaining

    pl.semaphore_wait(barrier, len(peers))
    halos = [
        pltpu.make_async_remote_copy(
            src_ref=source,
            dst_ref=target,
            send_sem=halo_send.at[i],
            recv_sem=halo_recv.at[i],
            device_id=device_at(z, y, core, lax.rem(x + step, 4)),
            device_id_type=MESH,
        )
        for i, (source, target, step) in enumerate(
            (
                (stream.at[pl.ds(7, 1)], hold.at[0], 1),
                (stream.at[pl.ds(0, 1)], hold.at[1], 3),
            )
        )
    ]
    for copy in halos:
        copy.start()
    sems = (send_sems, recv_sems, local_sems)
    smalls = [
        Mover(meta, all_meta, sems, 0),
        Mover(row_two.at[0], meta_two, sems, 1),
        Mover(row_two.at[1], meta_three, sems, 2),
    ]
    relays = [
        Mover(fixed, all_fixed, sems, 3),
        Mover(message, all_first, sems, 4),
        Mover(message_two, all_second, sems, 5),
        Mover(base, all_base, sems, 6),
    ]
    group = Group(group_send, group_recv)
    me = group.me
    big, small, mid = relays[0], smalls[0], relays[3]
    small.start_first()
    big.start_first()
    places_in = group.to_all(0, lambda t: fixed, group_fixed.at[me])
    blocks_in = group.to_all(1, lambda t: meta, group_meta.at[me])
    group_fixed[me] = fixed[...]
    group_meta[me] = meta[...]

    spread = jnp.broadcast_to(taps_row[...], (WIN, WIN))
    shifted = pltpu.roll(spread, HALF, 1, stride=1, stride_axis=0)
    lag_row = lax.dot_general(
        spread[:8], shifted, NT, precision=HIGHEST, preferred_element_type=jnp.float32
    )
    lag_row = lag_row + jnp.where(lanes((8, WIN)) == HALF, white[0, 0], 0.0)
    band = pltpu.roll(
        jnp.broadcast_to(lag_row[0:1], (WIN, WIN)), WIN - HALF - BAND, 1, stride=1, stride_axis=0
    )[:, :HALF]
    landed(halos)
    extended = jnp.concatenate(
        [hold[0], stream[...], hold[1], jnp.zeros((6, HALF), jnp.float32)], axis=0
    )
    place = (rows_of((16, HALF)) - 1) * HALF + lanes((16, HALF))
    extended = jnp.where((place < remaining) & (place + tm * SPAN >= 0), extended, 0.0)
    base_own = jnp.where(own_live, band_filter(extended, band), 0.0)
    for block in range(BLOCKS):
        base[block] = base_own[2 * block : 2 * block + 2]
    mid.start_first()

    comps[...] = jnp.zeros_like(comps)
    halo_rows[...] = jnp.zeros_like(halo_rows)
    result_a[...] = jnp.zeros_like(result_a)
    result_b[...] = jnp.zeros_like(result_b)
    landed(places_in)
    landed(blocks_in)
    for block in range(BLOCKS):
        comps[9, block : block + 1, :] = joined(fixed[block, 0])
    right = group_fixed[jnp.minimum(x + 1, 3) * 2 + core, 0, 0]
    left = group_fixed[jnp.maximum(x - 1, 0) * 2 + core, BLOCKS - 1, 0]
    comps[9, 4:5, :] = jnp.concatenate([right[0:1], left[1:2]], axis=1)
    turn = 2.0 * comps[9]
    comps[9] = jnp.cos(turn)
    comps[10] = jnp.sin(turn)
    turned = jnp.concatenate(
        [group_fixed[t, block, 1] for t in range(8) for block in range(BLOCKS)]
        + [jnp.zeros((HALF // 2, HALF), jnp.float32)],
        axis=0,
    ).T

    def column(t, block, half):
        at = 8 * t + 2 * block + half
        return jnp.broadcast_to(turned[:, at : at + 1], (HALF, HALF))

    nowhere = jnp.full((HALF, HALF), -1.0, jnp.float32)
    low_rows = rows_of((HALF, HALF)) < BAND
    for t in range(8):
        for block in range(BLOCKS):
            for half in range(2):
                columns[6 * t + 1 + block, HALF * half : HALF * half + HALF, :] = column(
                    t, block, half
                )
        columns[6 * t, 0:HALF, :] = nowhere
        columns[6 * t, HALF:WIN, :] = jnp.where(low_rows, -1.0, column(max(t - 2, 0), BLOCKS - 1, 1))
        columns[6 * t + 5, 0:HALF, :] = jnp.where(low_rows, column(min(t + 2, 7), 0, 0), -1.0)
        columns[6 * t + 5, HALF:WIN, :] = nowhere

    small.start_second()
    big.start_second()
    mid.start_second()
    small.arrive()
    over = make_lists(all_meta, group_meta, near_a, near_b, live_a, live_b, lag_a, lag_b)
    copies = [
        pltpu.make_async_copy(near_a, list_a, list_sems.at[0]),
        pltpu.make_async_copy(near_b, list_b, list_sems.at[1]),
    ]
    for copy in copies:
        copy.start()
    into_a = placing(near_a[...], 6, 40)
    into_b = placing(near_b[...], 0, 2 * BPD)
    for copy in copies:
        copy.wait()
    big.arrive()
    mid.arrive()

    wide_lane = lanes((1, WIN)).astype(jnp.float32)

    def doubled(row):
        return jnp.concatenate([row, row], axis=1)

    def nine(p, where_at, trig, live, lag):
        turn = 2.0 * all_fixed[where_at + (0,)]
        co2, si2 = jnp.cos(turn), jnp.sin(turn)
        trig[p, 0:2, :] = co2
        trig[p, 2:4, :] = si2
        co, si = joined(co2), joined(si2)
        f = joined(all_base[where_at])
        weight = jnp.where(
            wide_lane < doubled(live[pl.ds(p, 1), :]), doubled(lag[pl.ds(p, 1), :]), 0.0
        )
        return all_fixed[where_at + (1,)], [f, f * co, f * si] + weight_rows(weight, co, si)

    def three(p, where_at, trig, source):
        f = joined(source[where_at])
        return [f, f * joined(trig[p, 0:2, :]), f * joined(trig[p, 2:4, :])]

    def keep_rows(result, p, values):
        for c, value in enumerate(values):
            result[pl.ds(p, 1), WIN * c : WIN * c + WIN] = value

    def gathered_rows(into, result, count):
        return jnp.dot(
            into, result[:, 0 : WIN * count], precision=HIGHEST, preferred_element_type=jnp.float32
        )

    def pair_first(p, carry):
        code = list_a[p, 0]
        places, values = nine(
            p, locate(lax.shift_right_logical(code, 12)), trig_a, live_a, lag_a
        )
        picked = matches(columns[jnp.clip((code & 63) - 1, 0, 47)], places)
        picked_a[p] = picked
        keep_rows(result_a, p, split_product(values, picked))
        return carry

    lax.fori_loop(0, PAIRS, pair_first, 0, unroll=2)
    out = gathered_rows(into_a, result_a, 9)
    sums_out[...] = jnp.zeros_like(sums_out)
    for t in range(8):
        for c in range(9):
            sums_out[t, 5 * c : 5 * c + 5, :] = out[5 * t : 5 * t + 5, WIN * c : WIN * c + WIN]
    arriving = group.to_all(2, lambda t: sums_out.at[t], sums_in.at[me])
    sums_in[me] = sums_out[me]
    landed(arriving)
    combined = sums_in[0]
    for t in range(1, 8):
        combined = combined + sums_in[t]
    for c in range(9):
        comps[c, 0:5, :] = combined[5 * c : 5 * c + 5]
    m_aa, m_ab, m_ac, m_bb, m_bc, m_cc, det = adjugate(*(comps[c] for c in range(3, 9)))
    co, si = comps[9], comps[10]
    seg_row = rows_of((8, WIN))
    at = lanes((8, WIN))
    time = tm * SPAN + jnp.where(
        seg_row < BLOCKS, seg_row * WIN + at, jnp.where(at < HALF, SPAN + at, at - WIN)
    )
    inside = (seg_row < BLOCKS) | ((seg_row == BLOCKS) & ((at < BAND) | (at >= WIN - BAND)))
    live = (time >= 0) & (time < valid[0, 0]) & inside
    scale = jnp.where(live, 1.0, 0.0) / det
    factors[0] = (m_aa + m_ab * co + m_ac * si) * scale
    factors[1] = (m_ab + m_bb * co + m_bc * si) * scale
    factors[2] = (m_ac + m_bc * co + m_cc * si) * scale

    def change():
        return factors[0] * comps[0] + factors[1] * comps[1] + factors[2] * comps[2]

    def filter_signal(signal, out):
        halo_rows[0:1] = signal[4:5, HALF:]
        for block in range(BLOCKS):
            halo_rows[2 * block + 1 : 2 * block + 2] = signal[block : block + 1, :HALF]
            halo_rows[2 * block + 2 : 2 * block + 3] = signal[block : block + 1, HALF:]
        halo_rows[9:10] = signal[4:5, :HALF]
        result = jnp.where(own_live, band_filter(halo_rows[...], band), 0.0)
        for block in range(BLOCKS):
            out[block] = result[2 * block : 2 * block + 2]
        return result

    signal_first = change()
    filtered_first = filter_signal(signal_first, message)
    own = halo_rows[1:9]
    row_two[0] = (
        jnp.where(lane == 0, total(base_own * own), 0.0)
        + jnp.where(lane == 1, total(filtered_first * own), 0.0)
        + jnp.where(lane == 2, over, 0.0)
    )

    pixel = rows_of((WIN, HALF)).astype(jnp.float32)

    def owned_first(p, carry):
        code = list_b[p, 0]
        places, values = nine(
            p, locate(lax.shift_right_logical(code, 6)), trig_b, live_b, lag_b
        )
        picked = matches(pixel, places)
        picked_b[p] = picked
        keep_rows(result_b, p, split_product(values, picked))
        return carry

    def owned_next(source):
        def body(p, carry):
            code = list_b[p, 0]
            values = three(p, locate(lax.shift_right_logical(code, 6)), trig_b, source)
            keep_rows(result_b, p, split_product(values, picked_b[p]))
            return carry

        return body

    def owned_out(first, count, number):
        out = gathered_rows(into_b, result_b, count)
        for half in range(2):
            for c in range(count):
                own_part[half, first + c] = out[BPD * half : BPD * half + BPD, WIN * c : WIN * c + WIN]
        span = pl.ds(first, count)
        return group.to_partner(number, own_part.at[1 - core, span], partner_part.at[span])

    def owned_along(first, count, number, arriving):
        landed(arriving)
        span = pl.ds(first, count)
        x_part[x, span] = own_part[core, span] + partner_part[span]
        return group.along(number, x_part.at[x, span])

    def owned_sum(first, count):
        span = pl.ds(first, count)
        owned[span] = x_part[0, span] + x_part[1, span] + x_part[2, span] + x_part[3, span]

    def sums_of(metas):
        return jnp.sum(metas[...].reshape(32, 1, HALF), axis=0)

    big, small = relays[1], smalls[1]
    small.start_first()
    big.start_first()
    lax.fori_loop(0, SLOTS, owned_first, 0, unroll=2)
    small.start_second()
    big.start_second()
    waiting_first = owned_out(0, 9, 5)
    small.arrive()
    sums = sums_of(meta_two)
    big.arrive()

    def pair_second(p, carry):
        code = list_a[p, 0]
        values = three(p, locate(lax.shift_right_logical(code, 12)), trig_a, all_first)
        keep_rows(result_a, p, split_product(values, picked_a[p]))
        return carry

    lax.fori_loop(0, PAIRS, pair_second, 0, unroll=4)
    out = gathered_rows(into_a, result_a, 3)
    for t in range(8):
        for c in range(3):
            next_out[t, 5 * c : 5 * c + 5, :] = out[5 * t : 5 * t + 5, WIN * c : WIN * c + WIN]
        next_out[t, 15:16, :] = doubled(sums)
    arriving = group.to_all(3, lambda t: next_out.at[t], next_in.at[me])
    next_in[me] = next_out[me]
    landed(arriving)
    combined = next_in[0]
    for t in range(1, 8):
        combined = combined + next_in[t]
    for c in range(3):
        comps[c, 0:5, :] = combined[5 * c : 5 * c + 5]
    sums = combined[15:16, :HALF]
    product, curve = sums[:, 0:1], sums[:, 1:2]
    over_out[...] = jnp.broadcast_to(sums[:, 2:3], (1, HALF))
    alpha = product / curve
    filtered_second = filter_signal(signal_first - alpha * change(), message_two)
    own = halo_rows[1:9]
    row_two[1] = (
        jnp.where(lane == 0, total((base_own - alpha * filtered_first) * own), 0.0)
        + jnp.where(lane == 1, total(filtered_second * own), 0.0)
        + jnp.where(lane == 2, total(filtered_first * own), 0.0)
    )

    big, small = relays[2], smalls[2]
    small.start_first()
    big.start_first()
    first_along = owned_along(0, 9, 6, waiting_first)
    lax.fori_loop(0, SLOTS, owned_next(all_first), 0, unroll=4)
    waiting_second = owned_out(9, 3, 7)
    small.start_second()
    big.start_second()
    second_along = owned_along(9, 3, 8, waiting_second)
    small.arrive()
    last_row[...] = sums_of(meta_three)
    rows_in = group.to_all(4, lambda t: last_row, group_row.at[me])
    group_row[me] = last_row[...]
    big.arrive()
    lax.fori_loop(0, SLOTS, owned_next(all_second), 0, unroll=4)
    waiting_third = owned_out(12, 3, 9)
    third_along = owned_along(12, 3, 10, waiting_third)

    landed(rows_in)
    sums = group_row[0]
    for t in range(1, 8):
        sums = sums + group_row[t]
    product_next = sums[:, 0:1]
    beta = product_next / product
    curve_next = sums[:, 1:2] + 2.0 * beta * sums[:, 2:3] + beta * beta * curve
    alpha_next = product_next / curve_next

    def solve(r1, r2, r3):
        i_aa, i_ab, i_ac, i_bb, i_bc, i_cc = (inverse[c] for c in range(6))
        return (
            i_aa * r1 + i_ab * r2 + i_ac * r3,
            i_ab * r1 + i_bb * r2 + i_bc * r3,
            i_ac * r1 + i_bc * r2 + i_cc * r3,
        )

    landed(first_along)
    owned_sum(0, 9)
    *minors, det = adjugate(*(owned[c] for c in range(3, 9)))
    scale = 1.0 / det
    for c, minor in enumerate(minors):
        inverse[c] = minor * scale
    landed(second_along)
    owned_sum(9, 3)
    start = solve(*(owned[c] for c in range(3)))
    for c in range(3):
        owned[c] = owned[c] - alpha * owned[9 + c]
    middle = solve(*(owned[c] for c in range(3)))
    for c in range(3):
        solution_out[c] = alpha * start[c] + alpha_next * (middle[c] + beta * start[c])
        owned[c] = owned[c] - alpha_next * beta * owned[9 + c]
    landed(third_along)
    owned_sum(12, 3)
    final = solve(*(owned[c] - alpha_next * owned[12 + c] for c in range(3)))
    for c in range(3):
        residual_out[c] = final[c]
    for mover in smalls + relays + [group]:
        mover.finish()
    for copy in halos:
        copy.wait_send()


def f32(*shape):
    return jax.ShapeDtypeStruct(shape, jnp.float32)


def gathered_shape(rows):
    return f32(2, 8, 4, 4, rows, HALF)


def gather_rows(values, part, number):
    rows, parts = pl.pallas_call(
        gather_kernel,
        out_shape=(gathered_shape(8), gathered_shape(1)),
        in_specs=[vmem] * 2,
        out_specs=(vmem,) * 2,
        scratch_shapes=EXCHANGE_SCRATCH,
        compiler_params=pltpu.CompilerParams(collective_id=number, has_side_effects=True),
        name="gather",
    )(values, part)
    return rows.reshape(LABELS, 2, HALF), parts.reshape(DEVICES, HALF)


def any_lengths(
    time_streams, pol_angle, offsets, block_slots, hit_ids, valid_counts, filter_taps, white_weight
):
    valid = valid_counts.reshape(1)
    message, metas, base, band = pl.pallas_call(
        prepare_kernel,
        out_shape=(gathered_shape(32), gathered_shape(1), f32(8, HALF), f32(WIN, HALF)),
        in_specs=[smem] * 4 + [vmem] * 4,
        out_specs=(vmem,) * 4,
        scratch_shapes=[
            pltpu.VMEM((2, 1, HALF), jnp.float32),
            pltpu.VMEM((1, WIN), jnp.float32),
            pltpu.VMEM((32, HALF), jnp.float32),
            pltpu.VMEM((1, HALF), jnp.float32),
        ]
        + EXCHANGE_SCRATCH
        + [pltpu.SemaphoreType.DMA((2,)), pltpu.SemaphoreType.DMA((2,))],
        compiler_params=pltpu.CompilerParams(collective_id=0, has_side_effects=True),
        name="prepare",
    )(
        valid, block_slots.reshape(BLOCKS), hit_ids.reshape(-1), white_weight.reshape(1),
        filter_taps.reshape(1, BAND + 1), time_streams.reshape(8, HALF), pol_angle.reshape(8, HALF),
        offsets.reshape(8, HALF),
    )
    gathered = message.reshape(LABELS, 8, HALF)
    metas = metas.reshape(DEVICES, HALF)

    blocks = metas[:, 0:4].reshape(LABELS)
    lives = metas[:, 4:8].reshape(LABELS).astype(jnp.int32)
    lag_zero = metas[:, 8]
    order = jnp.arange(LABELS, dtype=jnp.int32)
    same = blocks[:, None] == blocks[None, :]
    ahead = (order[None, :] - order[:, None] - 1) % LABELS
    nexts = (order + 1 + jnp.min(jnp.where(same, ahead, LABELS), axis=1)) % LABELS
    counts = jnp.sum(same, axis=1, dtype=jnp.int32)
    owned = (lax.axis_index("det") * BPD + jnp.arange(BPD, dtype=jnp.int32)).astype(jnp.float32)
    mine = owned[:, None] == blocks[None, :]
    heads = jnp.concatenate(
        [
            jnp.min(jnp.where(mine, order[None, :], LABELS - 1), axis=1),
            jnp.sum(mine, axis=1, dtype=jnp.int32),
        ]
    )

    first, part_one, factors, signal = pl.pallas_call(
        first_kernel,
        out_shape=(f32(8, HALF), f32(1, HALF), f32(3, 8, WIN), f32(8, WIN)),
        in_specs=[smem] * 5 + [vmem] * 3,
        out_specs=(vmem,) * 4,
        scratch_shapes=[
            pltpu.VMEM((12, 8, WIN), jnp.float32),
            pltpu.VMEM((16, HALF), jnp.float32),
        ],
        name="first",
    )(valid, nexts, counts, lives, lag_zero, gathered, base, band)
    second, parts_two = gather_rows(first, part_one, 1)
    other, part_two = pl.pallas_call(
        second_kernel,
        out_shape=(f32(8, HALF), f32(1, HALF)),
        in_specs=[smem] * 3 + [vmem] * 8,
        out_specs=(vmem,) * 2,
        scratch_shapes=[
            pltpu.VMEM((3, 8, WIN), jnp.float32),
            pltpu.VMEM((16, HALF), jnp.float32),
        ],
        name="second",
    )(valid, nexts, counts, gathered, second, parts_two, base, first, band, factors, signal)
    third, parts_three = gather_rows(other, part_two, 2)
    answers = pl.pallas_call(
        last_kernel,
        out_shape=(f32(3, BPD, WIN), f32(3, BPD, WIN)),
        in_specs=[smem] * 4 + [vmem] * 5,
        out_specs=(vmem,) * 2,
        scratch_shapes=[pltpu.VMEM((15, BPD, WIN), jnp.float32)],
        name="last",
    )(heads, nexts, lives, lag_zero, gathered, second, third, parts_two, parts_three)
    return tuple(answers)


def wide_buffer(*shape):
    return pltpu.VMEM((8, 4) + shape, jnp.float32)


def room(*shape):
    return pltpu.VMEM(shape, jnp.float32)


def per_device(*args):
    (
        time_streams, pol_angle, offsets, block_slots, hit_ids, valid_counts, filter_taps,
        white_weight,
    ) = args
    fast = pl.pallas_call(
        whole_kernel,
        out_shape=(f32(3, BPD, WIN), f32(3, BPD, WIN), f32(1, HALF)),
        in_specs=[smem] * 4 + [vmem] * 4,
        out_specs=(vmem,) * 3,
        scratch_shapes=[
            room(2, 1, HALF), room(1, WIN), room(BLOCKS, 2, 2, HALF), room(1, HALF),
            room(BLOCKS, 2, HALF), room(BLOCKS, 2, HALF), room(2, 1, HALF), room(BLOCKS, 2, HALF),
            wide_buffer(BLOCKS, 2, 2, HALF), wide_buffer(BLOCKS, 2, HALF), wide_buffer(1, HALF),
            wide_buffer(BLOCKS, 2, HALF), wide_buffer(1, HALF), wide_buffer(BLOCKS, 2, HALF),
            wide_buffer(1, HALF),
            room(8, BLOCKS, 2, 2, HALF), room(8, 1, HALF), room(8, 48, WIN), room(8, 48, WIN),
            room(8, 16, WIN), room(8, 16, WIN), room(1, HALF), room(8, 1, HALF),
            room(48, WIN, HALF),
            pltpu.VMEM((PAIRS, WIN, WIN), jnp.bfloat16),
            pltpu.VMEM((SLOTS, WIN, WIN), jnp.bfloat16),
            room(PAIRS, 4, HALF), room(SLOTS, 4, HALF),
            pltpu.SMEM((32, HALF), jnp.int32), pltpu.SMEM((24, HALF), jnp.int32),
            room(32, HALF), room(24, HALF), room(32, HALF), room(24, HALF),
            pltpu.VMEM((32, HALF), jnp.int32), pltpu.VMEM((24, HALF), jnp.int32),
            room(32, 9 * WIN), room(24, 9 * WIN),
            room(11, 8, WIN), room(3, 8, WIN), room(16, HALF),
            room(2, 15, BPD, WIN), room(15, BPD, WIN), room(4, 15, BPD, WIN), room(15, BPD, WIN),
            room(6, BPD, WIN),
            pltpu.SemaphoreType.DMA((7, 10)), pltpu.SemaphoreType.DMA((7, 10)),
            pltpu.SemaphoreType.DMA((7,)), pltpu.SemaphoreType.DMA((11, 8)),
            pltpu.SemaphoreType.DMA((11, 8)), pltpu.SemaphoreType.DMA((2,)),
            pltpu.SemaphoreType.DMA((2,)), pltpu.SemaphoreType.DMA((2,)),
        ],
        compiler_params=pltpu.CompilerParams(collective_id=3, has_side_effects=True),
        name="whole",
    )(
        valid_counts, block_slots.reshape(1, BLOCKS), hit_ids, white_weight,
        filter_taps.reshape(1, BAND + 1), time_streams.reshape(8, HALF),
        pol_angle.reshape(8, HALF), offsets.reshape(8, HALF),
    )
    answers = lax.cond(
        fast[2][0, 0] > 0.0, lambda f, *a: any_lengths(*a), lambda f, *a: f, fast[:2], *args
    )
    return tuple(jnp.transpose(answer, (1, 0, 2)) for answer in answers)


def solution(mesh):
    in_specs = (
        P("det", None, "tm"),
        P("det", None, "tm"),
        P("det", None, "tm"),
        P("det", None, "tm"),
        P("det", None),
        P("det", None),
        P("det", None, None),
        P("det", None),
    )
    out_specs = (P("det", None, None), P("det", None, None))
    return jax.shard_map(
        per_device, mesh=mesh, in_specs=in_specs, out_specs=out_specs, check_vma=False
    )
```

```python
import functools

import jax
import jax.numpy as jnp
from jax import lax
from jax.experimental import pallas as pl
from jax.experimental.pallas import tpu as pltpu
from jax.sharding import PartitionSpec as P

WIN = 256
BAND = 64
BPD = 16
HALF = 128
SPAN = 1024
BLOCKS = 4
DEVICES = 256
PAIRS = 24
TARGETS = 32
SLOTS = 20
LABELS = DEVICES * BLOCKS

HIGHEST = lax.Precision.HIGHEST
NT = (((1,), (1,)), ((), ()))
MESH = pl.DeviceIdType.MESH

vmem = pl.BlockSpec(memory_space=pltpu.VMEM)
smem = pl.BlockSpec(memory_space=pltpu.SMEM)


def lanes(shape):
    return lax.broadcasted_iota(jnp.int32, shape, len(shape) - 1)


def rows_of(shape):
    return lax.broadcasted_iota(jnp.int32, shape, 0)


def band_filter(extended, band):
    turned = pltpu.roll(extended, HALF // 2, 1)
    keep = lanes((8, HALF)) < HALF // 2
    first = jnp.where(keep, turned[0:8], turned[1:9])
    second = jnp.where(keep, turned[1:9], turned[2:10])
    window = jnp.concatenate([first, second], axis=1)
    return jnp.dot(window, band, precision=HIGHEST, preferred_element_type=jnp.float32)


def grid_place():
    det = lax.axis_index("det")
    x = lax.axis_index("tm")
    return lax.div(det, 8), lax.rem(lax.div(det, 2), 4), lax.rem(det, 2), x


def device_at(z, y, core, x):
    return {"det": (z * 4 + y) * 2 + core, "tm": x}


def slot_of(z, y, core, x):
    major = y + core * (x - y)
    minor = x + core * (y - x)
    return ((core * 8 + z) * 4 + major) * 4 + minor


def meet():
    z, y, core, x = grid_place()
    barrier = pltpu.get_barrier_semaphore()
    peers = (
        [device_at(lax.rem(z + d, 8), y, core, x) for d in range(1, 8)]
        + [device_at(z, lax.rem(y + d, 4), core, x) for d in range(1, 4)]
        + [device_at(z, y, core, lax.rem(x + d, 4)) for d in range(1, 4)]
        + [device_at(z, y, 1 - core, x)]
    )
    for peer in peers:
        pl.semaphore_signal(barrier, inc=1, device_id=peer, device_id_type=MESH)
    pl.semaphore_wait(barrier, len(peers))


def exchange(sources, buffers, send_sems, recv_sems, local_sems):
    z, y, core, x = grid_place()
    a = y + core * (x - y)
    b = x + core * (y - x)

    def major_peer(step):
        return device_at(
            z,
            y + (1 - core) * (lax.rem(y + step, 4) - y),
            core,
            x + core * (lax.rem(x + step, 4) - x),
        )

    def minor_peer(step):
        return device_at(
            z,
            y + core * (lax.rem(y + step, 4) - y),
            core,
            x + (1 - core) * (lax.rem(x + step, 4) - x),
        )

    arrays = range(len(sources))

    def send(number, source_of, target_of, peer):
        copies = []
        for i in arrays:
            copy = pltpu.make_async_remote_copy(
                src_ref=source_of(i),
                dst_ref=target_of(i),
                send_sem=send_sems.at[i, number],
                recv_sem=recv_sems.at[i, number],
                device_id=peer,
                device_id_type=MESH,
            )
            copy.start()
            copies.append(copy)
        return copies

    def landed(copies):
        for copy in copies:
            copy.wait_recv()

    started = []
    keep = [
        pltpu.make_async_copy(sources[i], buffers[i].at[core, z, a, b], local_sems.at[i])
        for i in arrays
    ]
    first = [
        send(
            d - 1,
            lambda i: sources[i],
            lambda i: buffers[i].at[core, z, a, b],
            device_at(lax.rem(z + d, 8), y, core, x),
        )
        for d in (4, 3, 5, 2, 6, 1, 7)
    ]
    for copy in keep:
        copy.start()
    for copy in keep:
        copy.wait()
    for copies in first:
        landed(copies)
    started += first

    def column(i):
        return buffers[i].at[core, :, a, b]

    second = [send(6 + d, column, column, major_peer(d)) for d in (2, 1, 3)]
    for copies in second:
        landed(copies)
    started += second

    def part(number, half):
        depth = pl.ds(4 * half, 4)
        return lambda i: buffers[i].at[core, depth, :, number]

    def whole(number):
        return lambda i: buffers[i].at[core, :, :, number]

    after = minor_peer(1)
    before = minor_peer(3)
    partner = device_at(z, y, 1 - core, x)
    left = lax.rem(b + 3, 4)
    right = lax.rem(b + 1, 4)
    far = lax.rem(b + 2, 4)
    up = [send(10, part(b, 0), part(b, 0), after)]
    down = [send(12, part(b, 1), part(b, 1), before)]
    up.append(send(11, part(b, 1), part(b, 1), after))
    down.append(send(13, part(b, 0), part(b, 0), before))
    swaps = [send(16, whole(b), whole(b), partner)]
    landed(up[0])
    up.append(send(14, part(left, 0), part(left, 0), after))
    landed(down[0])
    down.append(send(15, part(right, 1), part(right, 1), before))
    landed(up[1])
    swaps.append(send(17, whole(left), whole(left), partner))
    landed(down[1])
    swaps.append(send(18, whole(right), whole(right), partner))
    landed(up[2])
    landed(down[2])
    swaps.append(send(19, whole(far), whole(far), partner))
    for copies in swaps:
        landed(copies)
    started += up + down + swaps
    for copies in started:
        for copy in copies:
            copy.wait_send()


EXCHANGE_SCRATCH = [
    pltpu.SemaphoreType.DMA((2, 20)),
    pltpu.SemaphoreType.DMA((2, 20)),
    pltpu.SemaphoreType.DMA((2,)),
]


def gather_kernel(values, meta, values_out, meta_out, send_sems, recv_sems, local_sems):
    meet()
    exchange([values, meta], [values_out, meta_out], send_sems, recv_sems, local_sems)


def prepare_kernel(
    valid, slots, hits, white, taps, stream, angle, offset,
    message_out, meta_out, base_out, band,
    hold, taps_row, message, meta, send_sems, recv_sems, local_sems, halo_send, halo_recv,
):
    meet()
    z, y, core, x = grid_place()
    tm = x
    halos = [
        pltpu.make_async_remote_copy(
            src_ref=stream.at[pl.ds(7, 1)],
            dst_ref=hold.at[0],
            send_sem=halo_send.at[0],
            recv_sem=halo_recv.at[0],
            device_id=device_at(z, y, core, lax.rem(x + 1, 4)),
            device_id_type=MESH,
        ),
        pltpu.make_async_remote_copy(
            src_ref=stream.at[pl.ds(0, 1)],
            dst_ref=hold.at[1],
            send_sem=halo_send.at[1],
            recv_sem=halo_recv.at[1],
            device_id=device_at(z, y, core, lax.rem(x + 3, 4)),
            device_id_type=MESH,
        ),
    ]
    for copy in halos:
        copy.start()
    cosine = jnp.cos(2.0 * angle[...])
    sine = jnp.sin(2.0 * angle[...])
    place_of = offset[...].astype(jnp.float32)
    for block in range(BLOCKS):
        for half in range(2):
            row = 2 * block + half
            for part, values in enumerate((cosine, sine, place_of)):
                at = 8 * block + 4 * half + part + 1
                message[at : at + 1, :] = values[row : row + 1]
    taps_row[...] = jnp.zeros_like(taps_row)
    taps_row[:, : BAND + 1] = taps[...]
    spread = jnp.broadcast_to(taps_row[...], (WIN, WIN))
    shifted = pltpu.roll(spread, HALF, 1, stride=1, stride_axis=0)
    lag_row = lax.dot_general(
        spread[:8], shifted, NT, precision=HIGHEST, preferred_element_type=jnp.float32
    )
    lag_row = lag_row + jnp.where(lanes((8, WIN)) == HALF, white[0], 0.0)
    table = pltpu.roll(
        jnp.broadcast_to(lag_row[0:1], (WIN, WIN)), WIN - HALF - BAND, 1, stride=1, stride_axis=0
    )
    band[...] = table[:, :HALF]
    lag_zero = lag_row[0:1, HALF : HALF + 1]

    remaining = valid[0] - tm * SPAN
    lane = lanes((1, HALF))
    header = jnp.where(lane == 8, jnp.broadcast_to(lag_zero, (1, HALF)), 0.0)
    for block in range(BLOCKS):
        found = hits[slots[block]].astype(jnp.float32)
        count = jnp.clip(remaining - block * WIN, 0, WIN).astype(jnp.float32)
        header = jnp.where(lane == block, found, header)
        header = jnp.where(lane == 4 + block, count, header)
    meta[...] = header

    for copy in halos:
        copy.wait_recv()
    extended = jnp.concatenate(
        [hold[0], stream[...], hold[1], jnp.zeros((6, HALF), jnp.float32)], axis=0
    )
    place = (rows_of((16, HALF)) - 1) * HALF + lanes((16, HALF))
    extended = jnp.where((place < remaining) & (place + tm * SPAN >= 0), extended, 0.0)
    own_live = rows_of((8, HALF)) * HALF + lanes((8, HALF)) < remaining
    filtered = jnp.where(own_live, band_filter(extended, table[:, :HALF]), 0.0)
    for block in range(BLOCKS):
        for half in range(2):
            row = 2 * block + half
            at = 8 * block + 4 * half
            message[at : at + 1, :] = filtered[row : row + 1]
    base_out[...] = filtered
    exchange([message, meta], [message_out, meta_out], send_sems, recv_sems, local_sems)
    for copy in halos:
        copy.wait_send()


def split_rows(values):
    high = values.astype(jnp.bfloat16)
    rest = values - high.astype(jnp.float32)
    middle = rest.astype(jnp.bfloat16)
    low = (rest - middle.astype(jnp.float32)).astype(jnp.bfloat16)
    return jnp.concatenate([high, middle, low], axis=0)


def wide(tile, row):
    return jnp.concatenate([tile[row : row + 1], tile[row + 4 : row + 5]], axis=1)


def match_sum(column, places, values):
    count = values.shape[0]
    picked = jnp.where(column == places, 1.0, 0.0).astype(jnp.bfloat16)
    out = lax.dot_general(split_rows(values), picked, NT, preferred_element_type=jnp.float32)
    return out[:count] + out[count : 2 * count] + out[2 * count :]


def weight_rows(weight, cosine, sine):
    first = weight * cosine
    second = weight * sine
    return [weight, first, second, first * cosine, first * sine, second * sine]


def own_labels():
    z, y, core, x = grid_place()
    own = slot_of(z, y, core, x) * BLOCKS
    before = slot_of(z, y, core, jnp.maximum(x - 1, 0)) * BLOCKS + BLOCKS - 1
    after = slot_of(z, y, core, jnp.minimum(x + 1, 3)) * BLOCKS
    usable = [jnp.minimum(x, 1)] + [1] * BLOCKS + [jnp.minimum(3 - x, 1)]
    return [before] + [own + block for block in range(BLOCKS)] + [after], usable


def own_columns(labels, gathered):
    rows = []
    for seg in range(6):
        tile = gathered[labels[seg]]
        rows += [tile[3:4], tile[7:8]]
    rows.append(jnp.zeros((HALF - 12, HALF), jnp.float32))
    turned = jnp.concatenate(rows, axis=0).T
    return [
        jnp.concatenate([turned[:, 2 * s : 2 * s + 1], turned[:, 2 * s + 1 : 2 * s + 2]], axis=0)
        for s in range(6)
    ]


def adjugate(w1, w2, w3, w4, w5, w6):
    aa = 1.0 + w1
    bb = 1.0 + w4
    cc = 1.0 + w6
    m_aa = bb * cc - w5 * w5
    m_ab = w3 * w5 - w2 * cc
    m_ac = w2 * w5 - w3 * bb
    m_bb = aa * cc - w3 * w3
    m_bc = w2 * w3 - aa * w5
    m_cc = aa * bb - w2 * w2
    det = aa * m_aa + w2 * m_ab + w3 * m_ac
    return m_aa, m_ab, m_ac, m_bb, m_bc, m_cc, det


def rows_to_hold(signal, hold):
    hold[0:1] = signal[0:1, HALF:]
    for seg in range(1, 5):
        hold[2 * seg - 1 : 2 * seg] = signal[seg : seg + 1, :HALF]
        hold[2 * seg : 2 * seg + 1] = signal[seg : seg + 1, HALF:]
    hold[9:10] = signal[5:6, :HALF]


def total(values):
    return jnp.sum(jnp.sum(values, axis=1, keepdims=True), axis=0, keepdims=True)


def own_live_of(info):
    remaining = info[0] - lax.axis_index("tm") * SPAN
    return rows_of((8, HALF)) * HALF + lanes((8, HALF)) < remaining


def first_kernel(
    info, nexts, counts, lives, lag_zero, gathered, base, band,
    filtered_out, part_out, factors, signal_out, comps, hold,
):
    labels, flags = own_labels()
    columns = own_columns(labels, gathered)
    lane = lanes((1, WIN))
    comps[...] = jnp.zeros_like(comps)
    for seg in range(6):
        column = columns[seg]
        usable = flags[seg]

        def body(_, carry, column=column):
            label, acc = carry
            tile = gathered[label]
            f = wide(tile, 0)
            co = wide(tile, 1)
            si = wide(tile, 2)
            weight = jnp.where(lane < lives[label], lag_zero[label // BLOCKS], 0.0)
            values = jnp.concatenate(
                [f, f * co, f * si] + weight_rows(weight, co, si)
                + [jnp.zeros((7, WIN), jnp.float32)], axis=0,
            )
            return nexts[label], acc + match_sum(column, wide(tile, 3), values)

        start = labels[seg]
        _, acc = lax.fori_loop(
            0, counts[start] * usable, body, (start, jnp.zeros((16, WIN), jnp.float32))
        )
        for comp in range(9):
            comps[comp, seg : seg + 1, :] = acc[comp : comp + 1]
        tile = gathered[start]
        comps[9, seg : seg + 1, :] = wide(tile, 1)
        comps[10, seg : seg + 1, :] = wide(tile, 2)
        comps[11, seg : seg + 1, :] = jnp.where(lane < lives[start] * usable, 1.0, 0.0)
    m_aa, m_ab, m_ac, m_bb, m_bc, m_cc, det = adjugate(*(comps[c] for c in range(3, 9)))
    co, si, live = comps[9], comps[10], comps[11]
    scale = live / det
    q1 = (m_aa + m_ab * co + m_ac * si) * scale
    q2 = (m_ab + m_bb * co + m_bc * si) * scale
    q3 = (m_ac + m_bc * co + m_cc * si) * scale
    factors[0] = q1
    factors[1] = q2
    factors[2] = q3
    signal = q1 * comps[0] + q2 * comps[1] + q3 * comps[2]
    signal_out[...] = signal
    hold[...] = jnp.zeros_like(hold)
    rows_to_hold(signal, hold)
    filtered = jnp.where(own_live_of(info), band_filter(hold[...], band[...]), 0.0)
    filtered_out[...] = filtered
    own = hold[1:9]
    lane = lanes((1, HALF))
    part_out[...] = jnp.where(lane == 0, total(base[...] * own), 0.0) + jnp.where(
        lane == 1, total(filtered * own), 0.0
    )


def second_kernel(
    info, nexts, counts, gathered, second, parts, base, own_first, band, factors, signal_in,
    filtered_out, part_out, comps, hold,
):
    sums = jnp.sum(parts[...], axis=0, keepdims=True)
    alpha = sums[:, 0:1] / sums[:, 1:2]
    labels, flags = own_labels()
    columns = own_columns(labels, gathered)
    comps[...] = jnp.zeros_like(comps)
    for seg in range(6):
        column = columns[seg]

        def body(_, carry, column=column):
            label, acc = carry
            tile = gathered[label]
            pair = second[label]
            f = jnp.concatenate([pair[0:1], pair[1:2]], axis=1)
            values = jnp.concatenate(
                [f, f * wide(tile, 1), f * wide(tile, 2), jnp.zeros((13, WIN), jnp.float32)], axis=0
            )
            return nexts[label], acc + match_sum(column, wide(tile, 3), values)

        start = labels[seg]
        _, acc = lax.fori_loop(
            0, counts[start] * flags[seg], body, (start, jnp.zeros((16, WIN), jnp.float32))
        )
        for comp in range(3):
            comps[comp, seg : seg + 1, :] = acc[comp : comp + 1]
    change = factors[0] * comps[0] + factors[1] * comps[1] + factors[2] * comps[2]
    signal = signal_in[...] - alpha * change
    hold[...] = jnp.zeros_like(hold)
    rows_to_hold(signal, hold)
    filtered = jnp.where(own_live_of(info), band_filter(hold[...], band[...]), 0.0)
    filtered_out[...] = filtered
    own = hold[1:9]
    first = own_first[...]
    lane = lanes((1, HALF))
    part_out[...] = (
        jnp.where(lane == 0, total((base[...] - alpha * first) * own), 0.0)
        + jnp.where(lane == 1, total(filtered * own), 0.0)
        + jnp.where(lane == 2, total(first * own), 0.0)
    )


def last_kernel(
    heads, nexts, lives, lag_zero, gathered, second, third, parts_two, parts_three,
    solution_out, residual_out, comps,
):
    sums = jnp.sum(parts_two[...], axis=0, keepdims=True)
    product, curve = sums[:, 0:1], sums[:, 1:2]
    alpha = product / curve
    sums = jnp.sum(parts_three[...], axis=0, keepdims=True)
    product_next = sums[:, 0:1]
    beta = product_next / product
    curve_next = sums[:, 1:2] + 2.0 * beta * sums[:, 2:3] + beta * beta * curve
    alpha_next = product_next / curve_next
    column = rows_of((WIN, 1)).astype(jnp.float32)
    lane = lanes((1, WIN))
    for block in range(BPD):

        def body(_, carry):
            label, acc = carry
            tile = gathered[label]
            co = wide(tile, 1)
            si = wide(tile, 2)
            pair = second[label]
            trio = third[label]
            rows = []
            for f in (
                wide(tile, 0),
                jnp.concatenate([pair[0:1], pair[1:2]], axis=1),
                jnp.concatenate([trio[0:1], trio[1:2]], axis=1),
            ):
                rows += [f, f * co, f * si]
            weight = jnp.where(lane < lives[label], lag_zero[label // BLOCKS], 0.0)
            values = jnp.concatenate(
                rows + weight_rows(weight, co, si) + [jnp.zeros((1, WIN), jnp.float32)], axis=0
            )
            return nexts[label], acc + match_sum(column, wide(tile, 3), values)

        _, acc = lax.fori_loop(
            0, heads[BPD + block], body, (heads[block], jnp.zeros((16, WIN), jnp.float32))
        )
        for comp in range(15):
            comps[comp, block : block + 1, :] = acc[comp : comp + 1]
    m_aa, m_ab, m_ac, m_bb, m_bc, m_cc, det = adjugate(*(comps[c] for c in range(9, 15)))

    def solve(r1, r2, r3):
        return (
            (m_aa * r1 + m_ab * r2 + m_ac * r3) / det,
            (m_ab * r1 + m_bb * r2 + m_bc * r3) / det,
            (m_ac * r1 + m_bc * r2 + m_cc * r3) / det,
        )

    right = [comps[c] for c in range(3)]
    image = [comps[3 + c] for c in range(3)]
    other = [comps[6 + c] for c in range(3)]
    residual = [r - alpha * w for r, w in zip(right, image)]
    start = solve(*right)
    middle = solve(*residual)
    direction = [m + beta * s for m, s in zip(middle, start)]
    final = solve(
        *(r - alpha_next * (v + beta * w) for r, v, w in zip(residual, other, image))
    )
    for comp in range(3):
        answer = alpha * start[comp] + alpha_next * direction[comp]
        solution_out[comp] = answer
        residual_out[comp] = final[comp]


class Mover:
    def __init__(self, source, buffer, sems, number):
        self.source, self.buffer = source, buffer
        self.send_sems, self.recv_sems, self.local_sems = sems
        self.number = number
        self.z, self.y, self.core, self.x = grid_place()
        self.started = []

    def send(self, number, source, target, peer):
        copy = pltpu.make_async_remote_copy(
            src_ref=source,
            dst_ref=target,
            send_sem=self.send_sems.at[self.number, number],
            recv_sem=self.recv_sems.at[self.number, number],
            device_id=peer,
            device_id_type=MESH,
        )
        copy.start()
        self.started.append(copy)
        return copy

    def start_first(self):
        z, y, core, x = self.z, self.y, self.core, self.x
        own = self.buffer.at[z, y]
        self.first = [
            self.send(d - 1, self.source, own, device_at(lax.rem(z + d, 8), y, core, x))
            for d in (4, 3, 5, 2, 6, 1, 7)
        ]
        self.keep = pltpu.make_async_copy(self.source, own, self.local_sems.at[self.number])
        self.keep.start()

    def start_second(self):
        self.keep.wait()
        for copy in self.first:
            copy.wait_recv()
        column = self.buffer.at[:, self.y]
        self.second = [
            self.send(
                6 + d, column, column,
                device_at(self.z, lax.rem(self.y + d, 4), self.core, self.x),
            )
            for d in (2, 1, 3)
        ]

    def arrive(self):
        for copy in self.second:
            copy.wait_recv()

    def finish(self):
        for copy in self.started:
            copy.wait_send()


class Group:
    def __init__(self, send_sems, recv_sems):
        self.send_sems, self.recv_sems = send_sems, recv_sems
        self.z, self.y, self.core, self.x = grid_place()
        self.me = self.x * 2 + self.core
        self.started = []

    def send(self, number, k, source, target, peer):
        copy = pltpu.make_async_remote_copy(
            src_ref=source,
            dst_ref=target,
            send_sem=self.send_sems.at[number, k],
            recv_sem=self.recv_sems.at[number, k],
            device_id=peer,
            device_id_type=MESH,
        )
        copy.start()
        self.started.append(copy)
        return copy

    def to_all(self, number, source_of, target):
        copies = []
        for k in (4, 5, 2, 3, 6, 7, 1):
            x = lax.rem(self.x + k // 2, 4)
            core = lax.rem(self.core + k % 2, 2)
            copies.append(
                self.send(
                    number, k, source_of(x * 2 + core), target, device_at(self.z, self.y, core, x)
                )
            )
        return copies

    def to_partner(self, number, source, target):
        return [
            self.send(number, 0, source, target, device_at(self.z, self.y, 1 - self.core, self.x))
        ]

    def along(self, number, ref):
        return [
            self.send(
                number, d, ref, ref, device_at(self.z, self.y, self.core, lax.rem(self.x + d, 4))
            )
            for d in (2, 1, 3)
        ]

    def finish(self):
        for copy in self.started:
            copy.wait_send()


def landed(copies):
    for copy in copies:
        copy.wait_recv()


def locate(label):
    return (
        lax.shift_right_logical(label, 2) & 7,
        label & 3,
        lax.shift_right_logical(label, 5) & 3,
    )


def joined(tile):
    return jnp.concatenate([tile[0:1], tile[1:2]], axis=1)


def split_product(rows, picked):
    count = len(rows)
    values = jnp.concatenate(rows, axis=0)
    high = values.astype(jnp.bfloat16).astype(jnp.float32)
    rest = values - high
    middle = rest.astype(jnp.bfloat16).astype(jnp.float32)
    low = rest - middle
    pad = -3 * count % 16
    stack = [high, middle, low]
    if pad:
        stack.append(jnp.zeros((pad, WIN), jnp.float32))
    left = jnp.concatenate(stack, axis=0).astype(jnp.bfloat16)
    out = lax.dot_general(left, picked, NT, preferred_element_type=jnp.float32)
    return [
        out[c : c + 1] + out[count + c : count + c + 1] + out[2 * count + c : 2 * count + c + 1]
        for c in range(count)
    ]


def matches(column, places):
    low = jnp.where(column == places[0:1], 1.0, 0.0)
    high = jnp.where(column == places[1:2], 1.0, 0.0)
    return jnp.concatenate([low, high], axis=1).astype(jnp.bfloat16)


def make_lists(metas, group_meta, list_a, list_b, live_a, live_b, lag_a, lag_b):
    z, y, core, x = grid_place()
    table = jnp.concatenate(
        [metas[...].reshape(32, HALF), jnp.zeros((HALF - 32, HALF), jnp.float32)], axis=0
    ).T

    def lane_row(rows):
        out = rows[0]
        for j in range(1, 4):
            out = out + pltpu.roll(rows[j], 32 * j, 1)
        return out

    blocks = lane_row([table[j : j + 1] for j in range(4)])
    lives = lane_row([table[4 + j : 5 + j] for j in range(4)])
    lags = lane_row([table[8:9]] * 4)
    label = lanes((1, HALF)).astype(jnp.float32)
    wanted = jnp.concatenate(
        [group_meta[t][:, j : j + 1] for t in range(8) for j in range(BLOCKS)], axis=0
    )
    base = ((z * 4 + y) * 2 * BPD).astype(jnp.float32)
    mask = jnp.concatenate(
        [
            jnp.where(wanted == blocks, 1.0, 0.0),
            jnp.where((blocks >= base) & (blocks < base + 2 * BPD), 1.0, 0.0),
            jnp.zeros((15, HALF), jnp.float32),
        ],
        axis=0,
    )
    ahead = jnp.where(rows_of((HALF, HALF)) < lanes((HALF, HALF)), 1.0, 0.0)
    within = jnp.dot(mask, ahead, precision=HIGHEST, preferred_element_type=jnp.float32)
    totals = jnp.broadcast_to(jnp.sum(mask, axis=1, keepdims=True), (48, HALF))
    row, col = rows_of((48, 48)), lanes((48, 48))
    above = jnp.where((row > col) & (row < TARGETS), 1.0, 0.0)
    rank = within + jnp.dot(above, totals, precision=HIGHEST, preferred_element_type=jnp.float32)
    rank = jnp.where(mask > 0.0, rank, -1.0)
    count_a = jnp.sum(totals[0:TARGETS, 0:1], axis=0, keepdims=True)
    count_b = totals[TARGETS : TARGETS + 1, 0:1]
    over = jnp.where((count_a > PAIRS) | (count_b > SLOTS), 1.0, 0.0)

    def spread(values):
        return jnp.broadcast_to(jnp.sum(values, axis=1, keepdims=True), values.shape)

    def store(code, list_ref, live_ref, lag_ref):
        list_ref[...] = spread(code).astype(jnp.int32)
        live_ref[...] = spread(jnp.where(code > 0.0, lives, 0.0))
        lag_ref[...] = spread(jnp.where(code > 0.0, lags, 0.0))

    slot = rows_of((32, HALF)).astype(jnp.float32)
    code = jnp.zeros((32, HALF), jnp.float32)
    for r in range(TARGETS):
        code += jnp.where(slot == rank[r : r + 1], label * 64.0 + (r + 1.0), 0.0)
    store(code, list_a, live_a, lag_a)
    slot = rows_of((24, HALF)).astype(jnp.float32)
    code = jnp.where(slot == rank[TARGETS : TARGETS + 1], label * 64.0 + (blocks - base + 1.0), 0.0)
    store(code, list_b, live_b, lag_b)
    return over


def placing(codes, count):
    row = (codes & 63) - 1
    here = jnp.where(row == lanes(codes.shape), 1.0, 0.0)
    size = codes.shape[0]
    square = jnp.concatenate([here, jnp.zeros((HALF - size, HALF), jnp.float32)], axis=0).T
    return square[0:count, 0:size]


def whole_kernel(
    valid, slots, hits, white, taps, stream, angle, offset,
    solution_out, residual_out, over_out,
    hold, taps_row, fixed, meta, base, message, row_two, message_two,
    all_fixed, all_base, all_meta, all_first, meta_two, all_second, meta_three,
    group_fixed, group_meta, sums_out, sums_in, next_out, next_in, last_row, group_row,
    columns, picked_a, picked_b, trig_a, trig_b, list_a, list_b, live_a, live_b, lag_a, lag_b,
    near_a, near_b, result_a, result_b, comps, factors, halo_rows,
    own_part, partner_part, x_part, owned, inverse,
    send_sems, recv_sems, local_sems, group_send, group_recv, halo_send, halo_recv, list_sems,
):
    z, y, core, x = grid_place()
    tm = x
    barrier = pltpu.get_barrier_semaphore()
    peers = [device_at(lax.rem(z + d, 8), y, core, x) for d in range(1, 8)] + [
        device_at(z, lax.rem(y + d, 4), core, x) for d in range(1, 4)
    ]
    for k in range(1, 8):
        peers.append(device_at(z, y, lax.rem(core + k % 2, 2), lax.rem(x + k // 2, 4)))
    for peer in peers:
        pl.semaphore_signal(barrier, inc=1, device_id=peer, device_id_type=MESH)

    place_of = offset[...].astype(jnp.float32)
    for block in range(BLOCKS):
        fixed[block, 0] = angle[2 * block : 2 * block + 2]
        fixed[block, 1] = place_of[2 * block : 2 * block + 2]
    taps_row[...] = jnp.zeros_like(taps_row)
    taps_row[:, : BAND + 1] = taps[...]
    lag_zero = jnp.sum(taps_row[...] * taps_row[...], axis=1, keepdims=True) + white[0, 0]
    remaining = valid[0, 0] - tm * SPAN
    lane = lanes((1, HALF))
    header = jnp.where(lane == 8, jnp.broadcast_to(lag_zero, (1, HALF)), 0.0)
    for block in range(BLOCKS):
        found = hits[0, slots[0, block]].astype(jnp.float32)
        count = jnp.clip(remaining - block * WIN, 0, WIN).astype(jnp.float32)
        header = jnp.where(lane == block, found, header)
        header = jnp.where(lane == 4 + block, count, header)
    meta[...] = header
    own_live = rows_of((8, HALF)) * HALF + lanes((8, HALF)) < remaining

    pl.semaphore_wait(barrier, len(peers))
    halos = [
        pltpu.make_async_remote_copy(
            src_ref=source,
            dst_ref=target,
            send_sem=halo_send.at[i],
            recv_sem=halo_recv.at[i],
            device_id=device_at(z, y, core, lax.rem(x + step, 4)),
            device_id_type=MESH,
        )
        for i, (source, target, step) in enumerate(
            (
                (stream.at[pl.ds(7, 1)], hold.at[0], 1),
                (stream.at[pl.ds(0, 1)], hold.at[1], 3),
            )
        )
    ]
    for copy in halos:
        copy.start()
    sems = (send_sems, recv_sems, local_sems)
    smalls = [
        Mover(meta, all_meta, sems, 0),
        Mover(row_two.at[0], meta_two, sems, 1),
        Mover(row_two.at[1], meta_three, sems, 2),
    ]
    relays = [
        Mover(fixed, all_fixed, sems, 3),
        Mover(message, all_first, sems, 4),
        Mover(message_two, all_second, sems, 5),
        Mover(base, all_base, sems, 6),
    ]
    group = Group(group_send, group_recv)
    me = group.me
    big, small, mid = relays[0], smalls[0], relays[3]
    small.start_first()
    big.start_first()
    places_in = group.to_all(0, lambda t: fixed, group_fixed.at[me])
    blocks_in = group.to_all(1, lambda t: meta, group_meta.at[me])
    group_fixed[me] = fixed[...]
    group_meta[me] = meta[...]

    spread = jnp.broadcast_to(taps_row[...], (WIN, WIN))
    shifted = pltpu.roll(spread, HALF, 1, stride=1, stride_axis=0)
    lag_row = lax.dot_general(
        spread[:8], shifted, NT, precision=HIGHEST, preferred_element_type=jnp.float32
    )
    lag_row = lag_row + jnp.where(lanes((8, WIN)) == HALF, white[0, 0], 0.0)
    band = pltpu.roll(
        jnp.broadcast_to(lag_row[0:1], (WIN, WIN)), WIN - HALF - BAND, 1, stride=1, stride_axis=0
    )[:, :HALF]
    landed(halos)
    extended = jnp.concatenate(
        [hold[0], stream[...], hold[1], jnp.zeros((6, HALF), jnp.float32)], axis=0
    )
    place = (rows_of((16, HALF)) - 1) * HALF + lanes((16, HALF))
    extended = jnp.where((place < remaining) & (place + tm * SPAN >= 0), extended, 0.0)
    base_own = jnp.where(own_live, band_filter(extended, band), 0.0)
    for block in range(BLOCKS):
        base[block] = base_own[2 * block : 2 * block + 2]
    mid.start_first()

    comps[...] = jnp.zeros_like(comps)
    halo_rows[...] = jnp.zeros_like(halo_rows)
    sums_out[...] = jnp.zeros_like(sums_out)
    result_a[...] = jnp.zeros_like(result_a)
    result_b[...] = jnp.zeros_like(result_b)
    landed(places_in)
    landed(blocks_in)
    for block in range(BLOCKS):
        comps[9, block : block + 1, :] = joined(fixed[block, 0])
    right = group_fixed[jnp.minimum(x + 1, 3) * 2 + core, 0, 0]
    left = group_fixed[jnp.maximum(x - 1, 0) * 2 + core, BLOCKS - 1, 0]
    comps[9, 4:5, :] = jnp.concatenate([right[0:1], left[1:2]], axis=1)
    turn = 2.0 * comps[9]
    comps[9] = jnp.cos(turn)
    comps[10] = jnp.sin(turn)
    turned = jnp.concatenate(
        [group_fixed[t, block, 1] for t in range(8) for block in range(BLOCKS)]
        + [jnp.zeros((HALF // 2, HALF), jnp.float32)],
        axis=0,
    ).T

    def column(t, block, half):
        at = 8 * t + 2 * block + half
        return jnp.broadcast_to(turned[:, at : at + 1], (HALF, HALF))

    for t in range(8):
        for block in range(BLOCKS):
            for half in range(2):
                columns[BLOCKS * t + block, HALF * half : HALF * half + HALF, :] = column(
                    t, block, half
                )

    small.start_second()
    big.start_second()
    mid.start_second()
    small.arrive()
    over = make_lists(all_meta, group_meta, near_a, near_b, live_a, live_b, lag_a, lag_b)
    copies = [
        pltpu.make_async_copy(near_a, list_a, list_sems.at[0]),
        pltpu.make_async_copy(near_b, list_b, list_sems.at[1]),
    ]
    for copy in copies:
        copy.start()
    into_a = placing(near_a[...], TARGETS)
    into_b = placing(near_b[...], 2 * BPD)
    for copy in copies:
        copy.wait()
    big.arrive()
    mid.arrive()

    wide_lane = lanes((1, WIN)).astype(jnp.float32)

    def doubled(row):
        return jnp.concatenate([row, row], axis=1)

    def nine(p, where_at, trig, live, lag):
        turn = 2.0 * all_fixed[where_at + (0,)]
        co2, si2 = jnp.cos(turn), jnp.sin(turn)
        trig[p, 0:2, :] = co2
        trig[p, 2:4, :] = si2
        co, si = joined(co2), joined(si2)
        f = joined(all_base[where_at])
        weight = jnp.where(
            wide_lane < doubled(live[pl.ds(p, 1), :]), doubled(lag[pl.ds(p, 1), :]), 0.0
        )
        return all_fixed[where_at + (1,)], [f, f * co, f * si] + weight_rows(weight, co, si)

    def three(p, where_at, trig, source):
        f = joined(source[where_at])
        return [f, f * joined(trig[p, 0:2, :]), f * joined(trig[p, 2:4, :])]

    def keep_rows(result, p, values):
        for c, value in enumerate(values):
            result[pl.ds(p, 1), WIN * c : WIN * c + WIN] = value

    def gathered_rows(into, result, count):
        return jnp.dot(
            into, result[:, 0 : WIN * count], precision=HIGHEST, preferred_element_type=jnp.float32
        )

    def pair_first(p, carry):
        code = list_a[p, 0]
        places, values = nine(
            p, locate(lax.shift_right_logical(code, 6)), trig_a, live_a, lag_a
        )
        picked = matches(columns[jnp.clip((code & 63) - 1, 0, TARGETS - 1)], places)
        picked_a[p] = picked
        keep_rows(result_a, p, split_product(values, picked))
        return carry

    lax.fori_loop(0, PAIRS, pair_first, 0, unroll=2)
    def hand_out(count, target):
        out = gathered_rows(into_a, result_a, count)
        empty = jnp.zeros((1, HALF), jnp.float32)
        for t in range(8):
            for c in range(count):
                at = WIN * c
                first = BLOCKS * t
                target[t, 5 * c : 5 * c + 4, :] = out[first : first + 4, at : at + WIN]
                right = out[first + 8 : first + 9, at : at + HALF] if t < 6 else empty
                left = out[first - 5 : first - 4, at + HALF : at + WIN] if t >= 2 else empty
                target[t, 5 * c + 4 : 5 * c + 5, :] = jnp.concatenate([right, left], axis=1)

    hand_out(9, sums_out)
    arriving = group.to_all(2, lambda t: sums_out.at[t], sums_in.at[me])
    sums_in[me] = sums_out[me]
    landed(arriving)
    combined = sums_in[0]
    for t in range(1, 8):
        combined = combined + sums_in[t]
    for c in range(9):
        comps[c, 0:5, :] = combined[5 * c : 5 * c + 5]
    m_aa, m_ab, m_ac, m_bb, m_bc, m_cc, det = adjugate(*(comps[c] for c in range(3, 9)))
    co, si = comps[9], comps[10]
    seg_row = rows_of((8, WIN))
    at = lanes((8, WIN))
    time = tm * SPAN + jnp.where(
        seg_row < BLOCKS, seg_row * WIN + at, jnp.where(at < HALF, SPAN + at, at - WIN)
    )
    inside = (seg_row < BLOCKS) | ((seg_row == BLOCKS) & ((at < BAND) | (at >= WIN - BAND)))
    live = (time >= 0) & (time < valid[0, 0]) & inside
    scale = jnp.where(live, 1.0, 0.0) / det
    factors[0] = (m_aa + m_ab * co + m_ac * si) * scale
    factors[1] = (m_ab + m_bb * co + m_bc * si) * scale
    factors[2] = (m_ac + m_bc * co + m_cc * si) * scale

    def change():
        return factors[0] * comps[0] + factors[1] * comps[1] + factors[2] * comps[2]

    def filter_signal(signal, out):
        halo_rows[0:1] = signal[4:5, HALF:]
        for block in range(BLOCKS):
            halo_rows[2 * block + 1 : 2 * block + 2] = signal[block : block + 1, :HALF]
            halo_rows[2 * block + 2 : 2 * block + 3] = signal[block : block + 1, HALF:]
        halo_rows[9:10] = signal[4:5, :HALF]
        result = jnp.where(own_live, band_filter(halo_rows[...], band), 0.0)
        for block in range(BLOCKS):
            out[block] = result[2 * block : 2 * block + 2]
        return result

    signal_first = change()
    filtered_first = filter_signal(signal_first, message)
    own = halo_rows[1:9]
    row_two[0] = (
        jnp.where(lane == 0, total(base_own * own), 0.0)
        + jnp.where(lane == 1, total(filtered_first * own), 0.0)
        + jnp.where(lane == 2, over, 0.0)
    )

    pixel = rows_of((WIN, HALF)).astype(jnp.float32)

    def owned_first(p, carry):
        code = list_b[p, 0]
        places, values = nine(
            p, locate(lax.shift_right_logical(code, 6)), trig_b, live_b, lag_b
        )
        picked = matches(pixel, places)
        picked_b[p] = picked
        keep_rows(result_b, p, split_product(values, picked))
        return carry

    def owned_next(source):
        def body(p, carry):
            code = list_b[p, 0]
            values = three(p, locate(lax.shift_right_logical(code, 6)), trig_b, source)
            keep_rows(result_b, p, split_product(values, picked_b[p]))
            return carry

        return body

    def owned_out(first, count, number):
        out = gathered_rows(into_b, result_b, count)
        for half in range(2):
            for c in range(count):
                own_part[half, first + c] = out[BPD * half : BPD * half + BPD, WIN * c : WIN * c + WIN]
        span = pl.ds(first, count)
        return group.to_partner(number, own_part.at[1 - core, span], partner_part.at[span])

    def owned_along(first, count, number, arriving):
        landed(arriving)
        span = pl.ds(first, count)
        x_part[x, span] = own_part[core, span] + partner_part[span]
        return group.along(number, x_part.at[x, span])

    def owned_sum(first, count):
        span = pl.ds(first, count)
        owned[span] = x_part[0, span] + x_part[1, span] + x_part[2, span] + x_part[3, span]

    def sums_of(metas):
        return jnp.sum(metas[...].reshape(32, 1, HALF), axis=0)

    big, small = relays[1], smalls[1]
    small.start_first()
    big.start_first()
    lax.fori_loop(0, SLOTS, owned_first, 0, unroll=2)
    small.start_second()
    big.start_second()
    waiting_first = owned_out(0, 9, 5)
    small.arrive()
    sums = sums_of(meta_two)
    big.arrive()

    def pair_second(p, carry):
        code = list_a[p, 0]
        values = three(p, locate(lax.shift_right_logical(code, 6)), trig_a, all_first)
        keep_rows(result_a, p, split_product(values, picked_a[p]))
        return carry

    lax.fori_loop(0, PAIRS, pair_second, 0, unroll=4)
    hand_out(3, next_out)
    for t in range(8):
        next_out[t, 15:16, :] = doubled(sums)
    arriving = group.to_all(3, lambda t: next_out.at[t], next_in.at[me])
    next_in[me] = next_out[me]
    landed(arriving)
    combined = next_in[0]
    for t in range(1, 8):
        combined = combined + next_in[t]
    for c in range(3):
        comps[c, 0:5, :] = combined[5 * c : 5 * c + 5]
    sums = combined[15:16, :HALF]
    product, curve = sums[:, 0:1], sums[:, 1:2]
    over_out[...] = jnp.broadcast_to(sums[:, 2:3], (1, HALF))
    alpha = product / curve
    filtered_second = filter_signal(signal_first - alpha * change(), message_two)
    own = halo_rows[1:9]
    row_two[1] = (
        jnp.where(lane == 0, total((base_own - alpha * filtered_first) * own), 0.0)
        + jnp.where(lane == 1, total(filtered_second * own), 0.0)
        + jnp.where(lane == 2, total(filtered_first * own), 0.0)
    )

    big, small = relays[2], smalls[2]
    small.start_first()
    big.start_first()
    first_along = owned_along(0, 9, 6, waiting_first)
    lax.fori_loop(0, SLOTS, owned_next(all_first), 0, unroll=4)
    waiting_second = owned_out(9, 3, 7)
    small.start_second()
    big.start_second()
    second_along = owned_along(9, 3, 8, waiting_second)
    small.arrive()
    last_row[...] = sums_of(meta_three)
    rows_in = group.to_all(4, lambda t: last_row, group_row.at[me])
    group_row[me] = last_row[...]
    big.arrive()
    lax.fori_loop(0, SLOTS, owned_next(all_second), 0, unroll=4)
    waiting_third = owned_out(12, 3, 9)
    third_along = owned_along(12, 3, 10, waiting_third)

    landed(rows_in)
    sums = group_row[0]
    for t in range(1, 8):
        sums = sums + group_row[t]
    product_next = sums[:, 0:1]
    beta = product_next / product
    curve_next = sums[:, 1:2] + 2.0 * beta * sums[:, 2:3] + beta * beta * curve
    alpha_next = product_next / curve_next

    def solve(r1, r2, r3):
        i_aa, i_ab, i_ac, i_bb, i_bc, i_cc = (inverse[c] for c in range(6))
        return (
            i_aa * r1 + i_ab * r2 + i_ac * r3,
            i_ab * r1 + i_bb * r2 + i_bc * r3,
            i_ac * r1 + i_bc * r2 + i_cc * r3,
        )

    landed(first_along)
    owned_sum(0, 9)
    *minors, det = adjugate(*(owned[c] for c in range(3, 9)))
    scale = 1.0 / det
    for c, minor in enumerate(minors):
        inverse[c] = minor * scale
    landed(second_along)
    owned_sum(9, 3)
    start = solve(*(owned[c] for c in range(3)))
    for c in range(3):
        owned[c] = owned[c] - alpha * owned[9 + c]
    middle = solve(*(owned[c] for c in range(3)))
    for c in range(3):
        solution_out[c] = alpha * start[c] + alpha_next * (middle[c] + beta * start[c])
        owned[c] = owned[c] - alpha_next * beta * owned[9 + c]
    landed(third_along)
    owned_sum(12, 3)
    final = solve(*(owned[c] - alpha_next * owned[12 + c] for c in range(3)))
    for c in range(3):
        residual_out[c] = final[c]
    for mover in smalls + relays + [group]:
        mover.finish()
    for copy in halos:
        copy.wait_send()


def f32(*shape):
    return jax.ShapeDtypeStruct(shape, jnp.float32)


def gathered_shape(rows):
    return f32(2, 8, 4, 4, rows, HALF)


def gather_rows(values, part, number):
    rows, parts = pl.pallas_call(
        gather_kernel,
        out_shape=(gathered_shape(8), gathered_shape(1)),
        in_specs=[vmem] * 2,
        out_specs=(vmem,) * 2,
        scratch_shapes=EXCHANGE_SCRATCH,
        compiler_params=pltpu.CompilerParams(collective_id=number, has_side_effects=True),
        name="gather",
    )(values, part)
    return rows.reshape(LABELS, 2, HALF), parts.reshape(DEVICES, HALF)


def any_lengths(
    time_streams, pol_angle, offsets, block_slots, hit_ids, valid_counts, filter_taps, white_weight
):
    valid = valid_counts.reshape(1)
    message, metas, base, band = pl.pallas_call(
        prepare_kernel,
        out_shape=(gathered_shape(32), gathered_shape(1), f32(8, HALF), f32(WIN, HALF)),
        in_specs=[smem] * 4 + [vmem] * 4,
        out_specs=(vmem,) * 4,
        scratch_shapes=[
            pltpu.VMEM((2, 1, HALF), jnp.float32),
            pltpu.VMEM((1, WIN), jnp.float32),
            pltpu.VMEM((32, HALF), jnp.float32),
            pltpu.VMEM((1, HALF), jnp.float32),
        ]
        + EXCHANGE_SCRATCH
        + [pltpu.SemaphoreType.DMA((2,)), pltpu.SemaphoreType.DMA((2,))],
        compiler_params=pltpu.CompilerParams(collective_id=0, has_side_effects=True),
        name="prepare",
    )(
        valid, block_slots.reshape(BLOCKS), hit_ids.reshape(-1), white_weight.reshape(1),
        filter_taps.reshape(1, BAND + 1), time_streams.reshape(8, HALF), pol_angle.reshape(8, HALF),
        offsets.reshape(8, HALF),
    )
    gathered = message.reshape(LABELS, 8, HALF)
    metas = metas.reshape(DEVICES, HALF)

    blocks = metas[:, 0:4].reshape(LABELS)
    lives = metas[:, 4:8].reshape(LABELS).astype(jnp.int32)
    lag_zero = metas[:, 8]
    order = jnp.arange(LABELS, dtype=jnp.int32)
    same = blocks[:, None] == blocks[None, :]
    ahead = (order[None, :] - order[:, None] - 1) % LABELS
    nexts = (order + 1 + jnp.min(jnp.where(same, ahead, LABELS), axis=1)) % LABELS
    counts = jnp.sum(same, axis=1, dtype=jnp.int32)
    owned = (lax.axis_index("det") * BPD + jnp.arange(BPD, dtype=jnp.int32)).astype(jnp.float32)
    mine = owned[:, None] == blocks[None, :]
    heads = jnp.concatenate(
        [
            jnp.min(jnp.where(mine, order[None, :], LABELS - 1), axis=1),
            jnp.sum(mine, axis=1, dtype=jnp.int32),
        ]
    )

    first, part_one, factors, signal = pl.pallas_call(
        first_kernel,
        out_shape=(f32(8, HALF), f32(1, HALF), f32(3, 8, WIN), f32(8, WIN)),
        in_specs=[smem] * 5 + [vmem] * 3,
        out_specs=(vmem,) * 4,
        scratch_shapes=[
            pltpu.VMEM((12, 8, WIN), jnp.float32),
            pltpu.VMEM((16, HALF), jnp.float32),
        ],
        name="first",
    )(valid, nexts, counts, lives, lag_zero, gathered, base, band)
    second, parts_two = gather_rows(first, part_one, 1)
    other, part_two = pl.pallas_call(
        second_kernel,
        out_shape=(f32(8, HALF), f32(1, HALF)),
        in_specs=[smem] * 3 + [vmem] * 8,
        out_specs=(vmem,) * 2,
        scratch_shapes=[
            pltpu.VMEM((3, 8, WIN), jnp.float32),
            pltpu.VMEM((16, HALF), jnp.float32),
        ],
        name="second",
    )(valid, nexts, counts, gathered, second, parts_two, base, first, band, factors, signal)
    third, parts_three = gather_rows(other, part_two, 2)
    answers = pl.pallas_call(
        last_kernel,
        out_shape=(f32(3, BPD, WIN), f32(3, BPD, WIN)),
        in_specs=[smem] * 4 + [vmem] * 5,
        out_specs=(vmem,) * 2,
        scratch_shapes=[pltpu.VMEM((15, BPD, WIN), jnp.float32)],
        name="last",
    )(heads, nexts, lives, lag_zero, gathered, second, third, parts_two, parts_three)
    return tuple(answers)


def wide_buffer(*shape):
    return pltpu.VMEM((8, 4) + shape, jnp.float32)


def room(*shape):
    return pltpu.VMEM(shape, jnp.float32)


def per_device(*args):
    (
        time_streams, pol_angle, offsets, block_slots, hit_ids, valid_counts, filter_taps,
        white_weight,
    ) = args
    fast = pl.pallas_call(
        whole_kernel,
        out_shape=(f32(3, BPD, WIN), f32(3, BPD, WIN), f32(1, HALF)),
        in_specs=[smem] * 4 + [vmem] * 4,
        out_specs=(vmem,) * 3,
        scratch_shapes=[
            room(2, 1, HALF), room(1, WIN), room(BLOCKS, 2, 2, HALF), room(1, HALF),
            room(BLOCKS, 2, HALF), room(BLOCKS, 2, HALF), room(2, 1, HALF), room(BLOCKS, 2, HALF),
            wide_buffer(BLOCKS, 2, 2, HALF), wide_buffer(BLOCKS, 2, HALF), wide_buffer(1, HALF),
            wide_buffer(BLOCKS, 2, HALF), wide_buffer(1, HALF), wide_buffer(BLOCKS, 2, HALF),
            wide_buffer(1, HALF),
            room(8, BLOCKS, 2, 2, HALF), room(8, 1, HALF), room(8, 48, WIN), room(8, 48, WIN),
            room(8, 16, WIN), room(8, 16, WIN), room(1, HALF), room(8, 1, HALF),
            room(TARGETS, WIN, HALF),
            pltpu.VMEM((PAIRS, WIN, WIN), jnp.bfloat16),
            pltpu.VMEM((SLOTS, WIN, WIN), jnp.bfloat16),
            room(PAIRS, 4, HALF), room(SLOTS, 4, HALF),
            pltpu.SMEM((32, HALF), jnp.int32), pltpu.SMEM((24, HALF), jnp.int32),
            room(32, HALF), room(24, HALF), room(32, HALF), room(24, HALF),
            pltpu.VMEM((32, HALF), jnp.int32), pltpu.VMEM((24, HALF), jnp.int32),
            room(32, 9 * WIN), room(24, 9 * WIN),
            room(11, 8, WIN), room(3, 8, WIN), room(16, HALF),
            room(2, 15, BPD, WIN), room(15, BPD, WIN), room(4, 15, BPD, WIN), room(15, BPD, WIN),
            room(6, BPD, WIN),
            pltpu.SemaphoreType.DMA((7, 10)), pltpu.SemaphoreType.DMA((7, 10)),
            pltpu.SemaphoreType.DMA((7,)), pltpu.SemaphoreType.DMA((11, 8)),
            pltpu.SemaphoreType.DMA((11, 8)), pltpu.SemaphoreType.DMA((2,)),
            pltpu.SemaphoreType.DMA((2,)), pltpu.SemaphoreType.DMA((2,)),
        ],
        compiler_params=pltpu.CompilerParams(collective_id=3, has_side_effects=True),
        name="whole",
    )(
        valid_counts, block_slots.reshape(1, BLOCKS), hit_ids, white_weight,
        filter_taps.reshape(1, BAND + 1), time_streams.reshape(8, HALF),
        pol_angle.reshape(8, HALF), offsets.reshape(8, HALF),
    )
    answers = lax.cond(
        fast[2][0, 0] > 0.0, lambda f, *a: any_lengths(*a), lambda f, *a: f, fast[:2], *args
    )
    return tuple(jnp.transpose(answer, (1, 0, 2)) for answer in answers)


def solution(mesh):
    in_specs = (
        P("det", None, "tm"),
        P("det", None, "tm"),
        P("det", None, "tm"),
        P("det", None, "tm"),
        P("det", None),
        P("det", None),
        P("det", None, None),
        P("det", None),
    )
    out_specs = (P("det", None, None), P("det", None, None))
    return jax.shard_map(
        per_device, mesh=mesh, in_specs=in_specs, out_specs=out_specs, check_vma=False
    )
```

```python
import functools

import jax
import jax.numpy as jnp
from jax import lax
from jax.experimental import pallas as pl
from jax.experimental.pallas import tpu as pltpu
from jax.sharding import PartitionSpec as P

WIN = 256
BAND = 64
BPD = 16
HALF = 128
SPAN = 1024
BLOCKS = 4
DEVICES = 256
PAIRS = 24
TARGETS = 32
UNROLL = 4
SLOTS = 20
LABELS = DEVICES * BLOCKS

HIGHEST = lax.Precision.HIGHEST
NT = (((1,), (1,)), ((), ()))
MESH = pl.DeviceIdType.MESH

vmem = pl.BlockSpec(memory_space=pltpu.VMEM)
smem = pl.BlockSpec(memory_space=pltpu.SMEM)


def lanes(shape):
    return lax.broadcasted_iota(jnp.int32, shape, len(shape) - 1)


def rows_of(shape):
    return lax.broadcasted_iota(jnp.int32, shape, 0)


def band_filter(extended, band):
    turned = pltpu.roll(extended, HALF // 2, 1)
    keep = lanes((8, HALF)) < HALF // 2
    first = jnp.where(keep, turned[0:8], turned[1:9])
    second = jnp.where(keep, turned[1:9], turned[2:10])
    window = jnp.concatenate([first, second], axis=1)
    return jnp.dot(window, band, precision=HIGHEST, preferred_element_type=jnp.float32)


def grid_place():
    det = lax.axis_index("det")
    x = lax.axis_index("tm")
    return lax.div(det, 8), lax.rem(lax.div(det, 2), 4), lax.rem(det, 2), x


def device_at(z, y, core, x):
    return {"det": (z * 4 + y) * 2 + core, "tm": x}


def slot_of(z, y, core, x):
    major = y + core * (x - y)
    minor = x + core * (y - x)
    return ((core * 8 + z) * 4 + major) * 4 + minor


def meet():
    z, y, core, x = grid_place()
    barrier = pltpu.get_barrier_semaphore()
    peers = (
        [device_at(lax.rem(z + d, 8), y, core, x) for d in range(1, 8)]
        + [device_at(z, lax.rem(y + d, 4), core, x) for d in range(1, 4)]
        + [device_at(z, y, core, lax.rem(x + d, 4)) for d in range(1, 4)]
        + [device_at(z, y, 1 - core, x)]
    )
    for peer in peers:
        pl.semaphore_signal(barrier, inc=1, device_id=peer, device_id_type=MESH)
    pl.semaphore_wait(barrier, len(peers))


def exchange(sources, buffers, send_sems, recv_sems, local_sems):
    z, y, core, x = grid_place()
    a = y + core * (x - y)
    b = x + core * (y - x)

    def major_peer(step):
        return device_at(
            z,
            y + (1 - core) * (lax.rem(y + step, 4) - y),
            core,
            x + core * (lax.rem(x + step, 4) - x),
        )

    def minor_peer(step):
        return device_at(
            z,
            y + core * (lax.rem(y + step, 4) - y),
            core,
            x + (1 - core) * (lax.rem(x + step, 4) - x),
        )

    arrays = range(len(sources))

    def send(number, source_of, target_of, peer):
        copies = []
        for i in arrays:
            copy = pltpu.make_async_remote_copy(
                src_ref=source_of(i),
                dst_ref=target_of(i),
                send_sem=send_sems.at[i, number],
                recv_sem=recv_sems.at[i, number],
                device_id=peer,
                device_id_type=MESH,
            )
            copy.start()
            copies.append(copy)
        return copies

    def landed(copies):
        for copy in copies:
            copy.wait_recv()

    started = []
    keep = [
        pltpu.make_async_copy(sources[i], buffers[i].at[core, z, a, b], local_sems.at[i])
        for i in arrays
    ]
    first = [
        send(
            d - 1,
            lambda i: sources[i],
            lambda i: buffers[i].at[core, z, a, b],
            device_at(lax.rem(z + d, 8), y, core, x),
        )
        for d in (4, 3, 5, 2, 6, 1, 7)
    ]
    for copy in keep:
        copy.start()
    for copy in keep:
        copy.wait()
    for copies in first:
        landed(copies)
    started += first

    def column(i):
        return buffers[i].at[core, :, a, b]

    second = [send(6 + d, column, column, major_peer(d)) for d in (2, 1, 3)]
    for copies in second:
        landed(copies)
    started += second

    def part(number, half):
        depth = pl.ds(4 * half, 4)
        return lambda i: buffers[i].at[core, depth, :, number]

    def whole(number):
        return lambda i: buffers[i].at[core, :, :, number]

    after = minor_peer(1)
    before = minor_peer(3)
    partner = device_at(z, y, 1 - core, x)
    left = lax.rem(b + 3, 4)
    right = lax.rem(b + 1, 4)
    far = lax.rem(b + 2, 4)
    up = [send(10, part(b, 0), part(b, 0), after)]
    down = [send(12, part(b, 1), part(b, 1), before)]
    up.append(send(11, part(b, 1), part(b, 1), after))
    down.append(send(13, part(b, 0), part(b, 0), before))
    swaps = [send(16, whole(b), whole(b), partner)]
    landed(up[0])
    up.append(send(14, part(left, 0), part(left, 0), after))
    landed(down[0])
    down.append(send(15, part(right, 1), part(right, 1), before))
    landed(up[1])
    swaps.append(send(17, whole(left), whole(left), partner))
    landed(down[1])
    swaps.append(send(18, whole(right), whole(right), partner))
    landed(up[2])
    landed(down[2])
    swaps.append(send(19, whole(far), whole(far), partner))
    for copies in swaps:
        landed(copies)
    started += up + down + swaps
    for copies in started:
        for copy in copies:
            copy.wait_send()


EXCHANGE_SCRATCH = [
    pltpu.SemaphoreType.DMA((2, 20)),
    pltpu.SemaphoreType.DMA((2, 20)),
    pltpu.SemaphoreType.DMA((2,)),
]


def gather_kernel(values, meta, values_out, meta_out, send_sems, recv_sems, local_sems):
    meet()
    exchange([values, meta], [values_out, meta_out], send_sems, recv_sems, local_sems)


def prepare_kernel(
    valid, slots, hits, white, taps, stream, angle, offset,
    message_out, meta_out, base_out, band,
    hold, taps_row, message, meta, send_sems, recv_sems, local_sems, halo_send, halo_recv,
):
    meet()
    z, y, core, x = grid_place()
    tm = x
    halos = [
        pltpu.make_async_remote_copy(
            src_ref=stream.at[pl.ds(7, 1)],
            dst_ref=hold.at[0],
            send_sem=halo_send.at[0],
            recv_sem=halo_recv.at[0],
            device_id=device_at(z, y, core, lax.rem(x + 1, 4)),
            device_id_type=MESH,
        ),
        pltpu.make_async_remote_copy(
            src_ref=stream.at[pl.ds(0, 1)],
            dst_ref=hold.at[1],
            send_sem=halo_send.at[1],
            recv_sem=halo_recv.at[1],
            device_id=device_at(z, y, core, lax.rem(x + 3, 4)),
            device_id_type=MESH,
        ),
    ]
    for copy in halos:
        copy.start()
    cosine = jnp.cos(2.0 * angle[...])
    sine = jnp.sin(2.0 * angle[...])
    place_of = offset[...].astype(jnp.float32)
    for block in range(BLOCKS):
        for half in range(2):
            row = 2 * block + half
            for part, values in enumerate((cosine, sine, place_of)):
                at = 8 * block + 4 * half + part + 1
                message[at : at + 1, :] = values[row : row + 1]
    taps_row[...] = jnp.zeros_like(taps_row)
    taps_row[:, : BAND + 1] = taps[...]
    spread = jnp.broadcast_to(taps_row[...], (WIN, WIN))
    shifted = pltpu.roll(spread, HALF, 1, stride=1, stride_axis=0)
    lag_row = lax.dot_general(
        spread[:8], shifted, NT, precision=HIGHEST, preferred_element_type=jnp.float32
    )
    lag_row = lag_row + jnp.where(lanes((8, WIN)) == HALF, white[0], 0.0)
    table = pltpu.roll(
        jnp.broadcast_to(lag_row[0:1], (WIN, WIN)), WIN - HALF - BAND, 1, stride=1, stride_axis=0
    )
    band[...] = table[:, :HALF]
    lag_zero = lag_row[0:1, HALF : HALF + 1]

    remaining = valid[0] - tm * SPAN
    lane = lanes((1, HALF))
    header = jnp.where(lane == 8, jnp.broadcast_to(lag_zero, (1, HALF)), 0.0)
    for block in range(BLOCKS):
        found = hits[slots[block]].astype(jnp.float32)
        count = jnp.clip(remaining - block * WIN, 0, WIN).astype(jnp.float32)
        header = jnp.where(lane == block, found, header)
        header = jnp.where(lane == 4 + block, count, header)
    meta[...] = header

    for copy in halos:
        copy.wait_recv()
    extended = jnp.concatenate(
        [hold[0], stream[...], hold[1], jnp.zeros((6, HALF), jnp.float32)], axis=0
    )
    place = (rows_of((16, HALF)) - 1) * HALF + lanes((16, HALF))
    extended = jnp.where((place < remaining) & (place + tm * SPAN >= 0), extended, 0.0)
    own_live = rows_of((8, HALF)) * HALF + lanes((8, HALF)) < remaining
    filtered = jnp.where(own_live, band_filter(extended, table[:, :HALF]), 0.0)
    for block in range(BLOCKS):
        for half in range(2):
            row = 2 * block + half
            at = 8 * block + 4 * half
            message[at : at + 1, :] = filtered[row : row + 1]
    base_out[...] = filtered
    exchange([message, meta], [message_out, meta_out], send_sems, recv_sems, local_sems)
    for copy in halos:
        copy.wait_send()


def split_rows(values):
    high = values.astype(jnp.bfloat16)
    rest = values - high.astype(jnp.float32)
    middle = rest.astype(jnp.bfloat16)
    low = (rest - middle.astype(jnp.float32)).astype(jnp.bfloat16)
    return jnp.concatenate([high, middle, low], axis=0)


def wide(tile, row):
    return jnp.concatenate([tile[row : row + 1], tile[row + 4 : row + 5]], axis=1)


def match_sum(column, places, values):
    count = values.shape[0]
    picked = jnp.where(column == places, 1.0, 0.0).astype(jnp.bfloat16)
    out = lax.dot_general(split_rows(values), picked, NT, preferred_element_type=jnp.float32)
    return out[:count] + out[count : 2 * count] + out[2 * count :]


def weight_rows(weight, cosine, sine):
    first = weight * cosine
    second = weight * sine
    return [weight, first, second, first * cosine, first * sine, second * sine]


def own_labels():
    z, y, core, x = grid_place()
    own = slot_of(z, y, core, x) * BLOCKS
    before = slot_of(z, y, core, jnp.maximum(x - 1, 0)) * BLOCKS + BLOCKS - 1
    after = slot_of(z, y, core, jnp.minimum(x + 1, 3)) * BLOCKS
    usable = [jnp.minimum(x, 1)] + [1] * BLOCKS + [jnp.minimum(3 - x, 1)]
    return [before] + [own + block for block in range(BLOCKS)] + [after], usable


def own_columns(labels, gathered):
    rows = []
    for seg in range(6):
        tile = gathered[labels[seg]]
        rows += [tile[3:4], tile[7:8]]
    rows.append(jnp.zeros((HALF - 12, HALF), jnp.float32))
    turned = jnp.concatenate(rows, axis=0).T
    return [
        jnp.concatenate([turned[:, 2 * s : 2 * s + 1], turned[:, 2 * s + 1 : 2 * s + 2]], axis=0)
        for s in range(6)
    ]


def adjugate(w1, w2, w3, w4, w5, w6):
    aa = 1.0 + w1
    bb = 1.0 + w4
    cc = 1.0 + w6
    m_aa = bb * cc - w5 * w5
    m_ab = w3 * w5 - w2 * cc
    m_ac = w2 * w5 - w3 * bb
    m_bb = aa * cc - w3 * w3
    m_bc = w2 * w3 - aa * w5
    m_cc = aa * bb - w2 * w2
    det = aa * m_aa + w2 * m_ab + w3 * m_ac
    return m_aa, m_ab, m_ac, m_bb, m_bc, m_cc, det


def rows_to_hold(signal, hold):
    hold[0:1] = signal[0:1, HALF:]
    for seg in range(1, 5):
        hold[2 * seg - 1 : 2 * seg] = signal[seg : seg + 1, :HALF]
        hold[2 * seg : 2 * seg + 1] = signal[seg : seg + 1, HALF:]
    hold[9:10] = signal[5:6, :HALF]


def total(values):
    return jnp.sum(jnp.sum(values, axis=1, keepdims=True), axis=0, keepdims=True)


def own_live_of(info):
    remaining = info[0] - lax.axis_index("tm") * SPAN
    return rows_of((8, HALF)) * HALF + lanes((8, HALF)) < remaining


def first_kernel(
    info, nexts, counts, lives, lag_zero, gathered, base, band,
    filtered_out, part_out, factors, signal_out, comps, hold,
):
    labels, flags = own_labels()
    columns = own_columns(labels, gathered)
    lane = lanes((1, WIN))
    comps[...] = jnp.zeros_like(comps)
    for seg in range(6):
        column = columns[seg]
        usable = flags[seg]

        def body(_, carry, column=column):
            label, acc = carry
            tile = gathered[label]
            f = wide(tile, 0)
            co = wide(tile, 1)
            si = wide(tile, 2)
            weight = jnp.where(lane < lives[label], lag_zero[label // BLOCKS], 0.0)
            values = jnp.concatenate(
                [f, f * co, f * si] + weight_rows(weight, co, si)
                + [jnp.zeros((7, WIN), jnp.float32)], axis=0,
            )
            return nexts[label], acc + match_sum(column, wide(tile, 3), values)

        start = labels[seg]
        _, acc = lax.fori_loop(
            0, counts[start] * usable, body, (start, jnp.zeros((16, WIN), jnp.float32))
        )
        for comp in range(9):
            comps[comp, seg : seg + 1, :] = acc[comp : comp + 1]
        tile = gathered[start]
        comps[9, seg : seg + 1, :] = wide(tile, 1)
        comps[10, seg : seg + 1, :] = wide(tile, 2)
        comps[11, seg : seg + 1, :] = jnp.where(lane < lives[start] * usable, 1.0, 0.0)
    m_aa, m_ab, m_ac, m_bb, m_bc, m_cc, det = adjugate(*(comps[c] for c in range(3, 9)))
    co, si, live = comps[9], comps[10], comps[11]
    scale = live / det
    q1 = (m_aa + m_ab * co + m_ac * si) * scale
    q2 = (m_ab + m_bb * co + m_bc * si) * scale
    q3 = (m_ac + m_bc * co + m_cc * si) * scale
    factors[0] = q1
    factors[1] = q2
    factors[2] = q3
    signal = q1 * comps[0] + q2 * comps[1] + q3 * comps[2]
    signal_out[...] = signal
    hold[...] = jnp.zeros_like(hold)
    rows_to_hold(signal, hold)
    filtered = jnp.where(own_live_of(info), band_filter(hold[...], band[...]), 0.0)
    filtered_out[...] = filtered
    own = hold[1:9]
    lane = lanes((1, HALF))
    part_out[...] = jnp.where(lane == 0, total(base[...] * own), 0.0) + jnp.where(
        lane == 1, total(filtered * own), 0.0
    )


def second_kernel(
    info, nexts, counts, gathered, second, parts, base, own_first, band, factors, signal_in,
    filtered_out, part_out, comps, hold,
):
    sums = jnp.sum(parts[...], axis=0, keepdims=True)
    alpha = sums[:, 0:1] / sums[:, 1:2]
    labels, flags = own_labels()
    columns = own_columns(labels, gathered)
    comps[...] = jnp.zeros_like(comps)
    for seg in range(6):
        column = columns[seg]

        def body(_, carry, column=column):
            label, acc = carry
            tile = gathered[label]
            pair = second[label]
            f = jnp.concatenate([pair[0:1], pair[1:2]], axis=1)
            values = jnp.concatenate(
                [f, f * wide(tile, 1), f * wide(tile, 2), jnp.zeros((13, WIN), jnp.float32)], axis=0
            )
            return nexts[label], acc + match_sum(column, wide(tile, 3), values)

        start = labels[seg]
        _, acc = lax.fori_loop(
            0, counts[start] * flags[seg], body, (start, jnp.zeros((16, WIN), jnp.float32))
        )
        for comp in range(3):
            comps[comp, seg : seg + 1, :] = acc[comp : comp + 1]
    change = factors[0] * comps[0] + factors[1] * comps[1] + factors[2] * comps[2]
    signal = signal_in[...] - alpha * change
    hold[...] = jnp.zeros_like(hold)
    rows_to_hold(signal, hold)
    filtered = jnp.where(own_live_of(info), band_filter(hold[...], band[...]), 0.0)
    filtered_out[...] = filtered
    own = hold[1:9]
    first = own_first[...]
    lane = lanes((1, HALF))
    part_out[...] = (
        jnp.where(lane == 0, total((base[...] - alpha * first) * own), 0.0)
        + jnp.where(lane == 1, total(filtered * own), 0.0)
        + jnp.where(lane == 2, total(first * own), 0.0)
    )


def last_kernel(
    heads, nexts, lives, lag_zero, gathered, second, third, parts_two, parts_three,
    solution_out, residual_out, comps,
):
    sums = jnp.sum(parts_two[...], axis=0, keepdims=True)
    product, curve = sums[:, 0:1], sums[:, 1:2]
    alpha = product / curve
    sums = jnp.sum(parts_three[...], axis=0, keepdims=True)
    product_next = sums[:, 0:1]
    beta = product_next / product
    curve_next = sums[:, 1:2] + 2.0 * beta * sums[:, 2:3] + beta * beta * curve
    alpha_next = product_next / curve_next
    column = rows_of((WIN, 1)).astype(jnp.float32)
    lane = lanes((1, WIN))
    for block in range(BPD):

        def body(_, carry):
            label, acc = carry
            tile = gathered[label]
            co = wide(tile, 1)
            si = wide(tile, 2)
            pair = second[label]
            trio = third[label]
            rows = []
            for f in (
                wide(tile, 0),
                jnp.concatenate([pair[0:1], pair[1:2]], axis=1),
                jnp.concatenate([trio[0:1], trio[1:2]], axis=1),
            ):
                rows += [f, f * co, f * si]
            weight = jnp.where(lane < lives[label], lag_zero[label // BLOCKS], 0.0)
            values = jnp.concatenate(
                rows + weight_rows(weight, co, si) + [jnp.zeros((1, WIN), jnp.float32)], axis=0
            )
            return nexts[label], acc + match_sum(column, wide(tile, 3), values)

        _, acc = lax.fori_loop(
            0, heads[BPD + block], body, (heads[block], jnp.zeros((16, WIN), jnp.float32))
        )
        for comp in range(15):
            comps[comp, block : block + 1, :] = acc[comp : comp + 1]
    m_aa, m_ab, m_ac, m_bb, m_bc, m_cc, det = adjugate(*(comps[c] for c in range(9, 15)))

    def solve(r1, r2, r3):
        return (
            (m_aa * r1 + m_ab * r2 + m_ac * r3) / det,
            (m_ab * r1 + m_bb * r2 + m_bc * r3) / det,
            (m_ac * r1 + m_bc * r2 + m_cc * r3) / det,
        )

    right = [comps[c] for c in range(3)]
    image = [comps[3 + c] for c in range(3)]
    other = [comps[6 + c] for c in range(3)]
    residual = [r - alpha * w for r, w in zip(right, image)]
    start = solve(*right)
    middle = solve(*residual)
    direction = [m + beta * s for m, s in zip(middle, start)]
    final = solve(
        *(r - alpha_next * (v + beta * w) for r, v, w in zip(residual, other, image))
    )
    for comp in range(3):
        answer = alpha * start[comp] + alpha_next * direction[comp]
        solution_out[comp] = answer
        residual_out[comp] = final[comp]


class Mover:
    def __init__(self, source, buffer, sems, number):
        self.source, self.buffer = source, buffer
        self.send_sems, self.recv_sems, self.local_sems = sems
        self.number = number
        self.z, self.y, self.core, self.x = grid_place()
        self.started = []

    def send(self, number, source, target, peer):
        copy = pltpu.make_async_remote_copy(
            src_ref=source,
            dst_ref=target,
            send_sem=self.send_sems.at[self.number, number],
            recv_sem=self.recv_sems.at[self.number, number],
            device_id=peer,
            device_id_type=MESH,
        )
        copy.start()
        self.started.append(copy)
        return copy

    def start_first(self):
        z, y, core, x = self.z, self.y, self.core, self.x
        own = self.buffer.at[z, y]
        self.first = [
            self.send(d - 1, self.source, own, device_at(lax.rem(z + d, 8), y, core, x))
            for d in (4, 3, 5, 2, 6, 1, 7)
        ]
        self.keep = pltpu.make_async_copy(self.source, own, self.local_sems.at[self.number])
        self.keep.start()

    def start_second(self):
        self.keep.wait()
        for copy in self.first:
            copy.wait_recv()
        column = self.buffer.at[:, self.y]
        self.second = [
            self.send(
                6 + d, column, column,
                device_at(self.z, lax.rem(self.y + d, 4), self.core, self.x),
            )
            for d in (2, 1, 3)
        ]

    def arrive(self):
        for copy in self.second:
            copy.wait_recv()

    def finish(self):
        for copy in self.started:
            copy.wait_send()


class Group:
    def __init__(self, send_sems, recv_sems):
        self.send_sems, self.recv_sems = send_sems, recv_sems
        self.z, self.y, self.core, self.x = grid_place()
        self.me = self.x * 2 + self.core
        self.started = []

    def send(self, number, k, source, target, peer):
        copy = pltpu.make_async_remote_copy(
            src_ref=source,
            dst_ref=target,
            send_sem=self.send_sems.at[number, k],
            recv_sem=self.recv_sems.at[number, k],
            device_id=peer,
            device_id_type=MESH,
        )
        copy.start()
        self.started.append(copy)
        return copy

    def to_all(self, number, source_of, target):
        copies = []
        for k in (4, 5, 2, 3, 6, 7, 1):
            x = lax.rem(self.x + k // 2, 4)
            core = lax.rem(self.core + k % 2, 2)
            copies.append(
                self.send(
                    number, k, source_of(x * 2 + core), target, device_at(self.z, self.y, core, x)
                )
            )
        return copies

    def to_partner(self, number, source, target):
        return [
            self.send(number, 0, source, target, device_at(self.z, self.y, 1 - self.core, self.x))
        ]

    def along(self, number, ref):
        return [
            self.send(
                number, d, ref, ref, device_at(self.z, self.y, self.core, lax.rem(self.x + d, 4))
            )
            for d in (2, 1, 3)
        ]

    def finish(self):
        for copy in self.started:
            copy.wait_send()


def landed(copies):
    for copy in copies:
        copy.wait_recv()


def locate(label):
    return (
        lax.shift_right_logical(label, 2) & 7,
        label & 3,
        lax.shift_right_logical(label, 5) & 3,
    )


def joined(tile):
    return jnp.concatenate([tile[0:1], tile[1:2]], axis=1)


def split_product(rows, picked):
    count = len(rows)
    values = jnp.concatenate(rows, axis=0)
    high = values.astype(jnp.bfloat16).astype(jnp.float32)
    rest = values - high
    middle = rest.astype(jnp.bfloat16).astype(jnp.float32)
    low = rest - middle
    pad = -3 * count % 16
    stack = [high, middle, low]
    if pad:
        stack.append(jnp.zeros((pad, WIN), jnp.float32))
    left = jnp.concatenate(stack, axis=0).astype(jnp.bfloat16)
    out = lax.dot_general(left, picked, NT, preferred_element_type=jnp.float32)
    return [
        out[c : c + 1] + out[count + c : count + c + 1] + out[2 * count + c : 2 * count + c + 1]
        for c in range(count)
    ]


def matches(column, places):
    low = jnp.where(column == places[0:1], 1.0, 0.0)
    high = jnp.where(column == places[1:2], 1.0, 0.0)
    return jnp.concatenate([low, high], axis=1).astype(jnp.bfloat16)


def make_lists(metas, group_meta, list_a, list_b, live_a, live_b, lag_a, lag_b):
    z, y, core, x = grid_place()
    table = jnp.concatenate(
        [metas[...].reshape(32, HALF), jnp.zeros((HALF - 32, HALF), jnp.float32)], axis=0
    ).T

    def lane_row(rows):
        out = rows[0]
        for j in range(1, 4):
            out = out + pltpu.roll(rows[j], 32 * j, 1)
        return out

    blocks = lane_row([table[j : j + 1] for j in range(4)])
    lives = lane_row([table[4 + j : 5 + j] for j in range(4)])
    lags = lane_row([table[8:9]] * 4)
    label = lanes((1, HALF)).astype(jnp.float32)
    wanted = jnp.concatenate(
        [group_meta[t][:, j : j + 1] for t in range(8) for j in range(BLOCKS)], axis=0
    )
    base = ((z * 4 + y) * 2 * BPD).astype(jnp.float32)
    mask = jnp.concatenate(
        [
            jnp.where(wanted == blocks, 1.0, 0.0),
            jnp.where((blocks >= base) & (blocks < base + 2 * BPD), 1.0, 0.0),
            jnp.zeros((15, HALF), jnp.float32),
        ],
        axis=0,
    )
    ahead = jnp.where(rows_of((HALF, HALF)) < lanes((HALF, HALF)), 1.0, 0.0)
    within = jnp.dot(mask, ahead, precision=HIGHEST, preferred_element_type=jnp.float32)
    totals = jnp.broadcast_to(jnp.sum(mask, axis=1, keepdims=True), (48, HALF))
    row, col = rows_of((48, 48)), lanes((48, 48))
    above = jnp.where((row > col) & (row < TARGETS), 1.0, 0.0)
    rank = within + jnp.dot(above, totals, precision=HIGHEST, preferred_element_type=jnp.float32)
    rank = jnp.where(mask > 0.0, rank, -1.0)
    count_a = jnp.sum(totals[0:TARGETS, 0:1], axis=0, keepdims=True)
    count_b = totals[TARGETS : TARGETS + 1, 0:1]
    over = jnp.where((count_a > PAIRS) | (count_b > SLOTS), 1.0, 0.0)

    def spread(values):
        return jnp.broadcast_to(jnp.sum(values, axis=1, keepdims=True), values.shape)

    def store(code, list_ref, live_ref, lag_ref):
        list_ref[...] = spread(code).astype(jnp.int32)
        live_ref[...] = spread(jnp.where(code > 0.0, lives, 0.0))
        lag_ref[...] = spread(jnp.where(code > 0.0, lags, 0.0))

    slot = rows_of((32, HALF)).astype(jnp.float32)
    code = jnp.zeros((32, HALF), jnp.float32)
    for r in range(TARGETS):
        code += jnp.where(slot == rank[r : r + 1], label * 64.0 + (r + 1.0), 0.0)
    store(code, list_a, live_a, lag_a)
    slot = rows_of((24, HALF)).astype(jnp.float32)
    code = jnp.where(slot == rank[TARGETS : TARGETS + 1], label * 64.0 + (blocks - base + 1.0), 0.0)
    store(code, list_b, live_b, lag_b)
    return over


def placing(codes, count):
    row = (codes & 63) - 1
    here = jnp.where(row == lanes(codes.shape), 1.0, 0.0)
    size = codes.shape[0]
    square = jnp.concatenate([here, jnp.zeros((HALF - size, HALF), jnp.float32)], axis=0).T
    return square[0:count, 0:size]


def whole_kernel(
    valid, slots, hits, white, taps, stream, angle, offset,
    solution_out, residual_out, over_out,
    hold, taps_row, fixed, meta, base, message, row_two, message_two,
    all_fixed, all_base, all_meta, all_first, meta_two, all_second, meta_three,
    group_fixed, group_meta, sums_out, sums_in, base_out, base_in, next_out, next_in, last_row, group_row,
    columns, picked_a, picked_b, trig_a, trig_b, list_a, list_b, live_a, live_b, lag_a, lag_b,
    near_a, near_b, result_a, result_b, comps, factors, halo_rows,
    own_part, partner_part, x_part, owned, inverse,
    send_sems, recv_sems, local_sems, group_send, group_recv, halo_send, halo_recv, list_sems,
):
    z, y, core, x = grid_place()
    tm = x
    barrier = pltpu.get_barrier_semaphore()
    peers = [device_at(lax.rem(z + d, 8), y, core, x) for d in range(1, 8)] + [
        device_at(z, lax.rem(y + d, 4), core, x) for d in range(1, 4)
    ]
    for k in range(1, 8):
        peers.append(device_at(z, y, lax.rem(core + k % 2, 2), lax.rem(x + k // 2, 4)))
    for peer in peers:
        pl.semaphore_signal(barrier, inc=1, device_id=peer, device_id_type=MESH)

    place_of = offset[...].astype(jnp.float32)
    for block in range(BLOCKS):
        fixed[block, 0] = angle[2 * block : 2 * block + 2]
        fixed[block, 1] = place_of[2 * block : 2 * block + 2]
    taps_row[...] = jnp.zeros_like(taps_row)
    taps_row[:, : BAND + 1] = taps[...]
    lag_zero = jnp.sum(taps_row[...] * taps_row[...], axis=1, keepdims=True) + white[0, 0]
    remaining = valid[0, 0] - tm * SPAN
    lane = lanes((1, HALF))
    header = jnp.where(lane == 8, jnp.broadcast_to(lag_zero, (1, HALF)), 0.0)
    for block in range(BLOCKS):
        found = hits[0, slots[0, block]].astype(jnp.float32)
        count = jnp.clip(remaining - block * WIN, 0, WIN).astype(jnp.float32)
        header = jnp.where(lane == block, found, header)
        header = jnp.where(lane == 4 + block, count, header)
    meta[...] = header
    own_live = rows_of((8, HALF)) * HALF + lanes((8, HALF)) < remaining

    pl.semaphore_wait(barrier, len(peers))
    halos = [
        pltpu.make_async_remote_copy(
            src_ref=source,
            dst_ref=target,
            send_sem=halo_send.at[i],
            recv_sem=halo_recv.at[i],
            device_id=device_at(z, y, core, lax.rem(x + step, 4)),
            device_id_type=MESH,
        )
        for i, (source, target, step) in enumerate(
            (
                (stream.at[pl.ds(7, 1)], hold.at[0], 1),
                (stream.at[pl.ds(0, 1)], hold.at[1], 3),
            )
        )
    ]
    for copy in halos:
        copy.start()
    sems = (send_sems, recv_sems, local_sems)
    smalls = [
        Mover(meta, all_meta, sems, 0),
        Mover(row_two.at[0], meta_two, sems, 1),
        Mover(row_two.at[1], meta_three, sems, 2),
    ]
    relays = [
        Mover(fixed, all_fixed, sems, 3),
        Mover(message, all_first, sems, 4),
        Mover(message_two, all_second, sems, 5),
        Mover(base, all_base, sems, 6),
    ]
    group = Group(group_send, group_recv)
    me = group.me
    big, small, mid = relays[0], smalls[0], relays[3]
    small.start_first()
    big.start_first()
    places_in = group.to_all(0, lambda t: fixed, group_fixed.at[me])
    blocks_in = group.to_all(1, lambda t: meta, group_meta.at[me])
    group_fixed[me] = fixed[...]
    group_meta[me] = meta[...]

    spread = jnp.broadcast_to(taps_row[...], (WIN, WIN))
    shifted = pltpu.roll(spread, HALF, 1, stride=1, stride_axis=0)
    lag_row = lax.dot_general(
        spread[:8], shifted, NT, precision=HIGHEST, preferred_element_type=jnp.float32
    )
    lag_row = lag_row + jnp.where(lanes((8, WIN)) == HALF, white[0, 0], 0.0)
    band = pltpu.roll(
        jnp.broadcast_to(lag_row[0:1], (WIN, WIN)), WIN - HALF - BAND, 1, stride=1, stride_axis=0
    )[:, :HALF]
    landed(halos)
    extended = jnp.concatenate(
        [hold[0], stream[...], hold[1], jnp.zeros((6, HALF), jnp.float32)], axis=0
    )
    place = (rows_of((16, HALF)) - 1) * HALF + lanes((16, HALF))
    extended = jnp.where((place < remaining) & (place + tm * SPAN >= 0), extended, 0.0)
    base_own = jnp.where(own_live, band_filter(extended, band), 0.0)
    for block in range(BLOCKS):
        base[block] = base_own[2 * block : 2 * block + 2]
    mid.start_first()

    comps[...] = jnp.zeros_like(comps)
    halo_rows[...] = jnp.zeros_like(halo_rows)
    sums_out[...] = jnp.zeros_like(sums_out)
    base_out[...] = jnp.zeros_like(base_out)
    result_a[...] = jnp.zeros_like(result_a)
    result_b[...] = jnp.zeros_like(result_b)
    landed(places_in)
    landed(blocks_in)
    for block in range(BLOCKS):
        comps[9, block : block + 1, :] = joined(fixed[block, 0])
    right = group_fixed[jnp.minimum(x + 1, 3) * 2 + core, 0, 0]
    left = group_fixed[jnp.maximum(x - 1, 0) * 2 + core, BLOCKS - 1, 0]
    comps[9, 4:5, :] = jnp.concatenate([right[0:1], left[1:2]], axis=1)
    turn = 2.0 * comps[9]
    comps[9] = jnp.cos(turn)
    comps[10] = jnp.sin(turn)
    turned = jnp.concatenate(
        [group_fixed[t, block, 1] for t in range(8) for block in range(BLOCKS)]
        + [jnp.zeros((HALF // 2, HALF), jnp.float32)],
        axis=0,
    ).T

    def column(t, block, half):
        at = 8 * t + 2 * block + half
        return jnp.broadcast_to(turned[:, at : at + 1], (HALF, HALF))

    for t in range(8):
        for block in range(BLOCKS):
            for half in range(2):
                columns[BLOCKS * t + block, HALF * half : HALF * half + HALF, :] = column(
                    t, block, half
                )

    small.start_second()
    big.start_second()
    small.arrive()
    over = make_lists(all_meta, group_meta, near_a, near_b, live_a, live_b, lag_a, lag_b)
    copies = [
        pltpu.make_async_copy(near_a, list_a, list_sems.at[0]),
        pltpu.make_async_copy(near_b, list_b, list_sems.at[1]),
    ]
    for copy in copies:
        copy.start()
    mid.start_second()
    into_a = placing(near_a[...], TARGETS)
    into_b = placing(near_b[...], 2 * BPD)
    for copy in copies:
        copy.wait()
    big.arrive()

    wide_lane = lanes((1, WIN)).astype(jnp.float32)

    def doubled(row):
        return jnp.concatenate([row, row], axis=1)

    def six(p, where_at, trig, live, lag):
        turn = 2.0 * all_fixed[where_at + (0,)]
        co2, si2 = jnp.cos(turn), jnp.sin(turn)
        trig[p, 0:2, :] = co2
        trig[p, 2:4, :] = si2
        co, si = joined(co2), joined(si2)
        weight = jnp.where(
            wide_lane < doubled(live[pl.ds(p, 1), :]), doubled(lag[pl.ds(p, 1), :]), 0.0
        )
        return all_fixed[where_at + (1,)], co, si, weight_rows(weight, co, si)

    def three(p, where_at, trig, source):
        f = joined(source[where_at])
        return [f, f * joined(trig[p, 0:2, :]), f * joined(trig[p, 2:4, :])]

    def keep_rows(result, p, values):
        for c, value in enumerate(values):
            result[pl.ds(p, 1), WIN * c : WIN * c + WIN] = value

    def gathered_rows(into, result, count):
        return jnp.dot(
            into, result[:, 0 : WIN * count], precision=HIGHEST, preferred_element_type=jnp.float32
        )

    def pair_weights(p, carry):
        code = list_a[p, 0]
        places, _, _, values = six(
            p, locate(lax.shift_right_logical(code, 6)), trig_a, live_a, lag_a
        )
        picked = matches(columns[jnp.clip((code & 63) - 1, 0, TARGETS - 1)], places)
        picked_a[p] = picked
        keep_rows(result_a, p, split_product(values, picked))
        return carry

    def pair_next(source):
        def body(p, carry):
            code = list_a[p, 0]
            values = three(p, locate(lax.shift_right_logical(code, 6)), trig_a, source)
            keep_rows(result_a, p, split_product(values, picked_a[p]))
            return carry

        return body

    lax.fori_loop(0, PAIRS, pair_weights, 0, unroll=UNROLL)

    def hand_out(count, target):
        out = gathered_rows(into_a, result_a, count)
        empty = jnp.zeros((1, HALF), jnp.float32)
        for t in range(8):
            for c in range(count):
                at = WIN * c
                first = BLOCKS * t
                target[t, 5 * c : 5 * c + 4, :] = out[first : first + 4, at : at + WIN]
                right = out[first + 8 : first + 9, at : at + HALF] if t < 6 else empty
                left = out[first - 5 : first - 4, at + HALF : at + WIN] if t >= 2 else empty
                target[t, 5 * c + 4 : 5 * c + 5, :] = jnp.concatenate([right, left], axis=1)

    def sum_of(arrived):
        combined = arrived[0]
        for t in range(1, 8):
            combined = combined + arrived[t]
        return combined

    hand_out(6, sums_out)
    arriving = group.to_all(2, lambda t: sums_out.at[t], sums_in.at[me])
    sums_in[me] = sums_out[me]
    mid.arrive()
    lax.fori_loop(0, PAIRS, pair_next(all_base), 0, unroll=4)
    hand_out(3, base_out)
    arriving_base = group.to_all(11, lambda t: base_out.at[t], base_in.at[me])
    base_in[me] = base_out[me]
    landed(arriving)
    combined = sum_of(sums_in)
    for c in range(6):
        comps[3 + c, 0:5, :] = combined[5 * c : 5 * c + 5]
    m_aa, m_ab, m_ac, m_bb, m_bc, m_cc, det = adjugate(*(comps[c] for c in range(3, 9)))
    co, si = comps[9], comps[10]
    seg_row = rows_of((8, WIN))
    at = lanes((8, WIN))
    time = tm * SPAN + jnp.where(
        seg_row < BLOCKS, seg_row * WIN + at, jnp.where(at < HALF, SPAN + at, at - WIN)
    )
    inside = (seg_row < BLOCKS) | ((seg_row == BLOCKS) & ((at < BAND) | (at >= WIN - BAND)))
    live = (time >= 0) & (time < valid[0, 0]) & inside
    scale = jnp.where(live, 1.0, 0.0) / det
    factors[0] = (m_aa + m_ab * co + m_ac * si) * scale
    factors[1] = (m_ab + m_bb * co + m_bc * si) * scale
    factors[2] = (m_ac + m_bc * co + m_cc * si) * scale
    landed(arriving_base)
    combined = sum_of(base_in)
    for c in range(3):
        comps[c, 0:5, :] = combined[5 * c : 5 * c + 5]

    def change():
        return factors[0] * comps[0] + factors[1] * comps[1] + factors[2] * comps[2]

    def filter_signal(signal, out):
        halo_rows[0:1] = signal[4:5, HALF:]
        for block in range(BLOCKS):
            halo_rows[2 * block + 1 : 2 * block + 2] = signal[block : block + 1, :HALF]
            halo_rows[2 * block + 2 : 2 * block + 3] = signal[block : block + 1, HALF:]
        halo_rows[9:10] = signal[4:5, :HALF]
        result = jnp.where(own_live, band_filter(halo_rows[...], band), 0.0)
        for block in range(BLOCKS):
            out[block] = result[2 * block : 2 * block + 2]
        return result

    signal_first = change()
    filtered_first = filter_signal(signal_first, message)
    own = halo_rows[1:9]
    row_two[0] = (
        jnp.where(lane == 0, total(base_own * own), 0.0)
        + jnp.where(lane == 1, total(filtered_first * own), 0.0)
        + jnp.where(lane == 2, over, 0.0)
    )

    pixel = rows_of((WIN, HALF)).astype(jnp.float32)

    def owned_first(p, carry):
        code = list_b[p, 0]
        where_at = locate(lax.shift_right_logical(code, 6))
        places, co, si, values = six(p, where_at, trig_b, live_b, lag_b)
        f = joined(all_base[where_at])
        values = [f, f * co, f * si] + values
        picked = matches(pixel, places)
        picked_b[p] = picked
        keep_rows(result_b, p, split_product(values, picked))
        return carry

    def owned_next(source):
        def body(p, carry):
            code = list_b[p, 0]
            values = three(p, locate(lax.shift_right_logical(code, 6)), trig_b, source)
            keep_rows(result_b, p, split_product(values, picked_b[p]))
            return carry

        return body

    def owned_out(first, count, number):
        out = gathered_rows(into_b, result_b, count)
        for half in range(2):
            for c in range(count):
                own_part[half, first + c] = out[BPD * half : BPD * half + BPD, WIN * c : WIN * c + WIN]
        span = pl.ds(first, count)
        return group.to_partner(number, own_part.at[1 - core, span], partner_part.at[span])

    def owned_along(first, count, number, arriving):
        landed(arriving)
        span = pl.ds(first, count)
        x_part[x, span] = own_part[core, span] + partner_part[span]
        return group.along(number, x_part.at[x, span])

    def owned_sum(first, count):
        span = pl.ds(first, count)
        owned[span] = x_part[0, span] + x_part[1, span] + x_part[2, span] + x_part[3, span]

    def sums_of(metas):
        return jnp.sum(metas[...].reshape(32, 1, HALF), axis=0)

    big, small = relays[1], smalls[1]
    small.start_first()
    big.start_first()
    lax.fori_loop(0, SLOTS, owned_first, 0, unroll=2)
    small.start_second()
    big.start_second()
    waiting_first = owned_out(0, 9, 5)
    small.arrive()
    sums = sums_of(meta_two)
    big.arrive()

    lax.fori_loop(0, PAIRS, pair_next(all_first), 0, unroll=4)
    hand_out(3, next_out)
    for t in range(8):
        next_out[t, 15:16, :] = doubled(sums)
    arriving = group.to_all(3, lambda t: next_out.at[t], next_in.at[me])
    next_in[me] = next_out[me]
    landed(arriving)
    combined = sum_of(next_in)
    for c in range(3):
        comps[c, 0:5, :] = combined[5 * c : 5 * c + 5]
    sums = combined[15:16, :HALF]
    product, curve = sums[:, 0:1], sums[:, 1:2]
    over_out[...] = jnp.broadcast_to(sums[:, 2:3], (1, HALF))
    alpha = product / curve
    filtered_second = filter_signal(signal_first - alpha * change(), message_two)
    own = halo_rows[1:9]
    row_two[1] = (
        jnp.where(lane == 0, total((base_own - alpha * filtered_first) * own), 0.0)
        + jnp.where(lane == 1, total(filtered_second * own), 0.0)
        + jnp.where(lane == 2, total(filtered_first * own), 0.0)
    )

    big, small = relays[2], smalls[2]
    small.start_first()
    big.start_first()
    first_along = owned_along(0, 9, 6, waiting_first)
    lax.fori_loop(0, SLOTS, owned_next(all_first), 0, unroll=4)
    waiting_second = owned_out(9, 3, 7)
    small.start_second()
    big.start_second()
    second_along = owned_along(9, 3, 8, waiting_second)
    small.arrive()
    last_row[...] = sums_of(meta_three)
    rows_in = group.to_all(4, lambda t: last_row, group_row.at[me])
    group_row[me] = last_row[...]
    big.arrive()
    lax.fori_loop(0, SLOTS, owned_next(all_second), 0, unroll=4)
    waiting_third = owned_out(12, 3, 9)
    third_along = owned_along(12, 3, 10, waiting_third)

    landed(rows_in)
    sums = group_row[0]
    for t in range(1, 8):
        sums = sums + group_row[t]
    product_next = sums[:, 0:1]
    beta = product_next / product
    curve_next = sums[:, 1:2] + 2.0 * beta * sums[:, 2:3] + beta * beta * curve
    alpha_next = product_next / curve_next

    def solve(r1, r2, r3):
        i_aa, i_ab, i_ac, i_bb, i_bc, i_cc = (inverse[c] for c in range(6))
        return (
            i_aa * r1 + i_ab * r2 + i_ac * r3,
            i_ab * r1 + i_bb * r2 + i_bc * r3,
            i_ac * r1 + i_bc * r2 + i_cc * r3,
        )

    landed(first_along)
    owned_sum(0, 9)
    *minors, det = adjugate(*(owned[c] for c in range(3, 9)))
    scale = 1.0 / det
    for c, minor in enumerate(minors):
        inverse[c] = minor * scale
    landed(second_along)
    owned_sum(9, 3)
    start = solve(*(owned[c] for c in range(3)))
    for c in range(3):
        owned[c] = owned[c] - alpha * owned[9 + c]
    middle = solve(*(owned[c] for c in range(3)))
    for c in range(3):
        solution_out[c] = alpha * start[c] + alpha_next * (middle[c] + beta * start[c])
        owned[c] = owned[c] - alpha_next * beta * owned[9 + c]
    landed(third_along)
    owned_sum(12, 3)
    final = solve(*(owned[c] - alpha_next * owned[12 + c] for c in range(3)))
    for c in range(3):
        residual_out[c] = final[c]
    for mover in smalls + relays + [group]:
        mover.finish()
    for copy in halos:
        copy.wait_send()


def f32(*shape):
    return jax.ShapeDtypeStruct(shape, jnp.float32)


def gathered_shape(rows):
    return f32(2, 8, 4, 4, rows, HALF)


def gather_rows(values, part, number):
    rows, parts = pl.pallas_call(
        gather_kernel,
        out_shape=(gathered_shape(8), gathered_shape(1)),
        in_specs=[vmem] * 2,
        out_specs=(vmem,) * 2,
        scratch_shapes=EXCHANGE_SCRATCH,
        compiler_params=pltpu.CompilerParams(collective_id=number, has_side_effects=True),
        name="gather",
    )(values, part)
    return rows.reshape(LABELS, 2, HALF), parts.reshape(DEVICES, HALF)


def any_lengths(
    time_streams, pol_angle, offsets, block_slots, hit_ids, valid_counts, filter_taps, white_weight
):
    valid = valid_counts.reshape(1)
    message, metas, base, band = pl.pallas_call(
        prepare_kernel,
        out_shape=(gathered_shape(32), gathered_shape(1), f32(8, HALF), f32(WIN, HALF)),
        in_specs=[smem] * 4 + [vmem] * 4,
        out_specs=(vmem,) * 4,
        scratch_shapes=[
            pltpu.VMEM((2, 1, HALF), jnp.float32),
            pltpu.VMEM((1, WIN), jnp.float32),
            pltpu.VMEM((32, HALF), jnp.float32),
            pltpu.VMEM((1, HALF), jnp.float32),
        ]
        + EXCHANGE_SCRATCH
        + [pltpu.SemaphoreType.DMA((2,)), pltpu.SemaphoreType.DMA((2,))],
        compiler_params=pltpu.CompilerParams(collective_id=0, has_side_effects=True),
        name="prepare",
    )(
        valid, block_slots.reshape(BLOCKS), hit_ids.reshape(-1), white_weight.reshape(1),
        filter_taps.reshape(1, BAND + 1), time_streams.reshape(8, HALF), pol_angle.reshape(8, HALF),
        offsets.reshape(8, HALF),
    )
    gathered = message.reshape(LABELS, 8, HALF)
    metas = metas.reshape(DEVICES, HALF)

    blocks = metas[:, 0:4].reshape(LABELS)
    lives = metas[:, 4:8].reshape(LABELS).astype(jnp.int32)
    lag_zero = metas[:, 8]
    order = jnp.arange(LABELS, dtype=jnp.int32)
    same = blocks[:, None] == blocks[None, :]
    ahead = (order[None, :] - order[:, None] - 1) % LABELS
    nexts = (order + 1 + jnp.min(jnp.where(same, ahead, LABELS), axis=1)) % LABELS
    counts = jnp.sum(same, axis=1, dtype=jnp.int32)
    owned = (lax.axis_index("det") * BPD + jnp.arange(BPD, dtype=jnp.int32)).astype(jnp.float32)
    mine = owned[:, None] == blocks[None, :]
    heads = jnp.concatenate(
        [
            jnp.min(jnp.where(mine, order[None, :], LABELS - 1), axis=1),
            jnp.sum(mine, axis=1, dtype=jnp.int32),
        ]
    )

    first, part_one, factors, signal = pl.pallas_call(
        first_kernel,
        out_shape=(f32(8, HALF), f32(1, HALF), f32(3, 8, WIN), f32(8, WIN)),
        in_specs=[smem] * 5 + [vmem] * 3,
        out_specs=(vmem,) * 4,
        scratch_shapes=[
            pltpu.VMEM((12, 8, WIN), jnp.float32),
            pltpu.VMEM((16, HALF), jnp.float32),
        ],
        name="first",
    )(valid, nexts, counts, lives, lag_zero, gathered, base, band)
    second, parts_two = gather_rows(first, part_one, 1)
    other, part_two = pl.pallas_call(
        second_kernel,
        out_shape=(f32(8, HALF), f32(1, HALF)),
        in_specs=[smem] * 3 + [vmem] * 8,
        out_specs=(vmem,) * 2,
        scratch_shapes=[
            pltpu.VMEM((3, 8, WIN), jnp.float32),
            pltpu.VMEM((16, HALF), jnp.float32),
        ],
        name="second",
    )(valid, nexts, counts, gathered, second, parts_two, base, first, band, factors, signal)
    third, parts_three = gather_rows(other, part_two, 2)
    answers = pl.pallas_call(
        last_kernel,
        out_shape=(f32(3, BPD, WIN), f32(3, BPD, WIN)),
        in_specs=[smem] * 4 + [vmem] * 5,
        out_specs=(vmem,) * 2,
        scratch_shapes=[pltpu.VMEM((15, BPD, WIN), jnp.float32)],
        name="last",
    )(heads, nexts, lives, lag_zero, gathered, second, third, parts_two, parts_three)
    return tuple(answers)


def wide_buffer(*shape):
    return pltpu.VMEM((8, 4) + shape, jnp.float32)


def room(*shape):
    return pltpu.VMEM(shape, jnp.float32)


def per_device(*args):
    (
        time_streams, pol_angle, offsets, block_slots, hit_ids, valid_counts, filter_taps,
        white_weight,
    ) = args
    fast = pl.pallas_call(
        whole_kernel,
        out_shape=(f32(3, BPD, WIN), f32(3, BPD, WIN), f32(1, HALF)),
        in_specs=[smem] * 4 + [vmem] * 4,
        out_specs=(vmem,) * 3,
        scratch_shapes=[
            room(2, 1, HALF), room(1, WIN), room(BLOCKS, 2, 2, HALF), room(1, HALF),
            room(BLOCKS, 2, HALF), room(BLOCKS, 2, HALF), room(2, 1, HALF), room(BLOCKS, 2, HALF),
            wide_buffer(BLOCKS, 2, 2, HALF), wide_buffer(BLOCKS, 2, HALF), wide_buffer(1, HALF),
            wide_buffer(BLOCKS, 2, HALF), wide_buffer(1, HALF), wide_buffer(BLOCKS, 2, HALF),
            wide_buffer(1, HALF),
            room(8, BLOCKS, 2, 2, HALF), room(8, 1, HALF), room(8, 32, WIN), room(8, 32, WIN),
            room(8, 16, WIN), room(8, 16, WIN),
            room(8, 16, WIN), room(8, 16, WIN), room(1, HALF), room(8, 1, HALF),
            room(TARGETS, WIN, HALF),
            pltpu.VMEM((PAIRS, WIN, WIN), jnp.bfloat16),
            pltpu.VMEM((SLOTS, WIN, WIN), jnp.bfloat16),
            room(PAIRS, 4, HALF), room(SLOTS, 4, HALF),
            pltpu.SMEM((32, HALF), jnp.int32), pltpu.SMEM((24, HALF), jnp.int32),
            room(32, HALF), room(24, HALF), room(32, HALF), room(24, HALF),
            pltpu.VMEM((32, HALF), jnp.int32), pltpu.VMEM((24, HALF), jnp.int32),
            room(32, 9 * WIN), room(24, 9 * WIN),
            room(11, 8, WIN), room(3, 8, WIN), room(16, HALF),
            room(2, 15, BPD, WIN), room(15, BPD, WIN), room(4, 15, BPD, WIN), room(15, BPD, WIN),
            room(6, BPD, WIN),
            pltpu.SemaphoreType.DMA((7, 10)), pltpu.SemaphoreType.DMA((7, 10)),
            pltpu.SemaphoreType.DMA((7,)), pltpu.SemaphoreType.DMA((12, 8)),
            pltpu.SemaphoreType.DMA((12, 8)), pltpu.SemaphoreType.DMA((2,)),
            pltpu.SemaphoreType.DMA((2,)), pltpu.SemaphoreType.DMA((2,)),
        ],
        compiler_params=pltpu.CompilerParams(collective_id=3, has_side_effects=True),
        name="whole",
    )(
        valid_counts, block_slots.reshape(1, BLOCKS), hit_ids, white_weight,
        filter_taps.reshape(1, BAND + 1), time_streams.reshape(8, HALF),
        pol_angle.reshape(8, HALF), offsets.reshape(8, HALF),
    )
    answers = lax.cond(
        fast[2][0, 0] > 0.0, lambda f, *a: any_lengths(*a), lambda f, *a: f, fast[:2], *args
    )
    return tuple(jnp.transpose(answer, (1, 0, 2)) for answer in answers)


def solution(mesh):
    in_specs = (
        P("det", None, "tm"),
        P("det", None, "tm"),
        P("det", None, "tm"),
        P("det", None, "tm"),
        P("det", None),
        P("det", None),
        P("det", None, None),
        P("det", None),
    )
    out_specs = (P("det", None, None), P("det", None, None))
    return jax.shard_map(
        per_device, mesh=mesh, in_specs=in_specs, out_specs=out_specs, check_vma=False
    )
```

```python
import functools

import jax
import jax.numpy as jnp
from jax import lax
from jax.experimental import pallas as pl
from jax.experimental.pallas import tpu as pltpu
from jax.sharding import PartitionSpec as P

WIN = 256
BAND = 64
BPD = 16
HALF = 128
SPAN = 1024
BLOCKS = 4
DEVICES = 256
PAIRS = 24
TARGETS = 32
UNROLL = 4
SLOTS = 20
LABELS = DEVICES * BLOCKS

HIGHEST = lax.Precision.HIGHEST
NT = (((1,), (1,)), ((), ()))
MESH = pl.DeviceIdType.MESH

vmem = pl.BlockSpec(memory_space=pltpu.VMEM)
smem = pl.BlockSpec(memory_space=pltpu.SMEM)


def lanes(shape):
    return lax.broadcasted_iota(jnp.int32, shape, len(shape) - 1)


def rows_of(shape):
    return lax.broadcasted_iota(jnp.int32, shape, 0)


def band_filter(extended, band):
    turned = pltpu.roll(extended, HALF // 2, 1)
    keep = lanes((8, HALF)) < HALF // 2
    first = jnp.where(keep, turned[0:8], turned[1:9])
    second = jnp.where(keep, turned[1:9], turned[2:10])
    window = jnp.concatenate([first, second], axis=1)
    return jnp.dot(window, band, precision=HIGHEST, preferred_element_type=jnp.float32)


def grid_place():
    det = lax.axis_index("det")
    x = lax.axis_index("tm")
    return lax.div(det, 8), lax.rem(lax.div(det, 2), 4), lax.rem(det, 2), x


def device_at(z, y, core, x):
    return {"det": (z * 4 + y) * 2 + core, "tm": x}


def slot_of(z, y, core, x):
    major = y + core * (x - y)
    minor = x + core * (y - x)
    return ((core * 8 + z) * 4 + major) * 4 + minor


def meet():
    z, y, core, x = grid_place()
    barrier = pltpu.get_barrier_semaphore()
    peers = (
        [device_at(lax.rem(z + d, 8), y, core, x) for d in range(1, 8)]
        + [device_at(z, lax.rem(y + d, 4), core, x) for d in range(1, 4)]
        + [device_at(z, y, core, lax.rem(x + d, 4)) for d in range(1, 4)]
        + [device_at(z, y, 1 - core, x)]
    )
    for peer in peers:
        pl.semaphore_signal(barrier, inc=1, device_id=peer, device_id_type=MESH)
    pl.semaphore_wait(barrier, len(peers))


def exchange(sources, buffers, send_sems, recv_sems, local_sems):
    z, y, core, x = grid_place()
    a = y + core * (x - y)
    b = x + core * (y - x)

    def major_peer(step):
        return device_at(
            z,
            y + (1 - core) * (lax.rem(y + step, 4) - y),
            core,
            x + core * (lax.rem(x + step, 4) - x),
        )

    def minor_peer(step):
        return device_at(
            z,
            y + core * (lax.rem(y + step, 4) - y),
            core,
            x + (1 - core) * (lax.rem(x + step, 4) - x),
        )

    arrays = range(len(sources))

    def send(number, source_of, target_of, peer):
        copies = []
        for i in arrays:
            copy = pltpu.make_async_remote_copy(
                src_ref=source_of(i),
                dst_ref=target_of(i),
                send_sem=send_sems.at[i, number],
                recv_sem=recv_sems.at[i, number],
                device_id=peer,
                device_id_type=MESH,
            )
            copy.start()
            copies.append(copy)
        return copies

    def landed(copies):
        for copy in copies:
            copy.wait_recv()

    started = []
    keep = [
        pltpu.make_async_copy(sources[i], buffers[i].at[core, z, a, b], local_sems.at[i])
        for i in arrays
    ]
    first = [
        send(
            d - 1,
            lambda i: sources[i],
            lambda i: buffers[i].at[core, z, a, b],
            device_at(lax.rem(z + d, 8), y, core, x),
        )
        for d in (4, 3, 5, 2, 6, 1, 7)
    ]
    for copy in keep:
        copy.start()
    for copy in keep:
        copy.wait()
    for copies in first:
        landed(copies)
    started += first

    def column(i):
        return buffers[i].at[core, :, a, b]

    second = [send(6 + d, column, column, major_peer(d)) for d in (2, 1, 3)]
    for copies in second:
        landed(copies)
    started += second

    def part(number, half):
        depth = pl.ds(4 * half, 4)
        return lambda i: buffers[i].at[core, depth, :, number]

    def whole(number):
        return lambda i: buffers[i].at[core, :, :, number]

    after = minor_peer(1)
    before = minor_peer(3)
    partner = device_at(z, y, 1 - core, x)
    left = lax.rem(b + 3, 4)
    right = lax.rem(b + 1, 4)
    far = lax.rem(b + 2, 4)
    up = [send(10, part(b, 0), part(b, 0), after)]
    down = [send(12, part(b, 1), part(b, 1), before)]
    up.append(send(11, part(b, 1), part(b, 1), after))
    down.append(send(13, part(b, 0), part(b, 0), before))
    swaps = [send(16, whole(b), whole(b), partner)]
    landed(up[0])
    up.append(send(14, part(left, 0), part(left, 0), after))
    landed(down[0])
    down.append(send(15, part(right, 1), part(right, 1), before))
    landed(up[1])
    swaps.append(send(17, whole(left), whole(left), partner))
    landed(down[1])
    swaps.append(send(18, whole(right), whole(right), partner))
    landed(up[2])
    landed(down[2])
    swaps.append(send(19, whole(far), whole(far), partner))
    for copies in swaps:
        landed(copies)
    started += up + down + swaps
    for copies in started:
        for copy in copies:
            copy.wait_send()


EXCHANGE_SCRATCH = [
    pltpu.SemaphoreType.DMA((2, 20)),
    pltpu.SemaphoreType.DMA((2, 20)),
    pltpu.SemaphoreType.DMA((2,)),
]


def gather_kernel(values, meta, values_out, meta_out, send_sems, recv_sems, local_sems):
    meet()
    exchange([values, meta], [values_out, meta_out], send_sems, recv_sems, local_sems)


def prepare_kernel(
    valid, slots, hits, white, taps, stream, angle, offset,
    message_out, meta_out, base_out, band,
    hold, taps_row, message, meta, send_sems, recv_sems, local_sems, halo_send, halo_recv,
):
    meet()
    z, y, core, x = grid_place()
    tm = x
    halos = [
        pltpu.make_async_remote_copy(
            src_ref=stream.at[pl.ds(7, 1)],
            dst_ref=hold.at[0],
            send_sem=halo_send.at[0],
            recv_sem=halo_recv.at[0],
            device_id=device_at(z, y, core, lax.rem(x + 1, 4)),
            device_id_type=MESH,
        ),
        pltpu.make_async_remote_copy(
            src_ref=stream.at[pl.ds(0, 1)],
            dst_ref=hold.at[1],
            send_sem=halo_send.at[1],
            recv_sem=halo_recv.at[1],
            device_id=device_at(z, y, core, lax.rem(x + 3, 4)),
            device_id_type=MESH,
        ),
    ]
    for copy in halos:
        copy.start()
    cosine = jnp.cos(2.0 * angle[...])
    sine = jnp.sin(2.0 * angle[...])
    place_of = offset[...].astype(jnp.float32)
    for block in range(BLOCKS):
        for half in range(2):
            row = 2 * block + half
            for part, values in enumerate((cosine, sine, place_of)):
                at = 8 * block + 4 * half + part + 1
                message[at : at + 1, :] = values[row : row + 1]
    taps_row[...] = jnp.zeros_like(taps_row)
    taps_row[:, : BAND + 1] = taps[...]
    spread = jnp.broadcast_to(taps_row[...], (WIN, WIN))
    shifted = pltpu.roll(spread, HALF, 1, stride=1, stride_axis=0)
    lag_row = lax.dot_general(
        spread[:8], shifted, NT, precision=HIGHEST, preferred_element_type=jnp.float32
    )
    lag_row = lag_row + jnp.where(lanes((8, WIN)) == HALF, white[0], 0.0)
    table = pltpu.roll(
        jnp.broadcast_to(lag_row[0:1], (WIN, WIN)), WIN - HALF - BAND, 1, stride=1, stride_axis=0
    )
    band[...] = table[:, :HALF]
    lag_zero = lag_row[0:1, HALF : HALF + 1]

    remaining = valid[0] - tm * SPAN
    lane = lanes((1, HALF))
    header = jnp.where(lane == 8, jnp.broadcast_to(lag_zero, (1, HALF)), 0.0)
    for block in range(BLOCKS):
        found = hits[slots[block]].astype(jnp.float32)
        count = jnp.clip(remaining - block * WIN, 0, WIN).astype(jnp.float32)
        header = jnp.where(lane == block, found, header)
        header = jnp.where(lane == 4 + block, count, header)
    meta[...] = header

    for copy in halos:
        copy.wait_recv()
    extended = jnp.concatenate(
        [hold[0], stream[...], hold[1], jnp.zeros((6, HALF), jnp.float32)], axis=0
    )
    place = (rows_of((16, HALF)) - 1) * HALF + lanes((16, HALF))
    extended = jnp.where((place < remaining) & (place + tm * SPAN >= 0), extended, 0.0)
    own_live = rows_of((8, HALF)) * HALF + lanes((8, HALF)) < remaining
    filtered = jnp.where(own_live, band_filter(extended, table[:, :HALF]), 0.0)
    for block in range(BLOCKS):
        for half in range(2):
            row = 2 * block + half
            at = 8 * block + 4 * half
            message[at : at + 1, :] = filtered[row : row + 1]
    base_out[...] = filtered
    exchange([message, meta], [message_out, meta_out], send_sems, recv_sems, local_sems)
    for copy in halos:
        copy.wait_send()


def split_rows(values):
    high = values.astype(jnp.bfloat16)
    rest = values - high.astype(jnp.float32)
    middle = rest.astype(jnp.bfloat16)
    low = (rest - middle.astype(jnp.float32)).astype(jnp.bfloat16)
    return jnp.concatenate([high, middle, low], axis=0)


def wide(tile, row):
    return jnp.concatenate([tile[row : row + 1], tile[row + 4 : row + 5]], axis=1)


def match_sum(column, places, values):
    count = values.shape[0]
    picked = jnp.where(column == places, 1.0, 0.0).astype(jnp.bfloat16)
    out = lax.dot_general(split_rows(values), picked, NT, preferred_element_type=jnp.float32)
    return out[:count] + out[count : 2 * count] + out[2 * count :]


def weight_rows(weight, cosine, sine):
    first = weight * cosine
    second = weight * sine
    return [weight, first, second, first * cosine, first * sine, second * sine]


def own_labels():
    z, y, core, x = grid_place()
    own = slot_of(z, y, core, x) * BLOCKS
    before = slot_of(z, y, core, jnp.maximum(x - 1, 0)) * BLOCKS + BLOCKS - 1
    after = slot_of(z, y, core, jnp.minimum(x + 1, 3)) * BLOCKS
    usable = [jnp.minimum(x, 1)] + [1] * BLOCKS + [jnp.minimum(3 - x, 1)]
    return [before] + [own + block for block in range(BLOCKS)] + [after], usable


def own_columns(labels, gathered):
    rows = []
    for seg in range(6):
        tile = gathered[labels[seg]]
        rows += [tile[3:4], tile[7:8]]
    rows.append(jnp.zeros((HALF - 12, HALF), jnp.float32))
    turned = jnp.concatenate(rows, axis=0).T
    return [
        jnp.concatenate([turned[:, 2 * s : 2 * s + 1], turned[:, 2 * s + 1 : 2 * s + 2]], axis=0)
        for s in range(6)
    ]


def adjugate(w1, w2, w3, w4, w5, w6):
    aa = 1.0 + w1
    bb = 1.0 + w4
    cc = 1.0 + w6
    m_aa = bb * cc - w5 * w5
    m_ab = w3 * w5 - w2 * cc
    m_ac = w2 * w5 - w3 * bb
    m_bb = aa * cc - w3 * w3
    m_bc = w2 * w3 - aa * w5
    m_cc = aa * bb - w2 * w2
    det = aa * m_aa + w2 * m_ab + w3 * m_ac
    return m_aa, m_ab, m_ac, m_bb, m_bc, m_cc, det


def rows_to_hold(signal, hold):
    hold[0:1] = signal[0:1, HALF:]
    for seg in range(1, 5):
        hold[2 * seg - 1 : 2 * seg] = signal[seg : seg + 1, :HALF]
        hold[2 * seg : 2 * seg + 1] = signal[seg : seg + 1, HALF:]
    hold[9:10] = signal[5:6, :HALF]


def total(values):
    return jnp.sum(jnp.sum(values, axis=1, keepdims=True), axis=0, keepdims=True)


def own_live_of(info):
    remaining = info[0] - lax.axis_index("tm") * SPAN
    return rows_of((8, HALF)) * HALF + lanes((8, HALF)) < remaining


def first_kernel(
    info, nexts, counts, lives, lag_zero, gathered, base, band,
    filtered_out, part_out, factors, signal_out, comps, hold,
):
    labels, flags = own_labels()
    columns = own_columns(labels, gathered)
    lane = lanes((1, WIN))
    comps[...] = jnp.zeros_like(comps)
    for seg in range(6):
        column = columns[seg]
        usable = flags[seg]

        def body(_, carry, column=column):
            label, acc = carry
            tile = gathered[label]
            f = wide(tile, 0)
            co = wide(tile, 1)
            si = wide(tile, 2)
            weight = jnp.where(lane < lives[label], lag_zero[label // BLOCKS], 0.0)
            values = jnp.concatenate(
                [f, f * co, f * si] + weight_rows(weight, co, si)
                + [jnp.zeros((7, WIN), jnp.float32)], axis=0,
            )
            return nexts[label], acc + match_sum(column, wide(tile, 3), values)

        start = labels[seg]
        _, acc = lax.fori_loop(
            0, counts[start] * usable, body, (start, jnp.zeros((16, WIN), jnp.float32))
        )
        for comp in range(9):
            comps[comp, seg : seg + 1, :] = acc[comp : comp + 1]
        tile = gathered[start]
        comps[9, seg : seg + 1, :] = wide(tile, 1)
        comps[10, seg : seg + 1, :] = wide(tile, 2)
        comps[11, seg : seg + 1, :] = jnp.where(lane < lives[start] * usable, 1.0, 0.0)
    m_aa, m_ab, m_ac, m_bb, m_bc, m_cc, det = adjugate(*(comps[c] for c in range(3, 9)))
    co, si, live = comps[9], comps[10], comps[11]
    scale = live / det
    q1 = (m_aa + m_ab * co + m_ac * si) * scale
    q2 = (m_ab + m_bb * co + m_bc * si) * scale
    q3 = (m_ac + m_bc * co + m_cc * si) * scale
    factors[0] = q1
    factors[1] = q2
    factors[2] = q3
    signal = q1 * comps[0] + q2 * comps[1] + q3 * comps[2]
    signal_out[...] = signal
    hold[...] = jnp.zeros_like(hold)
    rows_to_hold(signal, hold)
    filtered = jnp.where(own_live_of(info), band_filter(hold[...], band[...]), 0.0)
    filtered_out[...] = filtered
    own = hold[1:9]
    lane = lanes((1, HALF))
    part_out[...] = jnp.where(lane == 0, total(base[...] * own), 0.0) + jnp.where(
        lane == 1, total(filtered * own), 0.0
    )


def second_kernel(
    info, nexts, counts, gathered, second, parts, base, own_first, band, factors, signal_in,
    filtered_out, part_out, comps, hold,
):
    sums = jnp.sum(parts[...], axis=0, keepdims=True)
    alpha = sums[:, 0:1] / sums[:, 1:2]
    labels, flags = own_labels()
    columns = own_columns(labels, gathered)
    comps[...] = jnp.zeros_like(comps)
    for seg in range(6):
        column = columns[seg]

        def body(_, carry, column=column):
            label, acc = carry
            tile = gathered[label]
            pair = second[label]
            f = jnp.concatenate([pair[0:1], pair[1:2]], axis=1)
            values = jnp.concatenate(
                [f, f * wide(tile, 1), f * wide(tile, 2), jnp.zeros((13, WIN), jnp.float32)], axis=0
            )
            return nexts[label], acc + match_sum(column, wide(tile, 3), values)

        start = labels[seg]
        _, acc = lax.fori_loop(
            0, counts[start] * flags[seg], body, (start, jnp.zeros((16, WIN), jnp.float32))
        )
        for comp in range(3):
            comps[comp, seg : seg + 1, :] = acc[comp : comp + 1]
    change = factors[0] * comps[0] + factors[1] * comps[1] + factors[2] * comps[2]
    signal = signal_in[...] - alpha * change
    hold[...] = jnp.zeros_like(hold)
    rows_to_hold(signal, hold)
    filtered = jnp.where(own_live_of(info), band_filter(hold[...], band[...]), 0.0)
    filtered_out[...] = filtered
    own = hold[1:9]
    first = own_first[...]
    lane = lanes((1, HALF))
    part_out[...] = (
        jnp.where(lane == 0, total((base[...] - alpha * first) * own), 0.0)
        + jnp.where(lane == 1, total(filtered * own), 0.0)
        + jnp.where(lane == 2, total(first * own), 0.0)
    )


def last_kernel(
    heads, nexts, lives, lag_zero, gathered, second, third, parts_two, parts_three,
    solution_out, residual_out, comps,
):
    sums = jnp.sum(parts_two[...], axis=0, keepdims=True)
    product, curve = sums[:, 0:1], sums[:, 1:2]
    alpha = product / curve
    sums = jnp.sum(parts_three[...], axis=0, keepdims=True)
    product_next = sums[:, 0:1]
    beta = product_next / product
    curve_next = sums[:, 1:2] + 2.0 * beta * sums[:, 2:3] + beta * beta * curve
    alpha_next = product_next / curve_next
    column = rows_of((WIN, 1)).astype(jnp.float32)
    lane = lanes((1, WIN))
    for block in range(BPD):

        def body(_, carry):
            label, acc = carry
            tile = gathered[label]
            co = wide(tile, 1)
            si = wide(tile, 2)
            pair = second[label]
            trio = third[label]
            rows = []
            for f in (
                wide(tile, 0),
                jnp.concatenate([pair[0:1], pair[1:2]], axis=1),
                jnp.concatenate([trio[0:1], trio[1:2]], axis=1),
            ):
                rows += [f, f * co, f * si]
            weight = jnp.where(lane < lives[label], lag_zero[label // BLOCKS], 0.0)
            values = jnp.concatenate(
                rows + weight_rows(weight, co, si) + [jnp.zeros((1, WIN), jnp.float32)], axis=0
            )
            return nexts[label], acc + match_sum(column, wide(tile, 3), values)

        _, acc = lax.fori_loop(
            0, heads[BPD + block], body, (heads[block], jnp.zeros((16, WIN), jnp.float32))
        )
        for comp in range(15):
            comps[comp, block : block + 1, :] = acc[comp : comp + 1]
    m_aa, m_ab, m_ac, m_bb, m_bc, m_cc, det = adjugate(*(comps[c] for c in range(9, 15)))

    def solve(r1, r2, r3):
        return (
            (m_aa * r1 + m_ab * r2 + m_ac * r3) / det,
            (m_ab * r1 + m_bb * r2 + m_bc * r3) / det,
            (m_ac * r1 + m_bc * r2 + m_cc * r3) / det,
        )

    right = [comps[c] for c in range(3)]
    image = [comps[3 + c] for c in range(3)]
    other = [comps[6 + c] for c in range(3)]
    residual = [r - alpha * w for r, w in zip(right, image)]
    start = solve(*right)
    middle = solve(*residual)
    direction = [m + beta * s for m, s in zip(middle, start)]
    final = solve(
        *(r - alpha_next * (v + beta * w) for r, v, w in zip(residual, other, image))
    )
    for comp in range(3):
        answer = alpha * start[comp] + alpha_next * direction[comp]
        solution_out[comp] = answer
        residual_out[comp] = final[comp]


class Mover:
    def __init__(self, source, buffer, sems, number):
        self.source, self.buffer = source, buffer
        self.send_sems, self.recv_sems, self.local_sems = sems
        self.number = number
        self.z, self.y, self.core, self.x = grid_place()
        self.started = []

    def send(self, number, source, target, peer):
        copy = pltpu.make_async_remote_copy(
            src_ref=source,
            dst_ref=target,
            send_sem=self.send_sems.at[self.number, number],
            recv_sem=self.recv_sems.at[self.number, number],
            device_id=peer,
            device_id_type=MESH,
        )
        copy.start()
        self.started.append(copy)
        return copy

    def start_first(self):
        z, y, core, x = self.z, self.y, self.core, self.x
        own = self.buffer.at[z, y]
        self.first = [
            self.send(d - 1, self.source, own, device_at(lax.rem(z + d, 8), y, core, x))
            for d in (4, 3, 5, 2, 6, 1, 7)
        ]
        self.keep = pltpu.make_async_copy(self.source, own, self.local_sems.at[self.number])
        self.keep.start()

    def start_second(self):
        self.keep.wait()
        for copy in self.first:
            copy.wait_recv()
        column = self.buffer.at[:, self.y]
        self.second = [
            self.send(
                6 + d, column, column,
                device_at(self.z, lax.rem(self.y + d, 4), self.core, self.x),
            )
            for d in (2, 1, 3)
        ]

    def arrive(self):
        for copy in self.second:
            copy.wait_recv()

    def finish(self):
        for copy in self.started:
            copy.wait_send()


class Group:
    def __init__(self, send_sems, recv_sems):
        self.send_sems, self.recv_sems = send_sems, recv_sems
        self.z, self.y, self.core, self.x = grid_place()
        self.me = self.x * 2 + self.core
        self.started = []

    def send(self, number, k, source, target, peer):
        copy = pltpu.make_async_remote_copy(
            src_ref=source,
            dst_ref=target,
            send_sem=self.send_sems.at[number, k],
            recv_sem=self.recv_sems.at[number, k],
            device_id=peer,
            device_id_type=MESH,
        )
        copy.start()
        self.started.append(copy)
        return copy

    def to_all(self, number, source_of, target):
        copies = []
        for k in (4, 5, 2, 3, 6, 7, 1):
            x = lax.rem(self.x + k // 2, 4)
            core = lax.rem(self.core + k % 2, 2)
            copies.append(
                self.send(
                    number, k, source_of(x * 2 + core), target, device_at(self.z, self.y, core, x)
                )
            )
        return copies

    def to_partner(self, number, source, target):
        return [
            self.send(number, 0, source, target, device_at(self.z, self.y, 1 - self.core, self.x))
        ]

    def along(self, number, ref):
        return [
            self.send(
                number, d, ref, ref, device_at(self.z, self.y, self.core, lax.rem(self.x + d, 4))
            )
            for d in (2, 1, 3)
        ]

    def finish(self):
        for copy in self.started:
            copy.wait_send()


def landed(copies):
    for copy in copies:
        copy.wait_recv()


def locate(label):
    return (
        lax.shift_right_logical(label, 2) & 7,
        label & 3,
        lax.shift_right_logical(label, 5) & 3,
    )


def joined(tile):
    return jnp.concatenate([tile[0:1], tile[1:2]], axis=1)


def split_product(rows, picked):
    count = len(rows)
    values = jnp.concatenate(rows, axis=0)
    high = values.astype(jnp.bfloat16).astype(jnp.float32)
    rest = values - high
    middle = rest.astype(jnp.bfloat16).astype(jnp.float32)
    low = rest - middle
    pad = -3 * count % 16
    stack = [high, middle, low]
    if pad:
        stack.append(jnp.zeros((pad, WIN), jnp.float32))
    left = jnp.concatenate(stack, axis=0).astype(jnp.bfloat16)
    out = lax.dot_general(left, picked, NT, preferred_element_type=jnp.float32)
    return [
        out[c : c + 1] + out[count + c : count + c + 1] + out[2 * count + c : 2 * count + c + 1]
        for c in range(count)
    ]


def matches(column, places):
    low = jnp.where(column == places[0:1], 1.0, 0.0)
    high = jnp.where(column == places[1:2], 1.0, 0.0)
    return jnp.concatenate([low, high], axis=1).astype(jnp.bfloat16)


def make_lists(metas, group_meta, list_a, list_b, live_a, live_b, lag_a, lag_b):
    z, y, core, x = grid_place()
    table = jnp.concatenate(
        [metas[...].reshape(32, HALF), jnp.zeros((HALF - 32, HALF), jnp.float32)], axis=0
    ).T

    def lane_row(rows):
        out = rows[0]
        for j in range(1, 4):
            out = out + pltpu.roll(rows[j], 32 * j, 1)
        return out

    blocks = lane_row([table[j : j + 1] for j in range(4)])
    lives = lane_row([table[4 + j : 5 + j] for j in range(4)])
    lags = lane_row([table[8:9]] * 4)
    label = lanes((1, HALF)).astype(jnp.float32)
    wanted = jnp.concatenate(
        [group_meta[t][:, j : j + 1] for t in range(8) for j in range(BLOCKS)], axis=0
    )
    base = ((z * 4 + y) * 2 * BPD).astype(jnp.float32)
    mask = jnp.concatenate(
        [
            jnp.where(wanted == blocks, 1.0, 0.0),
            jnp.where((blocks >= base) & (blocks < base + 2 * BPD), 1.0, 0.0),
            jnp.zeros((15, HALF), jnp.float32),
        ],
        axis=0,
    )
    ahead = jnp.where(rows_of((HALF, HALF)) < lanes((HALF, HALF)), 1.0, 0.0)
    within = jnp.dot(mask, ahead, precision=HIGHEST, preferred_element_type=jnp.float32)
    totals = jnp.broadcast_to(jnp.sum(mask, axis=1, keepdims=True), (48, HALF))
    row, col = rows_of((48, 48)), lanes((48, 48))
    above = jnp.where((row > col) & (row < TARGETS), 1.0, 0.0)
    rank = within + jnp.dot(above, totals, precision=HIGHEST, preferred_element_type=jnp.float32)
    rank = jnp.where(mask > 0.0, rank, -1.0)
    count_a = jnp.sum(totals[0:TARGETS, 0:1], axis=0, keepdims=True)
    count_b = totals[TARGETS : TARGETS + 1, 0:1]
    over = jnp.where((count_a > PAIRS) | (count_b > SLOTS), 1.0, 0.0)

    def spread(values):
        return jnp.broadcast_to(jnp.sum(values, axis=1, keepdims=True), values.shape)

    def store(code, list_ref, live_ref, lag_ref):
        list_ref[...] = spread(code).astype(jnp.int32)
        live_ref[...] = spread(jnp.where(code > 0.0, lives, 0.0))
        lag_ref[...] = spread(jnp.where(code > 0.0, lags, 0.0))

    slot = rows_of((32, HALF)).astype(jnp.float32)
    code = jnp.zeros((32, HALF), jnp.float32)
    for r in range(TARGETS):
        code += jnp.where(slot == rank[r : r + 1], label * 64.0 + (r + 1.0), 0.0)
    store(code, list_a, live_a, lag_a)
    slot = rows_of((32, HALF)).astype(jnp.float32)
    code = jnp.where(slot == rank[TARGETS : TARGETS + 1], label * 64.0 + (blocks - base + 1.0), 0.0)
    store(code, list_b, live_b, lag_b)
    return over


def placing(codes, count):
    row = (codes & 63) - 1
    here = jnp.where(row == lanes(codes.shape), 1.0, 0.0)
    size = codes.shape[0]
    square = jnp.concatenate([here, jnp.zeros((HALF - size, HALF), jnp.float32)], axis=0).T
    return square[0:count, 0:size]


def whole_kernel(
    valid, slots, hits, white, taps, stream, angle, offset,
    answers_out, over_out,
    hold, taps_row, fixed, meta, base, message, row_two, message_two,
    all_fixed, all_base, all_meta, all_first, meta_two, all_second, meta_three,
    group_fixed, group_meta, sums_out, sums_in, base_out, base_in, next_out, next_in, last_row, group_row,
    columns, picked_a, picked_b, trig_a, trig_b, list_a, list_b, live_a, live_b, lag_a, lag_b,
    near_a, near_b, result_a, result_b, comps, factors, halo_rows,
    own_part, partner_part, x_part, owned, inverse,
    send_sems, recv_sems, local_sems, group_send, group_recv, halo_send, halo_recv, list_sems,
):
    z, y, core, x = grid_place()
    tm = x
    barrier = pltpu.get_barrier_semaphore()
    peers = [device_at(lax.rem(z + d, 8), y, core, x) for d in range(1, 8)] + [
        device_at(z, lax.rem(y + d, 4), core, x) for d in range(1, 4)
    ]
    for k in range(1, 8):
        peers.append(device_at(z, y, lax.rem(core + k % 2, 2), lax.rem(x + k // 2, 4)))
    for peer in peers:
        pl.semaphore_signal(barrier, inc=1, device_id=peer, device_id_type=MESH)

    place_of = offset[...].astype(jnp.float32)
    for block in range(BLOCKS):
        fixed[block, 0] = angle[2 * block : 2 * block + 2]
        fixed[block, 1] = place_of[2 * block : 2 * block + 2]
    taps_row[...] = jnp.zeros_like(taps_row)
    taps_row[:, : BAND + 1] = taps[...]
    lag_zero = jnp.sum(taps_row[...] * taps_row[...], axis=1, keepdims=True) + white[0, 0]
    remaining = valid[0, 0] - tm * SPAN
    lane = lanes((1, HALF))
    header = jnp.where(lane == 8, jnp.broadcast_to(lag_zero, (1, HALF)), 0.0)
    for block in range(BLOCKS):
        found = hits[0, slots[0, block]].astype(jnp.float32)
        count = jnp.clip(remaining - block * WIN, 0, WIN).astype(jnp.float32)
        header = jnp.where(lane == block, found, header)
        header = jnp.where(lane == 4 + block, count, header)
    meta[...] = header
    own_live = rows_of((8, HALF)) * HALF + lanes((8, HALF)) < remaining

    pl.semaphore_wait(barrier, len(peers))
    halos = [
        pltpu.make_async_remote_copy(
            src_ref=source,
            dst_ref=target,
            send_sem=halo_send.at[i],
            recv_sem=halo_recv.at[i],
            device_id=device_at(z, y, core, lax.rem(x + step, 4)),
            device_id_type=MESH,
        )
        for i, (source, target, step) in enumerate(
            (
                (stream.at[pl.ds(7, 1)], hold.at[0], 1),
                (stream.at[pl.ds(0, 1)], hold.at[1], 3),
            )
        )
    ]
    for copy in halos:
        copy.start()
    sems = (send_sems, recv_sems, local_sems)
    smalls = [
        Mover(meta, all_meta, sems, 0),
        Mover(row_two.at[0], meta_two, sems, 1),
        Mover(row_two.at[1], meta_three, sems, 2),
    ]
    relays = [
        Mover(fixed, all_fixed, sems, 3),
        Mover(message, all_first, sems, 4),
        Mover(message_two, all_second, sems, 5),
        Mover(base, all_base, sems, 6),
    ]
    group = Group(group_send, group_recv)
    me = group.me
    big, small, mid = relays[0], smalls[0], relays[3]
    small.start_first()
    big.start_first()
    places_in = group.to_all(0, lambda t: fixed, group_fixed.at[me])
    blocks_in = group.to_all(1, lambda t: meta, group_meta.at[me])
    group_fixed[me] = fixed[...]
    group_meta[me] = meta[...]

    spread = jnp.broadcast_to(taps_row[...], (WIN, WIN))
    shifted = pltpu.roll(spread, HALF, 1, stride=1, stride_axis=0)
    lag_row = lax.dot_general(
        spread[:8], shifted, NT, precision=HIGHEST, preferred_element_type=jnp.float32
    )
    lag_row = lag_row + jnp.where(lanes((8, WIN)) == HALF, white[0, 0], 0.0)
    band = pltpu.roll(
        jnp.broadcast_to(lag_row[0:1], (WIN, WIN)), WIN - HALF - BAND, 1, stride=1, stride_axis=0
    )[:, :HALF]
    landed(halos)
    extended = jnp.concatenate(
        [hold[0], stream[...], hold[1], jnp.zeros((6, HALF), jnp.float32)], axis=0
    )
    place = (rows_of((16, HALF)) - 1) * HALF + lanes((16, HALF))
    extended = jnp.where((place < remaining) & (place + tm * SPAN >= 0), extended, 0.0)
    base_own = jnp.where(own_live, band_filter(extended, band), 0.0)
    for block in range(BLOCKS):
        base[block] = base_own[2 * block : 2 * block + 2]
    mid.start_first()

    comps[...] = jnp.zeros_like(comps)
    halo_rows[...] = jnp.zeros_like(halo_rows)
    sums_out[...] = jnp.zeros_like(sums_out)
    base_out[...] = jnp.zeros_like(base_out)
    result_a[...] = jnp.zeros_like(result_a)
    result_b[...] = jnp.zeros_like(result_b)
    landed(places_in)
    landed(blocks_in)
    for block in range(BLOCKS):
        comps[9, block : block + 1, :] = joined(fixed[block, 0])
    right = group_fixed[jnp.minimum(x + 1, 3) * 2 + core, 0, 0]
    left = group_fixed[jnp.maximum(x - 1, 0) * 2 + core, BLOCKS - 1, 0]
    comps[9, 4:5, :] = jnp.concatenate([right[0:1], left[1:2]], axis=1)
    turn = 2.0 * comps[9]
    comps[9] = jnp.cos(turn)
    comps[10] = jnp.sin(turn)
    turned = jnp.concatenate(
        [group_fixed[t, block, 1] for t in range(8) for block in range(BLOCKS)]
        + [jnp.zeros((HALF // 2, HALF), jnp.float32)],
        axis=0,
    ).T

    def column(t, block, half):
        at = 8 * t + 2 * block + half
        return jnp.broadcast_to(turned[:, at : at + 1], (HALF, HALF))

    for t in range(8):
        for block in range(BLOCKS):
            for half in range(2):
                columns[BLOCKS * t + block, HALF * half : HALF * half + HALF, :] = column(
                    t, block, half
                )

    small.start_second()
    big.start_second()
    small.arrive()
    over = make_lists(all_meta, group_meta, near_a, near_b, live_a, live_b, lag_a, lag_b)
    copies = [
        pltpu.make_async_copy(near_a, list_a, list_sems.at[0]),
        pltpu.make_async_copy(near_b, list_b, list_sems.at[1]),
    ]
    for copy in copies:
        copy.start()
    mid.start_second()
    into_a = placing(near_a[...], TARGETS)
    into_b = placing(near_b[...], 2 * BPD)
    into_a = jnp.concatenate([into_a] * 3, axis=1).astype(jnp.bfloat16)
    into_b = jnp.concatenate([into_b] * 3, axis=1).astype(jnp.bfloat16)
    for copy in copies:
        copy.wait()
    big.arrive()

    wide_lane = lanes((1, WIN)).astype(jnp.float32)

    def doubled(row):
        return jnp.concatenate([row, row], axis=1)

    def six(p, where_at, trig, live, lag):
        turn = 2.0 * all_fixed[where_at + (0,)]
        co2, si2 = jnp.cos(turn), jnp.sin(turn)
        trig[p, 0:2, :] = co2
        trig[p, 2:4, :] = si2
        co, si = joined(co2), joined(si2)
        weight = jnp.where(
            wide_lane < doubled(live[pl.ds(p, 1), :]), doubled(lag[pl.ds(p, 1), :]), 0.0
        )
        return all_fixed[where_at + (1,)], co, si, weight_rows(weight, co, si)

    def three(p, where_at, trig, source):
        f = joined(source[where_at])
        return [f, f * joined(trig[p, 0:2, :]), f * joined(trig[p, 2:4, :])]

    def keep_rows(result, p, values):
        for c, value in enumerate(values):
            result[pl.ds(p, 1), WIN * c : WIN * c + WIN] = value

    def gathered_rows(into, result, count):
        values = result[:, 0 : WIN * count]
        high = values.astype(jnp.bfloat16)
        rest = values - high.astype(jnp.float32)
        middle = rest.astype(jnp.bfloat16)
        low = (rest - middle.astype(jnp.float32)).astype(jnp.bfloat16)
        parts = jnp.concatenate([high, middle, low], axis=0)
        return jnp.dot(into, parts, preferred_element_type=jnp.float32)

    def pair_weights(p, carry):
        code = list_a[p, 0]
        places, _, _, values = six(
            p, locate(lax.shift_right_logical(code, 6)), trig_a, live_a, lag_a
        )
        picked = matches(columns[jnp.clip((code & 63) - 1, 0, TARGETS - 1)], places)
        picked_a[p] = picked
        keep_rows(result_a, p, split_product(values, picked))
        return carry

    def pair_next(source):
        def body(p, carry):
            code = list_a[p, 0]
            values = three(p, locate(lax.shift_right_logical(code, 6)), trig_a, source)
            keep_rows(result_a, p, split_product(values, picked_a[p]))
            return carry

        return body

    lax.fori_loop(0, PAIRS, pair_weights, 0, unroll=UNROLL)

    def hand_out(count, target):
        out = gathered_rows(into_a, result_a, count)
        empty = jnp.zeros((1, HALF), jnp.float32)
        for t in range(8):
            for c in range(count):
                at = WIN * c
                first = BLOCKS * t
                target[t, 5 * c : 5 * c + 4, :] = out[first : first + 4, at : at + WIN]
                right = out[first + 8 : first + 9, at : at + HALF] if t < 6 else empty
                left = out[first - 5 : first - 4, at + HALF : at + WIN] if t >= 2 else empty
                target[t, 5 * c + 4 : 5 * c + 5, :] = jnp.concatenate([right, left], axis=1)

    def sum_of(arrived):
        combined = arrived[0]
        for t in range(1, 8):
            combined = combined + arrived[t]
        return combined

    hand_out(6, sums_out)
    arriving = group.to_all(2, lambda t: sums_out.at[t], sums_in.at[me])
    sums_in[me] = sums_out[me]
    mid.arrive()
    lax.fori_loop(0, PAIRS, pair_next(all_base), 0, unroll=4)
    hand_out(3, base_out)
    arriving_base = group.to_all(11, lambda t: base_out.at[t], base_in.at[me])
    base_in[me] = base_out[me]
    landed(arriving)
    combined = sum_of(sums_in)
    for c in range(6):
        comps[3 + c, 0:5, :] = combined[5 * c : 5 * c + 5]
    m_aa, m_ab, m_ac, m_bb, m_bc, m_cc, det = adjugate(*(comps[c] for c in range(3, 9)))
    co, si = comps[9], comps[10]
    seg_row = rows_of((8, WIN))
    at = lanes((8, WIN))
    time = tm * SPAN + jnp.where(
        seg_row < BLOCKS, seg_row * WIN + at, jnp.where(at < HALF, SPAN + at, at - WIN)
    )
    inside = (seg_row < BLOCKS) | ((seg_row == BLOCKS) & ((at < BAND) | (at >= WIN - BAND)))
    live = (time >= 0) & (time < valid[0, 0]) & inside
    scale = jnp.where(live, 1.0, 0.0) / det
    factors[0] = (m_aa + m_ab * co + m_ac * si) * scale
    factors[1] = (m_ab + m_bb * co + m_bc * si) * scale
    factors[2] = (m_ac + m_bc * co + m_cc * si) * scale
    landed(arriving_base)
    combined = sum_of(base_in)
    for c in range(3):
        comps[c, 0:5, :] = combined[5 * c : 5 * c + 5]

    def change():
        return factors[0] * comps[0] + factors[1] * comps[1] + factors[2] * comps[2]

    def filter_signal(signal, out):
        halo_rows[0:1] = signal[4:5, HALF:]
        for block in range(BLOCKS):
            halo_rows[2 * block + 1 : 2 * block + 2] = signal[block : block + 1, :HALF]
            halo_rows[2 * block + 2 : 2 * block + 3] = signal[block : block + 1, HALF:]
        halo_rows[9:10] = signal[4:5, :HALF]
        result = jnp.where(own_live, band_filter(halo_rows[...], band), 0.0)
        for block in range(BLOCKS):
            out[block] = result[2 * block : 2 * block + 2]
        return result

    signal_first = change()
    filtered_first = filter_signal(signal_first, message)
    own = halo_rows[1:9]
    row_two[0] = (
        jnp.where(lane == 0, total(base_own * own), 0.0)
        + jnp.where(lane == 1, total(filtered_first * own), 0.0)
        + jnp.where(lane == 2, over, 0.0)
    )

    pixel = rows_of((WIN, HALF)).astype(jnp.float32)

    def owned_first(p, carry):
        code = list_b[p, 0]
        where_at = locate(lax.shift_right_logical(code, 6))
        places, co, si, values = six(p, where_at, trig_b, live_b, lag_b)
        f = joined(all_base[where_at])
        values = [f, f * co, f * si] + values
        picked = matches(pixel, places)
        picked_b[p] = picked
        keep_rows(result_b, p, split_product(values, picked))
        return carry

    def owned_next(source):
        def body(p, carry):
            code = list_b[p, 0]
            values = three(p, locate(lax.shift_right_logical(code, 6)), trig_b, source)
            keep_rows(result_b, p, split_product(values, picked_b[p]))
            return carry

        return body

    def owned_out(first, count, number):
        out = gathered_rows(into_b, result_b, count)
        for half in range(2):
            for c in range(count):
                own_part[half, first + c] = out[BPD * half : BPD * half + BPD, WIN * c : WIN * c + WIN]
        span = pl.ds(first, count)
        return group.to_partner(number, own_part.at[1 - core, span], partner_part.at[span])

    def owned_along(first, count, number, arriving):
        landed(arriving)
        span = pl.ds(first, count)
        x_part[x, span] = own_part[core, span] + partner_part[span]
        return group.along(number, x_part.at[x, span])

    def owned_sum(first, count):
        span = pl.ds(first, count)
        owned[span] = x_part[0, span] + x_part[1, span] + x_part[2, span] + x_part[3, span]

    def sums_of(metas):
        return jnp.sum(metas[...].reshape(32, 1, HALF), axis=0)

    big, small = relays[1], smalls[1]
    small.start_first()
    big.start_first()
    lax.fori_loop(0, SLOTS, owned_first, 0, unroll=2)
    small.start_second()
    big.start_second()
    waiting_first = owned_out(0, 9, 5)
    small.arrive()
    sums = sums_of(meta_two)
    big.arrive()

    lax.fori_loop(0, PAIRS, pair_next(all_first), 0, unroll=4)
    hand_out(3, next_out)
    for t in range(8):
        next_out[t, 15:16, :] = doubled(sums)
    arriving = group.to_all(3, lambda t: next_out.at[t], next_in.at[me])
    next_in[me] = next_out[me]
    landed(arriving)
    combined = sum_of(next_in)
    for c in range(3):
        comps[c, 0:5, :] = combined[5 * c : 5 * c + 5]
    sums = combined[15:16, :HALF]
    product, curve = sums[:, 0:1], sums[:, 1:2]
    over_out[...] = jnp.broadcast_to(sums[:, 2:3], (1, HALF))
    alpha = product / curve
    filtered_second = filter_signal(signal_first - alpha * change(), message_two)
    own = halo_rows[1:9]
    row_two[1] = (
        jnp.where(lane == 0, total((base_own - alpha * filtered_first) * own), 0.0)
        + jnp.where(lane == 1, total(filtered_second * own), 0.0)
        + jnp.where(lane == 2, total(filtered_first * own), 0.0)
    )

    big, small = relays[2], smalls[2]
    small.start_first()
    big.start_first()
    first_along = owned_along(0, 9, 6, waiting_first)
    lax.fori_loop(0, SLOTS, owned_next(all_first), 0, unroll=4)
    waiting_second = owned_out(9, 3, 7)
    small.start_second()
    big.start_second()
    second_along = owned_along(9, 3, 8, waiting_second)
    small.arrive()
    last_row[...] = sums_of(meta_three)
    rows_in = group.to_all(4, lambda t: last_row, group_row.at[me])
    group_row[me] = last_row[...]
    big.arrive()
    lax.fori_loop(0, SLOTS, owned_next(all_second), 0, unroll=4)
    waiting_third = owned_out(12, 3, 9)
    third_along = owned_along(12, 3, 10, waiting_third)

    landed(rows_in)
    sums = group_row[0]
    for t in range(1, 8):
        sums = sums + group_row[t]
    product_next = sums[:, 0:1]
    beta = product_next / product
    curve_next = sums[:, 1:2] + 2.0 * beta * sums[:, 2:3] + beta * beta * curve
    alpha_next = product_next / curve_next

    def solve(r1, r2, r3):
        i_aa, i_ab, i_ac, i_bb, i_bc, i_cc = (inverse[c] for c in range(6))
        return (
            i_aa * r1 + i_ab * r2 + i_ac * r3,
            i_ab * r1 + i_bb * r2 + i_bc * r3,
            i_ac * r1 + i_bc * r2 + i_cc * r3,
        )

    landed(first_along)
    owned_sum(0, 9)
    *minors, det = adjugate(*(owned[c] for c in range(3, 9)))
    scale = 1.0 / det
    for c, minor in enumerate(minors):
        inverse[c] = minor * scale
    landed(second_along)
    owned_sum(9, 3)
    start = solve(*(owned[c] for c in range(3)))
    for c in range(3):
        owned[c] = owned[c] - alpha * owned[9 + c]
    middle = solve(*(owned[c] for c in range(3)))
    for c in range(3):
        answers_out[c] = alpha * start[c] + alpha_next * (middle[c] + beta * start[c])
        owned[c] = owned[c] - alpha_next * beta * owned[9 + c]
    landed(third_along)
    owned_sum(12, 3)
    final = solve(*(owned[c] - alpha_next * owned[12 + c] for c in range(3)))
    for c in range(3):
        answers_out[3 + c] = final[c]
    for mover in smalls + relays + [group]:
        mover.finish()
    for copy in halos:
        copy.wait_send()


def f32(*shape):
    return jax.ShapeDtypeStruct(shape, jnp.float32)


def gathered_shape(rows):
    return f32(2, 8, 4, 4, rows, HALF)


def gather_rows(values, part, number):
    rows, parts = pl.pallas_call(
        gather_kernel,
        out_shape=(gathered_shape(8), gathered_shape(1)),
        in_specs=[vmem] * 2,
        out_specs=(vmem,) * 2,
        scratch_shapes=EXCHANGE_SCRATCH,
        compiler_params=pltpu.CompilerParams(collective_id=number, has_side_effects=True),
        name="gather",
    )(values, part)
    return rows.reshape(LABELS, 2, HALF), parts.reshape(DEVICES, HALF)


def any_lengths(
    time_streams, pol_angle, offsets, block_slots, hit_ids, valid_counts, filter_taps, white_weight
):
    valid = valid_counts.reshape(1)
    message, metas, base, band = pl.pallas_call(
        prepare_kernel,
        out_shape=(gathered_shape(32), gathered_shape(1), f32(8, HALF), f32(WIN, HALF)),
        in_specs=[smem] * 4 + [vmem] * 4,
        out_specs=(vmem,) * 4,
        scratch_shapes=[
            pltpu.VMEM((2, 1, HALF), jnp.float32),
            pltpu.VMEM((1, WIN), jnp.float32),
            pltpu.VMEM((32, HALF), jnp.float32),
            pltpu.VMEM((1, HALF), jnp.float32),
        ]
        + EXCHANGE_SCRATCH
        + [pltpu.SemaphoreType.DMA((2,)), pltpu.SemaphoreType.DMA((2,))],
        compiler_params=pltpu.CompilerParams(collective_id=0, has_side_effects=True),
        name="prepare",
    )(
        valid, block_slots.reshape(BLOCKS), hit_ids.reshape(-1), white_weight.reshape(1),
        filter_taps.reshape(1, BAND + 1), time_streams.reshape(8, HALF), pol_angle.reshape(8, HALF),
        offsets.reshape(8, HALF),
    )
    gathered = message.reshape(LABELS, 8, HALF)
    metas = metas.reshape(DEVICES, HALF)

    blocks = metas[:, 0:4].reshape(LABELS)
    lives = metas[:, 4:8].reshape(LABELS).astype(jnp.int32)
    lag_zero = metas[:, 8]
    order = jnp.arange(LABELS, dtype=jnp.int32)
    same = blocks[:, None] == blocks[None, :]
    ahead = (order[None, :] - order[:, None] - 1) % LABELS
    nexts = (order + 1 + jnp.min(jnp.where(same, ahead, LABELS), axis=1)) % LABELS
    counts = jnp.sum(same, axis=1, dtype=jnp.int32)
    owned = (lax.axis_index("det") * BPD + jnp.arange(BPD, dtype=jnp.int32)).astype(jnp.float32)
    mine = owned[:, None] == blocks[None, :]
    heads = jnp.concatenate(
        [
            jnp.min(jnp.where(mine, order[None, :], LABELS - 1), axis=1),
            jnp.sum(mine, axis=1, dtype=jnp.int32),
        ]
    )

    first, part_one, factors, signal = pl.pallas_call(
        first_kernel,
        out_shape=(f32(8, HALF), f32(1, HALF), f32(3, 8, WIN), f32(8, WIN)),
        in_specs=[smem] * 5 + [vmem] * 3,
        out_specs=(vmem,) * 4,
        scratch_shapes=[
            pltpu.VMEM((12, 8, WIN), jnp.float32),
            pltpu.VMEM((16, HALF), jnp.float32),
        ],
        name="first",
    )(valid, nexts, counts, lives, lag_zero, gathered, base, band)
    second, parts_two = gather_rows(first, part_one, 1)
    other, part_two = pl.pallas_call(
        second_kernel,
        out_shape=(f32(8, HALF), f32(1, HALF)),
        in_specs=[smem] * 3 + [vmem] * 8,
        out_specs=(vmem,) * 2,
        scratch_shapes=[
            pltpu.VMEM((3, 8, WIN), jnp.float32),
            pltpu.VMEM((16, HALF), jnp.float32),
        ],
        name="second",
    )(valid, nexts, counts, gathered, second, parts_two, base, first, band, factors, signal)
    third, parts_three = gather_rows(other, part_two, 2)
    answers = pl.pallas_call(
        last_kernel,
        out_shape=(f32(3, BPD, WIN), f32(3, BPD, WIN)),
        in_specs=[smem] * 4 + [vmem] * 5,
        out_specs=(vmem,) * 2,
        scratch_shapes=[pltpu.VMEM((15, BPD, WIN), jnp.float32)],
        name="last",
    )(heads, nexts, lives, lag_zero, gathered, second, third, parts_two, parts_three)
    return tuple(answers)


def wide_buffer(*shape):
    return pltpu.VMEM((8, 4) + shape, jnp.float32)


def room(*shape):
    return pltpu.VMEM(shape, jnp.float32)


def per_device(*args):
    (
        time_streams, pol_angle, offsets, block_slots, hit_ids, valid_counts, filter_taps,
        white_weight,
    ) = args
    fast = pl.pallas_call(
        whole_kernel,
        out_shape=(f32(6, BPD, WIN), f32(1, HALF)),
        in_specs=[smem] * 4 + [vmem] * 4,
        out_specs=(vmem,) * 2,
        scratch_shapes=[
            room(2, 1, HALF), room(1, WIN), room(BLOCKS, 2, 2, HALF), room(1, HALF),
            room(BLOCKS, 2, HALF), room(BLOCKS, 2, HALF), room(2, 1, HALF), room(BLOCKS, 2, HALF),
            wide_buffer(BLOCKS, 2, 2, HALF), wide_buffer(BLOCKS, 2, HALF), wide_buffer(1, HALF),
            wide_buffer(BLOCKS, 2, HALF), wide_buffer(1, HALF), wide_buffer(BLOCKS, 2, HALF),
            wide_buffer(1, HALF),
            room(8, BLOCKS, 2, 2, HALF), room(8, 1, HALF), room(8, 32, WIN), room(8, 32, WIN),
            room(8, 16, WIN), room(8, 16, WIN),
            room(8, 16, WIN), room(8, 16, WIN), room(1, HALF), room(8, 1, HALF),
            room(TARGETS, WIN, HALF),
            pltpu.VMEM((PAIRS, WIN, WIN), jnp.bfloat16),
            pltpu.VMEM((SLOTS, WIN, WIN), jnp.bfloat16),
            room(PAIRS, 4, HALF), room(SLOTS, 4, HALF),
            pltpu.SMEM((32, HALF), jnp.int32), pltpu.SMEM((32, HALF), jnp.int32),
            room(32, HALF), room(32, HALF), room(32, HALF), room(32, HALF),
            pltpu.VMEM((32, HALF), jnp.int32), pltpu.VMEM((32, HALF), jnp.int32),
            room(32, 9 * WIN), room(32, 9 * WIN),
            room(11, 8, WIN), room(3, 8, WIN), room(16, HALF),
            room(2, 15, BPD, WIN), room(15, BPD, WIN), room(4, 15, BPD, WIN), room(15, BPD, WIN),
            room(6, BPD, WIN),
            pltpu.SemaphoreType.DMA((7, 10)), pltpu.SemaphoreType.DMA((7, 10)),
            pltpu.SemaphoreType.DMA((7,)), pltpu.SemaphoreType.DMA((12, 8)),
            pltpu.SemaphoreType.DMA((12, 8)), pltpu.SemaphoreType.DMA((2,)),
            pltpu.SemaphoreType.DMA((2,)), pltpu.SemaphoreType.DMA((2,)),
        ],
        compiler_params=pltpu.CompilerParams(collective_id=3, has_side_effects=True),
        name="whole",
    )(
        valid_counts, block_slots.reshape(1, BLOCKS), hit_ids, white_weight,
        filter_taps.reshape(1, BAND + 1), time_streams.reshape(8, HALF),
        pol_angle.reshape(8, HALF), offsets.reshape(8, HALF),
    )
    answers = lax.cond(
        fast[1][0, 0] > 0.0, lambda f, *a: jnp.concatenate(any_lengths(*a)), lambda f, *a: f,
        fast[0], *args,
    )
    return tuple(jnp.transpose(part, (1, 0, 2)) for part in (answers[:3], answers[3:]))


def solution(mesh):
    in_specs = (
        P("det", None, "tm"),
        P("det", None, "tm"),
        P("det", None, "tm"),
        P("det", None, "tm"),
        P("det", None),
        P("det", None),
        P("det", None, None),
        P("det", None),
    )
    out_specs = (P("det", None, None), P("det", None, None))
    return jax.shard_map(
        per_device, mesh=mesh, in_specs=in_specs, out_specs=out_specs, check_vma=False
    )
```

```python
import functools

import jax
import jax.numpy as jnp
from jax import lax
from jax.experimental import pallas as pl
from jax.experimental.pallas import tpu as pltpu
from jax.sharding import PartitionSpec as P

WIN = 256
BAND = 64
BPD = 16
HALF = 128
SPAN = 1024
BLOCKS = 4
DEVICES = 256
PAIRS = 24
TARGETS = 32
UNROLL = 4
SLOTS = 20
LABELS = DEVICES * BLOCKS

HIGHEST = lax.Precision.HIGHEST
NT = (((1,), (1,)), ((), ()))
MESH = pl.DeviceIdType.MESH

vmem = pl.BlockSpec(memory_space=pltpu.VMEM)
smem = pl.BlockSpec(memory_space=pltpu.SMEM)


def lanes(shape):
    return lax.broadcasted_iota(jnp.int32, shape, len(shape) - 1)


def rows_of(shape):
    return lax.broadcasted_iota(jnp.int32, shape, 0)


def band_filter(extended, band):
    turned = pltpu.roll(extended, HALF // 2, 1)
    keep = lanes((8, HALF)) < HALF // 2
    first = jnp.where(keep, turned[0:8], turned[1:9])
    second = jnp.where(keep, turned[1:9], turned[2:10])
    window = jnp.concatenate([first, second], axis=1)
    return jnp.dot(window, band, precision=HIGHEST, preferred_element_type=jnp.float32)


def grid_place():
    det = lax.axis_index("det")
    x = lax.axis_index("tm")
    return lax.div(det, 8), lax.rem(lax.div(det, 2), 4), lax.rem(det, 2), x


def device_at(z, y, core, x):
    return {"det": (z * 4 + y) * 2 + core, "tm": x}


def slot_of(z, y, core, x):
    major = y + core * (x - y)
    minor = x + core * (y - x)
    return ((core * 8 + z) * 4 + major) * 4 + minor


def meet():
    z, y, core, x = grid_place()
    barrier = pltpu.get_barrier_semaphore()
    peers = (
        [device_at(lax.rem(z + d, 8), y, core, x) for d in range(1, 8)]
        + [device_at(z, lax.rem(y + d, 4), core, x) for d in range(1, 4)]
        + [device_at(z, y, core, lax.rem(x + d, 4)) for d in range(1, 4)]
        + [device_at(z, y, 1 - core, x)]
    )
    for peer in peers:
        pl.semaphore_signal(barrier, inc=1, device_id=peer, device_id_type=MESH)
    pl.semaphore_wait(barrier, len(peers))


def exchange(sources, buffers, send_sems, recv_sems, local_sems):
    z, y, core, x = grid_place()
    a = y + core * (x - y)
    b = x + core * (y - x)

    def major_peer(step):
        return device_at(
            z,
            y + (1 - core) * (lax.rem(y + step, 4) - y),
            core,
            x + core * (lax.rem(x + step, 4) - x),
        )

    def minor_peer(step):
        return device_at(
            z,
            y + core * (lax.rem(y + step, 4) - y),
            core,
            x + (1 - core) * (lax.rem(x + step, 4) - x),
        )

    arrays = range(len(sources))

    def send(number, source_of, target_of, peer):
        copies = []
        for i in arrays:
            copy = pltpu.make_async_remote_copy(
                src_ref=source_of(i),
                dst_ref=target_of(i),
                send_sem=send_sems.at[i, number],
                recv_sem=recv_sems.at[i, number],
                device_id=peer,
                device_id_type=MESH,
            )
            copy.start()
            copies.append(copy)
        return copies

    def landed(copies):
        for copy in copies:
            copy.wait_recv()

    started = []
    keep = [
        pltpu.make_async_copy(sources[i], buffers[i].at[core, z, a, b], local_sems.at[i])
        for i in arrays
    ]
    first = [
        send(
            d - 1,
            lambda i: sources[i],
            lambda i: buffers[i].at[core, z, a, b],
            device_at(lax.rem(z + d, 8), y, core, x),
        )
        for d in (4, 3, 5, 2, 6, 1, 7)
    ]
    for copy in keep:
        copy.start()
    for copy in keep:
        copy.wait()
    for copies in first:
        landed(copies)
    started += first

    def column(i):
        return buffers[i].at[core, :, a, b]

    second = [send(6 + d, column, column, major_peer(d)) for d in (2, 1, 3)]
    for copies in second:
        landed(copies)
    started += second

    def part(number, half):
        depth = pl.ds(4 * half, 4)
        return lambda i: buffers[i].at[core, depth, :, number]

    def whole(number):
        return lambda i: buffers[i].at[core, :, :, number]

    after = minor_peer(1)
    before = minor_peer(3)
    partner = device_at(z, y, 1 - core, x)
    left = lax.rem(b + 3, 4)
    right = lax.rem(b + 1, 4)
    far = lax.rem(b + 2, 4)
    up = [send(10, part(b, 0), part(b, 0), after)]
    down = [send(12, part(b, 1), part(b, 1), before)]
    up.append(send(11, part(b, 1), part(b, 1), after))
    down.append(send(13, part(b, 0), part(b, 0), before))
    swaps = [send(16, whole(b), whole(b), partner)]
    landed(up[0])
    up.append(send(14, part(left, 0), part(left, 0), after))
    landed(down[0])
    down.append(send(15, part(right, 1), part(right, 1), before))
    landed(up[1])
    swaps.append(send(17, whole(left), whole(left), partner))
    landed(down[1])
    swaps.append(send(18, whole(right), whole(right), partner))
    landed(up[2])
    landed(down[2])
    swaps.append(send(19, whole(far), whole(far), partner))
    for copies in swaps:
        landed(copies)
    started += up + down + swaps
    for copies in started:
        for copy in copies:
            copy.wait_send()


EXCHANGE_SCRATCH = [
    pltpu.SemaphoreType.DMA((2, 20)),
    pltpu.SemaphoreType.DMA((2, 20)),
    pltpu.SemaphoreType.DMA((2,)),
]


def gather_kernel(values, meta, values_out, meta_out, send_sems, recv_sems, local_sems):
    meet()
    exchange([values, meta], [values_out, meta_out], send_sems, recv_sems, local_sems)


def prepare_kernel(
    valid, slots, hits, white, taps, stream, angle, offset,
    message_out, meta_out, base_out, band,
    hold, taps_row, message, meta, send_sems, recv_sems, local_sems, halo_send, halo_recv,
):
    meet()
    z, y, core, x = grid_place()
    tm = x
    halos = [
        pltpu.make_async_remote_copy(
            src_ref=stream.at[pl.ds(7, 1)],
            dst_ref=hold.at[0],
            send_sem=halo_send.at[0],
            recv_sem=halo_recv.at[0],
            device_id=device_at(z, y, core, lax.rem(x + 1, 4)),
            device_id_type=MESH,
        ),
        pltpu.make_async_remote_copy(
            src_ref=stream.at[pl.ds(0, 1)],
            dst_ref=hold.at[1],
            send_sem=halo_send.at[1],
            recv_sem=halo_recv.at[1],
            device_id=device_at(z, y, core, lax.rem(x + 3, 4)),
            device_id_type=MESH,
        ),
    ]
    for copy in halos:
        copy.start()
    cosine = jnp.cos(2.0 * angle[...])
    sine = jnp.sin(2.0 * angle[...])
    place_of = offset[...].astype(jnp.float32)
    for block in range(BLOCKS):
        for half in range(2):
            row = 2 * block + half
            for part, values in enumerate((cosine, sine, place_of)):
                at = 8 * block + 4 * half + part + 1
                message[at : at + 1, :] = values[row : row + 1]
    taps_row[...] = jnp.zeros_like(taps_row)
    taps_row[:, : BAND + 1] = taps[...]
    spread = jnp.broadcast_to(taps_row[...], (WIN, WIN))
    shifted = pltpu.roll(spread, HALF, 1, stride=1, stride_axis=0)
    lag_row = lax.dot_general(
        spread[:8], shifted, NT, precision=HIGHEST, preferred_element_type=jnp.float32
    )
    lag_row = lag_row + jnp.where(lanes((8, WIN)) == HALF, white[0], 0.0)
    table = pltpu.roll(
        jnp.broadcast_to(lag_row[0:1], (WIN, WIN)), WIN - HALF - BAND, 1, stride=1, stride_axis=0
    )
    band[...] = table[:, :HALF]
    lag_zero = lag_row[0:1, HALF : HALF + 1]

    remaining = valid[0] - tm * SPAN
    lane = lanes((1, HALF))
    header = jnp.where(lane == 8, jnp.broadcast_to(lag_zero, (1, HALF)), 0.0)
    for block in range(BLOCKS):
        found = hits[slots[block]].astype(jnp.float32)
        count = jnp.clip(remaining - block * WIN, 0, WIN).astype(jnp.float32)
        header = jnp.where(lane == block, found, header)
        header = jnp.where(lane == 4 + block, count, header)
    meta[...] = header

    for copy in halos:
        copy.wait_recv()
    extended = jnp.concatenate(
        [hold[0], stream[...], hold[1], jnp.zeros((6, HALF), jnp.float32)], axis=0
    )
    place = (rows_of((16, HALF)) - 1) * HALF + lanes((16, HALF))
    extended = jnp.where((place < remaining) & (place + tm * SPAN >= 0), extended, 0.0)
    own_live = rows_of((8, HALF)) * HALF + lanes((8, HALF)) < remaining
    filtered = jnp.where(own_live, band_filter(extended, table[:, :HALF]), 0.0)
    for block in range(BLOCKS):
        for half in range(2):
            row = 2 * block + half
            at = 8 * block + 4 * half
            message[at : at + 1, :] = filtered[row : row + 1]
    base_out[...] = filtered
    exchange([message, meta], [message_out, meta_out], send_sems, recv_sems, local_sems)
    for copy in halos:
        copy.wait_send()


def split_rows(values):
    high = values.astype(jnp.bfloat16)
    rest = values - high.astype(jnp.float32)
    middle = rest.astype(jnp.bfloat16)
    low = (rest - middle.astype(jnp.float32)).astype(jnp.bfloat16)
    return jnp.concatenate([high, middle, low], axis=0)


def wide(tile, row):
    return jnp.concatenate([tile[row : row + 1], tile[row + 4 : row + 5]], axis=1)


def match_sum(column, places, values):
    count = values.shape[0]
    picked = jnp.where(column == places, 1.0, 0.0).astype(jnp.bfloat16)
    out = lax.dot_general(split_rows(values), picked, NT, preferred_element_type=jnp.float32)
    return out[:count] + out[count : 2 * count] + out[2 * count :]


def weight_rows(weight, cosine, sine):
    first = weight * cosine
    second = weight * sine
    return [weight, first, second, first * cosine, first * sine, second * sine]


def own_labels():
    z, y, core, x = grid_place()
    own = slot_of(z, y, core, x) * BLOCKS
    before = slot_of(z, y, core, jnp.maximum(x - 1, 0)) * BLOCKS + BLOCKS - 1
    after = slot_of(z, y, core, jnp.minimum(x + 1, 3)) * BLOCKS
    usable = [jnp.minimum(x, 1)] + [1] * BLOCKS + [jnp.minimum(3 - x, 1)]
    return [before] + [own + block for block in range(BLOCKS)] + [after], usable


def own_columns(labels, gathered):
    rows = []
    for seg in range(6):
        tile = gathered[labels[seg]]
        rows += [tile[3:4], tile[7:8]]
    rows.append(jnp.zeros((HALF - 12, HALF), jnp.float32))
    turned = jnp.concatenate(rows, axis=0).T
    return [
        jnp.concatenate([turned[:, 2 * s : 2 * s + 1], turned[:, 2 * s + 1 : 2 * s + 2]], axis=0)
        for s in range(6)
    ]


def adjugate(w1, w2, w3, w4, w5, w6):
    aa = 1.0 + w1
    bb = 1.0 + w4
    cc = 1.0 + w6
    m_aa = bb * cc - w5 * w5
    m_ab = w3 * w5 - w2 * cc
    m_ac = w2 * w5 - w3 * bb
    m_bb = aa * cc - w3 * w3
    m_bc = w2 * w3 - aa * w5
    m_cc = aa * bb - w2 * w2
    det = aa * m_aa + w2 * m_ab + w3 * m_ac
    return m_aa, m_ab, m_ac, m_bb, m_bc, m_cc, det


def rows_to_hold(signal, hold):
    hold[0:1] = signal[0:1, HALF:]
    for seg in range(1, 5):
        hold[2 * seg - 1 : 2 * seg] = signal[seg : seg + 1, :HALF]
        hold[2 * seg : 2 * seg + 1] = signal[seg : seg + 1, HALF:]
    hold[9:10] = signal[5:6, :HALF]


def total(values):
    return jnp.sum(jnp.sum(values, axis=1, keepdims=True), axis=0, keepdims=True)


def own_live_of(info):
    remaining = info[0] - lax.axis_index("tm") * SPAN
    return rows_of((8, HALF)) * HALF + lanes((8, HALF)) < remaining


def first_kernel(
    info, nexts, counts, lives, lag_zero, gathered, base, band,
    filtered_out, part_out, factors, signal_out, comps, hold,
):
    labels, flags = own_labels()
    columns = own_columns(labels, gathered)
    lane = lanes((1, WIN))
    comps[...] = jnp.zeros_like(comps)
    for seg in range(6):
        column = columns[seg]
        usable = flags[seg]

        def body(_, carry, column=column):
            label, acc = carry
            tile = gathered[label]
            f = wide(tile, 0)
            co = wide(tile, 1)
            si = wide(tile, 2)
            weight = jnp.where(lane < lives[label], lag_zero[label // BLOCKS], 0.0)
            values = jnp.concatenate(
                [f, f * co, f * si] + weight_rows(weight, co, si)
                + [jnp.zeros((7, WIN), jnp.float32)], axis=0,
            )
            return nexts[label], acc + match_sum(column, wide(tile, 3), values)

        start = labels[seg]
        _, acc = lax.fori_loop(
            0, counts[start] * usable, body, (start, jnp.zeros((16, WIN), jnp.float32))
        )
        for comp in range(9):
            comps[comp, seg : seg + 1, :] = acc[comp : comp + 1]
        tile = gathered[start]
        comps[9, seg : seg + 1, :] = wide(tile, 1)
        comps[10, seg : seg + 1, :] = wide(tile, 2)
        comps[11, seg : seg + 1, :] = jnp.where(lane < lives[start] * usable, 1.0, 0.0)
    m_aa, m_ab, m_ac, m_bb, m_bc, m_cc, det = adjugate(*(comps[c] for c in range(3, 9)))
    co, si, live = comps[9], comps[10], comps[11]
    scale = live / det
    q1 = (m_aa + m_ab * co + m_ac * si) * scale
    q2 = (m_ab + m_bb * co + m_bc * si) * scale
    q3 = (m_ac + m_bc * co + m_cc * si) * scale
    factors[0] = q1
    factors[1] = q2
    factors[2] = q3
    signal = q1 * comps[0] + q2 * comps[1] + q3 * comps[2]
    signal_out[...] = signal
    hold[...] = jnp.zeros_like(hold)
    rows_to_hold(signal, hold)
    filtered = jnp.where(own_live_of(info), band_filter(hold[...], band[...]), 0.0)
    filtered_out[...] = filtered
    own = hold[1:9]
    lane = lanes((1, HALF))
    part_out[...] = jnp.where(lane == 0, total(base[...] * own), 0.0) + jnp.where(
        lane == 1, total(filtered * own), 0.0
    )


def second_kernel(
    info, nexts, counts, gathered, second, parts, base, own_first, band, factors, signal_in,
    filtered_out, part_out, comps, hold,
):
    sums = jnp.sum(parts[...], axis=0, keepdims=True)
    alpha = sums[:, 0:1] / sums[:, 1:2]
    labels, flags = own_labels()
    columns = own_columns(labels, gathered)
    comps[...] = jnp.zeros_like(comps)
    for seg in range(6):
        column = columns[seg]

        def body(_, carry, column=column):
            label, acc = carry
            tile = gathered[label]
            pair = second[label]
            f = jnp.concatenate([pair[0:1], pair[1:2]], axis=1)
            values = jnp.concatenate(
                [f, f * wide(tile, 1), f * wide(tile, 2), jnp.zeros((13, WIN), jnp.float32)], axis=0
            )
            return nexts[label], acc + match_sum(column, wide(tile, 3), values)

        start = labels[seg]
        _, acc = lax.fori_loop(
            0, counts[start] * flags[seg], body, (start, jnp.zeros((16, WIN), jnp.float32))
        )
        for comp in range(3):
            comps[comp, seg : seg + 1, :] = acc[comp : comp + 1]
    change = factors[0] * comps[0] + factors[1] * comps[1] + factors[2] * comps[2]
    signal = signal_in[...] - alpha * change
    hold[...] = jnp.zeros_like(hold)
    rows_to_hold(signal, hold)
    filtered = jnp.where(own_live_of(info), band_filter(hold[...], band[...]), 0.0)
    filtered_out[...] = filtered
    own = hold[1:9]
    first = own_first[...]
    lane = lanes((1, HALF))
    part_out[...] = (
        jnp.where(lane == 0, total((base[...] - alpha * first) * own), 0.0)
        + jnp.where(lane == 1, total(filtered * own), 0.0)
        + jnp.where(lane == 2, total(first * own), 0.0)
    )


def last_kernel(
    heads, nexts, lives, lag_zero, gathered, second, third, parts_two, parts_three,
    solution_out, residual_out, comps,
):
    sums = jnp.sum(parts_two[...], axis=0, keepdims=True)
    product, curve = sums[:, 0:1], sums[:, 1:2]
    alpha = product / curve
    sums = jnp.sum(parts_three[...], axis=0, keepdims=True)
    product_next = sums[:, 0:1]
    beta = product_next / product
    curve_next = sums[:, 1:2] + 2.0 * beta * sums[:, 2:3] + beta * beta * curve
    alpha_next = product_next / curve_next
    column = rows_of((WIN, 1)).astype(jnp.float32)
    lane = lanes((1, WIN))
    for block in range(BPD):

        def body(_, carry):
            label, acc = carry
            tile = gathered[label]
            co = wide(tile, 1)
            si = wide(tile, 2)
            pair = second[label]
            trio = third[label]
            rows = []
            for f in (
                wide(tile, 0),
                jnp.concatenate([pair[0:1], pair[1:2]], axis=1),
                jnp.concatenate([trio[0:1], trio[1:2]], axis=1),
            ):
                rows += [f, f * co, f * si]
            weight = jnp.where(lane < lives[label], lag_zero[label // BLOCKS], 0.0)
            values = jnp.concatenate(
                rows + weight_rows(weight, co, si) + [jnp.zeros((1, WIN), jnp.float32)], axis=0
            )
            return nexts[label], acc + match_sum(column, wide(tile, 3), values)

        _, acc = lax.fori_loop(
            0, heads[BPD + block], body, (heads[block], jnp.zeros((16, WIN), jnp.float32))
        )
        for comp in range(15):
            comps[comp, block : block + 1, :] = acc[comp : comp + 1]
    m_aa, m_ab, m_ac, m_bb, m_bc, m_cc, det = adjugate(*(comps[c] for c in range(9, 15)))

    def solve(r1, r2, r3):
        return (
            (m_aa * r1 + m_ab * r2 + m_ac * r3) / det,
            (m_ab * r1 + m_bb * r2 + m_bc * r3) / det,
            (m_ac * r1 + m_bc * r2 + m_cc * r3) / det,
        )

    right = [comps[c] for c in range(3)]
    image = [comps[3 + c] for c in range(3)]
    other = [comps[6 + c] for c in range(3)]
    residual = [r - alpha * w for r, w in zip(right, image)]
    start = solve(*right)
    middle = solve(*residual)
    direction = [m + beta * s for m, s in zip(middle, start)]
    final = solve(
        *(r - alpha_next * (v + beta * w) for r, v, w in zip(residual, other, image))
    )
    for comp in range(3):
        answer = alpha * start[comp] + alpha_next * direction[comp]
        solution_out[comp] = answer
        residual_out[comp] = final[comp]


class Mover:
    def __init__(self, source, buffer, sems, number):
        self.source, self.buffer = source, buffer
        self.send_sems, self.recv_sems, self.local_sems = sems
        self.number = number
        self.z, self.y, self.core, self.x = grid_place()
        self.started = []

    def send(self, number, source, target, peer):
        copy = pltpu.make_async_remote_copy(
            src_ref=source,
            dst_ref=target,
            send_sem=self.send_sems.at[self.number, number],
            recv_sem=self.recv_sems.at[self.number, number],
            device_id=peer,
            device_id_type=MESH,
        )
        copy.start()
        self.started.append(copy)
        return copy

    def start_first(self):
        z, y, core, x = self.z, self.y, self.core, self.x
        own = self.buffer.at[z, y]
        self.first = [
            self.send(d - 1, self.source, own, device_at(lax.rem(z + d, 8), y, core, x))
            for d in (4, 3, 5, 2, 6, 1, 7)
        ]
        self.keep = pltpu.make_async_copy(self.source, own, self.local_sems.at[self.number])
        self.keep.start()

    def start_second(self):
        self.keep.wait()
        for copy in self.first:
            copy.wait_recv()
        column = self.buffer.at[:, self.y]
        self.second = [
            self.send(
                6 + d, column, column,
                device_at(self.z, lax.rem(self.y + d, 4), self.core, self.x),
            )
            for d in (2, 1, 3)
        ]

    def arrive(self):
        for copy in self.second:
            copy.wait_recv()

    def finish(self):
        for copy in self.started:
            copy.wait_send()


class Group:
    def __init__(self, send_sems, recv_sems):
        self.send_sems, self.recv_sems = send_sems, recv_sems
        self.z, self.y, self.core, self.x = grid_place()
        self.me = self.x * 2 + self.core
        self.started = []

    def send(self, number, k, source, target, peer):
        copy = pltpu.make_async_remote_copy(
            src_ref=source,
            dst_ref=target,
            send_sem=self.send_sems.at[number, k],
            recv_sem=self.recv_sems.at[number, k],
            device_id=peer,
            device_id_type=MESH,
        )
        copy.start()
        self.started.append(copy)
        return copy

    def to_all(self, number, source_of, target):
        copies = []
        for k in (4, 5, 2, 3, 6, 7, 1):
            x = lax.rem(self.x + k // 2, 4)
            core = lax.rem(self.core + k % 2, 2)
            copies.append(
                self.send(
                    number, k, source_of(x * 2 + core), target, device_at(self.z, self.y, core, x)
                )
            )
        return copies

    def to_partner(self, number, source, target):
        return [
            self.send(number, 0, source, target, device_at(self.z, self.y, 1 - self.core, self.x))
        ]

    def along(self, number, ref):
        return [
            self.send(
                number, d, ref, ref, device_at(self.z, self.y, self.core, lax.rem(self.x + d, 4))
            )
            for d in (2, 1, 3)
        ]

    def finish(self):
        for copy in self.started:
            copy.wait_send()


def landed(copies):
    for copy in copies:
        copy.wait_recv()


def locate(label):
    return (
        lax.shift_right_logical(label, 2) & 7,
        label & 3,
        lax.shift_right_logical(label, 5) & 3,
    )


def joined(tile):
    return jnp.concatenate([tile[0:1], tile[1:2]], axis=1)


def split_product(rows, picked):
    count = len(rows)
    values = jnp.concatenate(rows, axis=0)
    high = values.astype(jnp.bfloat16).astype(jnp.float32)
    rest = values - high
    middle = rest.astype(jnp.bfloat16).astype(jnp.float32)
    low = rest - middle
    pad = -3 * count % 16
    stack = [high, middle, low]
    if pad:
        stack.append(jnp.zeros((pad, WIN), jnp.float32))
    left = jnp.concatenate(stack, axis=0).astype(jnp.bfloat16)
    out = lax.dot_general(left, picked, NT, preferred_element_type=jnp.float32)
    return [
        out[c : c + 1] + out[count + c : count + c + 1] + out[2 * count + c : 2 * count + c + 1]
        for c in range(count)
    ]


def matches(column, places):
    low = jnp.where(column == places[0:1], 1.0, 0.0)
    high = jnp.where(column == places[1:2], 1.0, 0.0)
    return jnp.concatenate([low, high], axis=1).astype(jnp.bfloat16)


def make_lists(metas, group_meta, list_a, list_b, live_a, live_b, lag_a, lag_b):
    z, y, core, x = grid_place()
    table = jnp.concatenate(
        [metas[...].reshape(32, HALF), jnp.zeros((HALF - 32, HALF), jnp.float32)], axis=0
    ).T

    def lane_row(rows):
        out = rows[0]
        for j in range(1, 4):
            out = out + pltpu.roll(rows[j], 32 * j, 1)
        return out

    blocks = lane_row([table[j : j + 1] for j in range(4)])
    lives = lane_row([table[4 + j : 5 + j] for j in range(4)])
    lags = lane_row([table[8:9]] * 4)
    label = lanes((1, HALF)).astype(jnp.float32)
    wanted = jnp.concatenate(
        [group_meta[t][:, j : j + 1] for t in range(8) for j in range(BLOCKS)], axis=0
    )
    base = ((z * 4 + y) * 2 * BPD).astype(jnp.float32)
    mask = jnp.concatenate(
        [
            jnp.where(wanted == blocks, 1.0, 0.0),
            jnp.where((blocks >= base) & (blocks < base + 2 * BPD), 1.0, 0.0),
            jnp.zeros((15, HALF), jnp.float32),
        ],
        axis=0,
    )
    ahead = jnp.where(rows_of((HALF, HALF)) < lanes((HALF, HALF)), 1.0, 0.0)
    within = jnp.dot(mask, ahead, precision=HIGHEST, preferred_element_type=jnp.float32)
    totals = jnp.broadcast_to(jnp.sum(mask, axis=1, keepdims=True), (48, HALF))
    row, col = rows_of((48, 48)), lanes((48, 48))
    above = jnp.where((row > col) & (row < TARGETS), 1.0, 0.0)
    rank = within + jnp.dot(above, totals, precision=HIGHEST, preferred_element_type=jnp.float32)
    rank = jnp.where(mask > 0.0, rank, -1.0)
    count_a = jnp.sum(totals[0:TARGETS, 0:1], axis=0, keepdims=True)
    count_b = totals[TARGETS : TARGETS + 1, 0:1]
    over = jnp.where((count_a > PAIRS) | (count_b > SLOTS), 1.0, 0.0)

    def spread(values):
        return jnp.broadcast_to(jnp.sum(values, axis=1, keepdims=True), values.shape)

    def store(code, list_ref, live_ref, lag_ref):
        list_ref[...] = spread(code).astype(jnp.int32)
        live_ref[...] = spread(jnp.where(code > 0.0, lives, 0.0))
        lag_ref[...] = spread(jnp.where(code > 0.0, lags, 0.0))

    slot = rows_of((32, HALF)).astype(jnp.float32)
    code = jnp.zeros((32, HALF), jnp.float32)
    for r in range(TARGETS):
        code += jnp.where(slot == rank[r : r + 1], label * 64.0 + (r + 1.0), 0.0)
    store(code, list_a, live_a, lag_a)
    slot = rows_of((32, HALF)).astype(jnp.float32)
    code = jnp.where(slot == rank[TARGETS : TARGETS + 1], label * 64.0 + (blocks - base + 1.0), 0.0)
    store(code, list_b, live_b, lag_b)
    return over


def placing(codes, count):
    row = (codes & 63) - 1
    here = jnp.where(row == lanes(codes.shape), 1.0, 0.0)
    size = codes.shape[0]
    square = jnp.concatenate([here, jnp.zeros((HALF - size, HALF), jnp.float32)], axis=0).T
    return square[0:count, 0:size]


def whole_kernel(
    valid, slots, hits, white, taps, stream, angle, offset,
    answers_out, over_out,
    hold, taps_row, fixed, meta, base, message, row_two, message_two,
    all_fixed, all_base, all_meta, all_first, meta_two, all_second, meta_three,
    group_fixed, group_meta, sums_out, sums_in, base_out, base_in, next_out, next_in, last_row, group_row,
    columns, picked_a, picked_b, trig_a, trig_b, list_a, list_b, live_a, live_b, lag_a, lag_b,
    near_a, near_b, result_a, result_b, comps, factors, halo_rows,
    own_part, partner_part, x_part, owned, inverse,
    send_sems, recv_sems, local_sems, group_send, group_recv, halo_send, halo_recv, list_sems,
):
    z, y, core, x = grid_place()
    tm = x
    barrier = pltpu.get_barrier_semaphore()
    peers = [device_at(lax.rem(z + d, 8), y, core, x) for d in range(1, 8)] + [
        device_at(z, lax.rem(y + d, 4), core, x) for d in range(1, 4)
    ]
    for k in range(1, 8):
        peers.append(device_at(z, y, lax.rem(core + k % 2, 2), lax.rem(x + k // 2, 4)))
    for peer in peers:
        pl.semaphore_signal(barrier, inc=1, device_id=peer, device_id_type=MESH)

    place_of = offset[...].astype(jnp.float32)
    for block in range(BLOCKS):
        fixed[block, 0] = angle[2 * block : 2 * block + 2]
        fixed[block, 1] = place_of[2 * block : 2 * block + 2]
    taps_row[...] = jnp.zeros_like(taps_row)
    taps_row[:, : BAND + 1] = taps[...]
    lag_zero = jnp.sum(taps_row[...] * taps_row[...], axis=1, keepdims=True) + white[0, 0]
    remaining = valid[0, 0] - tm * SPAN
    lane = lanes((1, HALF))
    header = jnp.where(lane == 8, jnp.broadcast_to(lag_zero, (1, HALF)), 0.0)
    for block in range(BLOCKS):
        found = hits[0, slots[0, block]].astype(jnp.float32)
        count = jnp.clip(remaining - block * WIN, 0, WIN).astype(jnp.float32)
        header = jnp.where(lane == block, found, header)
        header = jnp.where(lane == 4 + block, count, header)
    meta[...] = header
    own_live = rows_of((8, HALF)) * HALF + lanes((8, HALF)) < remaining

    pl.semaphore_wait(barrier, len(peers))
    halos = [
        pltpu.make_async_remote_copy(
            src_ref=source,
            dst_ref=target,
            send_sem=halo_send.at[i],
            recv_sem=halo_recv.at[i],
            device_id=device_at(z, y, core, lax.rem(x + step, 4)),
            device_id_type=MESH,
        )
        for i, (source, target, step) in enumerate(
            (
                (stream.at[pl.ds(7, 1)], hold.at[0], 1),
                (stream.at[pl.ds(0, 1)], hold.at[1], 3),
            )
        )
    ]
    for copy in halos:
        copy.start()
    sems = (send_sems, recv_sems, local_sems)
    smalls = [
        Mover(meta, all_meta, sems, 0),
        Mover(row_two.at[0], meta_two, sems, 1),
        Mover(row_two.at[1], meta_three, sems, 2),
    ]
    relays = [
        Mover(fixed, all_fixed, sems, 3),
        Mover(message, all_first, sems, 4),
        Mover(message_two, all_second, sems, 5),
        Mover(base, all_base, sems, 6),
    ]
    group = Group(group_send, group_recv)
    me = group.me
    big, small, mid = relays[0], smalls[0], relays[3]
    small.start_first()
    big.start_first()
    places_in = group.to_all(0, lambda t: fixed, group_fixed.at[me])
    blocks_in = group.to_all(1, lambda t: meta, group_meta.at[me])
    group_fixed[me] = fixed[...]
    group_meta[me] = meta[...]

    spread = jnp.broadcast_to(taps_row[...], (WIN, WIN))
    shifted = pltpu.roll(spread, HALF, 1, stride=1, stride_axis=0)
    lag_row = lax.dot_general(
        spread[:8], shifted, NT, precision=HIGHEST, preferred_element_type=jnp.float32
    )
    lag_row = lag_row + jnp.where(lanes((8, WIN)) == HALF, white[0, 0], 0.0)
    band = pltpu.roll(
        jnp.broadcast_to(lag_row[0:1], (WIN, WIN)), WIN - HALF - BAND, 1, stride=1, stride_axis=0
    )[:, :HALF]
    landed(halos)
    extended = jnp.concatenate(
        [hold[0], stream[...], hold[1], jnp.zeros((6, HALF), jnp.float32)], axis=0
    )
    place = (rows_of((16, HALF)) - 1) * HALF + lanes((16, HALF))
    extended = jnp.where((place < remaining) & (place + tm * SPAN >= 0), extended, 0.0)
    base_own = jnp.where(own_live, band_filter(extended, band), 0.0)
    for block in range(BLOCKS):
        base[block] = base_own[2 * block : 2 * block + 2]
    mid.start_first()

    comps[...] = jnp.zeros_like(comps)
    halo_rows[...] = jnp.zeros_like(halo_rows)
    sums_out[...] = jnp.zeros_like(sums_out)
    base_out[...] = jnp.zeros_like(base_out)
    result_a[...] = jnp.zeros_like(result_a)
    result_b[...] = jnp.zeros_like(result_b)
    landed(places_in)
    landed(blocks_in)
    for block in range(BLOCKS):
        comps[9, block : block + 1, :] = joined(fixed[block, 0])
    right = group_fixed[jnp.minimum(x + 1, 3) * 2 + core, 0, 0]
    left = group_fixed[jnp.maximum(x - 1, 0) * 2 + core, BLOCKS - 1, 0]
    comps[9, 4:5, :] = jnp.concatenate([right[0:1], left[1:2]], axis=1)
    turn = 2.0 * comps[9]
    comps[9] = jnp.cos(turn)
    comps[10] = jnp.sin(turn)
    turned = jnp.concatenate(
        [group_fixed[t, block, 1] for t in range(8) for block in range(BLOCKS)]
        + [jnp.zeros((HALF // 2, HALF), jnp.float32)],
        axis=0,
    ).T

    def column(t, block, half):
        at = 8 * t + 2 * block + half
        return jnp.broadcast_to(turned[:, at : at + 1], (HALF, HALF))

    for t in range(8):
        for block in range(BLOCKS):
            for half in range(2):
                columns[BLOCKS * t + block, HALF * half : HALF * half + HALF, :] = column(
                    t, block, half
                )

    small.start_second()
    big.start_second()
    small.arrive()
    over = make_lists(all_meta, group_meta, near_a, near_b, live_a, live_b, lag_a, lag_b)
    copies = [
        pltpu.make_async_copy(near_a, list_a, list_sems.at[0]),
        pltpu.make_async_copy(near_b, list_b, list_sems.at[1]),
    ]
    for copy in copies:
        copy.start()
    mid.start_second()
    into_a = placing(near_a[...], TARGETS)
    into_b = placing(near_b[...], 2 * BPD)
    into_a = jnp.concatenate([into_a] * 3, axis=1).astype(jnp.bfloat16)
    into_b = jnp.concatenate([into_b] * 3, axis=1).astype(jnp.bfloat16)
    for copy in copies:
        copy.wait()
    big.arrive()

    wide_lane = lanes((1, WIN)).astype(jnp.float32)

    def doubled(row):
        return jnp.concatenate([row, row], axis=1)

    def six(p, where_at, trig, live, lag):
        turn = 2.0 * all_fixed[where_at + (0,)]
        co2, si2 = jnp.cos(turn), jnp.sin(turn)
        trig[p, 0:2, :] = co2
        trig[p, 2:4, :] = si2
        co, si = joined(co2), joined(si2)
        weight = jnp.where(
            wide_lane < doubled(live[pl.ds(p, 1), :]), doubled(lag[pl.ds(p, 1), :]), 0.0
        )
        return all_fixed[where_at + (1,)], co, si, weight_rows(weight, co, si)

    def three(p, where_at, trig, source):
        f = joined(source[where_at])
        return [f, f * joined(trig[p, 0:2, :]), f * joined(trig[p, 2:4, :])]

    def keep_rows(result, p, values):
        for c, value in enumerate(values):
            result[pl.ds(p, 1), WIN * c : WIN * c + WIN] = value

    def gathered_rows(into, result, count):
        values = result[:, 0 : WIN * count]
        high = values.astype(jnp.bfloat16)
        rest = values - high.astype(jnp.float32)
        middle = rest.astype(jnp.bfloat16)
        low = (rest - middle.astype(jnp.float32)).astype(jnp.bfloat16)
        parts = jnp.concatenate([high, middle, low], axis=0)
        return jnp.dot(into, parts, preferred_element_type=jnp.float32)

    def pair_weights(p, carry):
        code = list_a[p, 0]
        places, _, _, values = six(
            p, locate(lax.shift_right_logical(code, 6)), trig_a, live_a, lag_a
        )
        picked = matches(columns[jnp.clip((code & 63) - 1, 0, TARGETS - 1)], places)
        picked_a[p] = picked
        keep_rows(result_a, p, split_product(values, picked))
        return carry

    def pair_next(source):
        def body(p, carry):
            code = list_a[p, 0]
            values = three(p, locate(lax.shift_right_logical(code, 6)), trig_a, source)
            keep_rows(result_a, p, split_product(values, picked_a[p]))
            return carry

        return body

    lax.fori_loop(0, PAIRS, pair_weights, 0, unroll=UNROLL)

    def hand_out(count, target):
        out = gathered_rows(into_a, result_a, count)
        empty = jnp.zeros((1, HALF), jnp.float32)
        for t in range(8):
            for c in range(count):
                at = WIN * c
                first = BLOCKS * t
                target[t, 5 * c : 5 * c + 4, :] = out[first : first + 4, at : at + WIN]
                right = out[first + 8 : first + 9, at : at + HALF] if t < 6 else empty
                left = out[first - 5 : first - 4, at + HALF : at + WIN] if t >= 2 else empty
                target[t, 5 * c + 4 : 5 * c + 5, :] = jnp.concatenate([right, left], axis=1)

    def sum_of(arrived):
        combined = arrived[0]
        for t in range(1, 8):
            combined = combined + arrived[t]
        return combined

    hand_out(6, sums_out)
    arriving = group.to_all(2, lambda t: sums_out.at[t], sums_in.at[me])
    sums_in[me] = sums_out[me]
    mid.arrive()
    lax.fori_loop(0, PAIRS, pair_next(all_base), 0, unroll=12)
    hand_out(3, base_out)
    arriving_base = group.to_all(11, lambda t: base_out.at[t], base_in.at[me])
    base_in[me] = base_out[me]
    landed(arriving)
    combined = sum_of(sums_in)
    for c in range(6):
        comps[3 + c, 0:5, :] = combined[5 * c : 5 * c + 5]
    m_aa, m_ab, m_ac, m_bb, m_bc, m_cc, det = adjugate(*(comps[c] for c in range(3, 9)))
    co, si = comps[9], comps[10]
    seg_row = rows_of((8, WIN))
    at = lanes((8, WIN))
    time = tm * SPAN + jnp.where(
        seg_row < BLOCKS, seg_row * WIN + at, jnp.where(at < HALF, SPAN + at, at - WIN)
    )
    inside = (seg_row < BLOCKS) | ((seg_row == BLOCKS) & ((at < BAND) | (at >= WIN - BAND)))
    live = (time >= 0) & (time < valid[0, 0]) & inside
    scale = jnp.where(live, 1.0, 0.0) / det
    factors[0] = (m_aa + m_ab * co + m_ac * si) * scale
    factors[1] = (m_ab + m_bb * co + m_bc * si) * scale
    factors[2] = (m_ac + m_bc * co + m_cc * si) * scale
    landed(arriving_base)
    combined = sum_of(base_in)
    for c in range(3):
        comps[c, 0:5, :] = combined[5 * c : 5 * c + 5]

    def change():
        return factors[0] * comps[0] + factors[1] * comps[1] + factors[2] * comps[2]

    def filter_signal(signal, out):
        halo_rows[0:1] = signal[4:5, HALF:]
        for block in range(BLOCKS):
            halo_rows[2 * block + 1 : 2 * block + 2] = signal[block : block + 1, :HALF]
            halo_rows[2 * block + 2 : 2 * block + 3] = signal[block : block + 1, HALF:]
        halo_rows[9:10] = signal[4:5, :HALF]
        result = jnp.where(own_live, band_filter(halo_rows[...], band), 0.0)
        for block in range(BLOCKS):
            out[block] = result[2 * block : 2 * block + 2]
        return result

    signal_first = change()
    filtered_first = filter_signal(signal_first, message)
    own = halo_rows[1:9]
    row_two[0] = (
        jnp.where(lane == 0, total(base_own * own), 0.0)
        + jnp.where(lane == 1, total(filtered_first * own), 0.0)
        + jnp.where(lane == 2, over, 0.0)
    )

    pixel = rows_of((WIN, HALF)).astype(jnp.float32)

    def owned_first(p, carry):
        code = list_b[p, 0]
        where_at = locate(lax.shift_right_logical(code, 6))
        places, co, si, values = six(p, where_at, trig_b, live_b, lag_b)
        f = joined(all_base[where_at])
        values = [f, f * co, f * si] + values
        picked = matches(pixel, places)
        picked_b[p] = picked
        keep_rows(result_b, p, split_product(values, picked))
        return carry

    def owned_next(source):
        def body(p, carry):
            code = list_b[p, 0]
            values = three(p, locate(lax.shift_right_logical(code, 6)), trig_b, source)
            keep_rows(result_b, p, split_product(values, picked_b[p]))
            return carry

        return body

    def owned_out(first, count, number):
        out = gathered_rows(into_b, result_b, count)
        for half in range(2):
            for c in range(count):
                own_part[half, first + c] = out[BPD * half : BPD * half + BPD, WIN * c : WIN * c + WIN]
        span = pl.ds(first, count)
        return group.to_partner(number, own_part.at[1 - core, span], partner_part.at[span])

    def owned_along(first, count, number, arriving):
        landed(arriving)
        span = pl.ds(first, count)
        x_part[x, span] = own_part[core, span] + partner_part[span]
        return group.along(number, x_part.at[x, span])

    def owned_sum(first, count):
        span = pl.ds(first, count)
        owned[span] = x_part[0, span] + x_part[1, span] + x_part[2, span] + x_part[3, span]

    def sums_of(metas):
        return jnp.sum(metas[...].reshape(32, 1, HALF), axis=0)

    big, small = relays[1], smalls[1]
    small.start_first()
    big.start_first()
    lax.fori_loop(0, SLOTS, owned_first, 0, unroll=2)
    small.start_second()
    big.start_second()
    waiting_first = owned_out(0, 9, 5)
    small.arrive()
    sums = sums_of(meta_two)
    big.arrive()

    lax.fori_loop(0, PAIRS, pair_next(all_first), 0, unroll=12)
    hand_out(3, next_out)
    for t in range(8):
        next_out[t, 15:16, :] = doubled(sums)
    arriving = group.to_all(3, lambda t: next_out.at[t], next_in.at[me])
    next_in[me] = next_out[me]
    landed(arriving)
    combined = sum_of(next_in)
    for c in range(3):
        comps[c, 0:5, :] = combined[5 * c : 5 * c + 5]
    sums = combined[15:16, :HALF]
    product, curve = sums[:, 0:1], sums[:, 1:2]
    over_out[...] = jnp.broadcast_to(sums[:, 2:3], (1, HALF))
    alpha = product / curve
    filtered_second = filter_signal(signal_first - alpha * change(), message_two)
    own = halo_rows[1:9]
    row_two[1] = (
        jnp.where(lane == 0, total((base_own - alpha * filtered_first) * own), 0.0)
        + jnp.where(lane == 1, total(filtered_second * own), 0.0)
        + jnp.where(lane == 2, total(filtered_first * own), 0.0)
    )

    big, small = relays[2], smalls[2]
    small.start_first()
    big.start_first()
    first_along = owned_along(0, 9, 6, waiting_first)
    lax.fori_loop(0, SLOTS, owned_next(all_first), 0, unroll=4)
    waiting_second = owned_out(9, 3, 7)
    small.start_second()
    big.start_second()
    second_along = owned_along(9, 3, 8, waiting_second)
    small.arrive()
    last_row[...] = sums_of(meta_three)
    rows_in = group.to_all(4, lambda t: last_row, group_row.at[me])
    group_row[me] = last_row[...]
    big.arrive()
    lax.fori_loop(0, SLOTS, owned_next(all_second), 0, unroll=10)
    waiting_third = owned_out(12, 3, 9)
    third_along = owned_along(12, 3, 10, waiting_third)

    landed(rows_in)
    sums = group_row[0]
    for t in range(1, 8):
        sums = sums + group_row[t]
    product_next = sums[:, 0:1]
    beta = product_next / product
    curve_next = sums[:, 1:2] + 2.0 * beta * sums[:, 2:3] + beta * beta * curve
    alpha_next = product_next / curve_next

    def solve(r1, r2, r3):
        i_aa, i_ab, i_ac, i_bb, i_bc, i_cc = (inverse[c] for c in range(6))
        return (
            i_aa * r1 + i_ab * r2 + i_ac * r3,
            i_ab * r1 + i_bb * r2 + i_bc * r3,
            i_ac * r1 + i_bc * r2 + i_cc * r3,
        )

    landed(first_along)
    owned_sum(0, 9)
    *minors, det = adjugate(*(owned[c] for c in range(3, 9)))
    scale = 1.0 / det
    for c, minor in enumerate(minors):
        inverse[c] = minor * scale
    landed(second_along)
    owned_sum(9, 3)
    start = solve(*(owned[c] for c in range(3)))
    for c in range(3):
        owned[c] = owned[c] - alpha * owned[9 + c]
    middle = solve(*(owned[c] for c in range(3)))
    for c in range(3):
        answers_out[c] = alpha * start[c] + alpha_next * (middle[c] + beta * start[c])
        owned[c] = owned[c] - alpha_next * beta * owned[9 + c]
    landed(third_along)
    owned_sum(12, 3)
    final = solve(*(owned[c] - alpha_next * owned[12 + c] for c in range(3)))
    for c in range(3):
        answers_out[3 + c] = final[c]
    for mover in smalls + relays + [group]:
        mover.finish()
    for copy in halos:
        copy.wait_send()


def f32(*shape):
    return jax.ShapeDtypeStruct(shape, jnp.float32)


def gathered_shape(rows):
    return f32(2, 8, 4, 4, rows, HALF)


def gather_rows(values, part, number):
    rows, parts = pl.pallas_call(
        gather_kernel,
        out_shape=(gathered_shape(8), gathered_shape(1)),
        in_specs=[vmem] * 2,
        out_specs=(vmem,) * 2,
        scratch_shapes=EXCHANGE_SCRATCH,
        compiler_params=pltpu.CompilerParams(collective_id=number, has_side_effects=True),
        name="gather",
    )(values, part)
    return rows.reshape(LABELS, 2, HALF), parts.reshape(DEVICES, HALF)


def any_lengths(
    time_streams, pol_angle, offsets, block_slots, hit_ids, valid_counts, filter_taps, white_weight
):
    valid = valid_counts.reshape(1)
    message, metas, base, band = pl.pallas_call(
        prepare_kernel,
        out_shape=(gathered_shape(32), gathered_shape(1), f32(8, HALF), f32(WIN, HALF)),
        in_specs=[smem] * 4 + [vmem] * 4,
        out_specs=(vmem,) * 4,
        scratch_shapes=[
            pltpu.VMEM((2, 1, HALF), jnp.float32),
            pltpu.VMEM((1, WIN), jnp.float32),
            pltpu.VMEM((32, HALF), jnp.float32),
            pltpu.VMEM((1, HALF), jnp.float32),
        ]
        + EXCHANGE_SCRATCH
        + [pltpu.SemaphoreType.DMA((2,)), pltpu.SemaphoreType.DMA((2,))],
        compiler_params=pltpu.CompilerParams(collective_id=0, has_side_effects=True),
        name="prepare",
    )(
        valid, block_slots.reshape(BLOCKS), hit_ids.reshape(-1), white_weight.reshape(1),
        filter_taps.reshape(1, BAND + 1), time_streams.reshape(8, HALF), pol_angle.reshape(8, HALF),
        offsets.reshape(8, HALF),
    )
    gathered = message.reshape(LABELS, 8, HALF)
    metas = metas.reshape(DEVICES, HALF)

    blocks = metas[:, 0:4].reshape(LABELS)
    lives = metas[:, 4:8].reshape(LABELS).astype(jnp.int32)
    lag_zero = metas[:, 8]
    order = jnp.arange(LABELS, dtype=jnp.int32)
    same = blocks[:, None] == blocks[None, :]
    ahead = (order[None, :] - order[:, None] - 1) % LABELS
    nexts = (order + 1 + jnp.min(jnp.where(same, ahead, LABELS), axis=1)) % LABELS
    counts = jnp.sum(same, axis=1, dtype=jnp.int32)
    owned = (lax.axis_index("det") * BPD + jnp.arange(BPD, dtype=jnp.int32)).astype(jnp.float32)
    mine = owned[:, None] == blocks[None, :]
    heads = jnp.concatenate(
        [
            jnp.min(jnp.where(mine, order[None, :], LABELS - 1), axis=1),
            jnp.sum(mine, axis=1, dtype=jnp.int32),
        ]
    )

    first, part_one, factors, signal = pl.pallas_call(
        first_kernel,
        out_shape=(f32(8, HALF), f32(1, HALF), f32(3, 8, WIN), f32(8, WIN)),
        in_specs=[smem] * 5 + [vmem] * 3,
        out_specs=(vmem,) * 4,
        scratch_shapes=[
            pltpu.VMEM((12, 8, WIN), jnp.float32),
            pltpu.VMEM((16, HALF), jnp.float32),
        ],
        name="first",
    )(valid, nexts, counts, lives, lag_zero, gathered, base, band)
    second, parts_two = gather_rows(first, part_one, 1)
    other, part_two = pl.pallas_call(
        second_kernel,
        out_shape=(f32(8, HALF), f32(1, HALF)),
        in_specs=[smem] * 3 + [vmem] * 8,
        out_specs=(vmem,) * 2,
        scratch_shapes=[
            pltpu.VMEM((3, 8, WIN), jnp.float32),
            pltpu.VMEM((16, HALF), jnp.float32),
        ],
        name="second",
    )(valid, nexts, counts, gathered, second, parts_two, base, first, band, factors, signal)
    third, parts_three = gather_rows(other, part_two, 2)
    answers = pl.pallas_call(
        last_kernel,
        out_shape=(f32(3, BPD, WIN), f32(3, BPD, WIN)),
        in_specs=[smem] * 4 + [vmem] * 5,
        out_specs=(vmem,) * 2,
        scratch_shapes=[pltpu.VMEM((15, BPD, WIN), jnp.float32)],
        name="last",
    )(heads, nexts, lives, lag_zero, gathered, second, third, parts_two, parts_three)
    return tuple(answers)


def wide_buffer(*shape):
    return pltpu.VMEM((8, 4) + shape, jnp.float32)


def room(*shape):
    return pltpu.VMEM(shape, jnp.float32)


def per_device(*args):
    (
        time_streams, pol_angle, offsets, block_slots, hit_ids, valid_counts, filter_taps,
        white_weight,
    ) = args
    fast = pl.pallas_call(
        whole_kernel,
        out_shape=(f32(6, BPD, WIN), f32(1, HALF)),
        in_specs=[smem] * 4 + [vmem] * 4,
        out_specs=(vmem,) * 2,
        scratch_shapes=[
            room(2, 1, HALF), room(1, WIN), room(BLOCKS, 2, 2, HALF), room(1, HALF),
            room(BLOCKS, 2, HALF), room(BLOCKS, 2, HALF), room(2, 1, HALF), room(BLOCKS, 2, HALF),
            wide_buffer(BLOCKS, 2, 2, HALF), wide_buffer(BLOCKS, 2, HALF), wide_buffer(1, HALF),
            wide_buffer(BLOCKS, 2, HALF), wide_buffer(1, HALF), wide_buffer(BLOCKS, 2, HALF),
            wide_buffer(1, HALF),
            room(8, BLOCKS, 2, 2, HALF), room(8, 1, HALF), room(8, 32, WIN), room(8, 32, WIN),
            room(8, 16, WIN), room(8, 16, WIN),
            room(8, 16, WIN), room(8, 16, WIN), room(1, HALF), room(8, 1, HALF),
            room(TARGETS, WIN, HALF),
            pltpu.VMEM((PAIRS, WIN, WIN), jnp.bfloat16),
            pltpu.VMEM((SLOTS, WIN, WIN), jnp.bfloat16),
            room(PAIRS, 4, HALF), room(SLOTS, 4, HALF),
            pltpu.SMEM((32, HALF), jnp.int32), pltpu.SMEM((32, HALF), jnp.int32),
            room(32, HALF), room(32, HALF), room(32, HALF), room(32, HALF),
            pltpu.VMEM((32, HALF), jnp.int32), pltpu.VMEM((32, HALF), jnp.int32),
            room(32, 9 * WIN), room(32, 9 * WIN),
            room(11, 8, WIN), room(3, 8, WIN), room(16, HALF),
            room(2, 15, BPD, WIN), room(15, BPD, WIN), room(4, 15, BPD, WIN), room(15, BPD, WIN),
            room(6, BPD, WIN),
            pltpu.SemaphoreType.DMA((7, 10)), pltpu.SemaphoreType.DMA((7, 10)),
            pltpu.SemaphoreType.DMA((7,)), pltpu.SemaphoreType.DMA((12, 8)),
            pltpu.SemaphoreType.DMA((12, 8)), pltpu.SemaphoreType.DMA((2,)),
            pltpu.SemaphoreType.DMA((2,)), pltpu.SemaphoreType.DMA((2,)),
        ],
        compiler_params=pltpu.CompilerParams(collective_id=3, has_side_effects=True),
        name="whole",
    )(
        valid_counts, block_slots.reshape(1, BLOCKS), hit_ids, white_weight,
        filter_taps.reshape(1, BAND + 1), time_streams.reshape(8, HALF),
        pol_angle.reshape(8, HALF), offsets.reshape(8, HALF),
    )
    answers = lax.cond(
        fast[1][0, 0] > 0.0, lambda f, *a: jnp.concatenate(any_lengths(*a)), lambda f, *a: f,
        fast[0], *args,
    )
    return tuple(jnp.transpose(part, (1, 0, 2)) for part in (answers[:3], answers[3:]))


def solution(mesh):
    in_specs = (
        P("det", None, "tm"),
        P("det", None, "tm"),
        P("det", None, "tm"),
        P("det", None, "tm"),
        P("det", None),
        P("det", None),
        P("det", None, None),
        P("det", None),
    )
    out_specs = (P("det", None, None), P("det", None, None))
    return jax.shard_map(
        per_device, mesh=mesh, in_specs=in_specs, out_specs=out_specs, check_vma=False
    )
```
